32 devices in a mesh: dp: 16 (over z, x, core), head: 2 (over y).
Axes of the slice: x: 2, y: 2, z: 4, core: 2. Of those that a mesh axis runs over, the one named last changes fastest.
Arguments:
- tokens: bfloat16 [32768, 512], P(('dp', 'head')), may hold values from -6 to 6
- lengths: int32 [128], P('dp'), may hold values from 40 to 256, as said below
- ln1_gain: float32 [512], replicated, may hold values from 0.5 to 1.5
- ln1_bias: float32 [512], replicated, may hold values from -1 to 1
- w_query: bfloat16 [512, 512], P(None, 'head'), may hold values from -0.25 to 0.25
- w_key: bfloat16 [512, 512], P(None, 'head'), may hold values from -0.25 to 0.25
- w_value: bfloat16 [512, 512], P(None, 'head'), may hold values from -0.25 to 0.25
- w_out: bfloat16 [512, 512], P('head'), may hold values from -1 to 1
- sort_first: bfloat16 [512, 512], replicated, may hold values from -0.25 to 0.25
- sort_second: bfloat16 [512, 8], replicated, may hold values from -0.5 to 0.5
- ln2_gain: float32 [512], replicated, may hold values from 0.5 to 1.5
- ln2_bias: float32 [512], replicated, may hold values from -1 to 1
- w_up: bfloat16 [512, 2048], replicated, may hold values from -0.25 to 0.25
- w_down: bfloat16 [2048, 512], replicated, may hold values from -0.125 to 0.125
- cotangent: bfloat16 [32768, 512], P(('dp', 'head')), may hold values from -6 to 6
Outputs:
- output: bfloat16 [32768, 512], P(('dp', 'head'))
- input_grad: bfloat16 [32768, 512], P(('dp', 'head'))
- grad_ln1_gain: float32 [512], replicated
- grad_ln1_bias: float32 [512], replicated
- grad_query: float32 [512, 512], P(None, 'head')
- grad_key: float32 [512, 512], P(None, 'head')
- grad_value: float32 [512, 512], P(None, 'head')
- grad_out: float32 [512, 512], P('head')
- grad_sort_first: float32 [512, 512], replicated
- grad_sort_second: float32 [512, 8], replicated
- grad_ln2_gain: float32 [512], replicated
- grad_ln2_bias: float32 [512], replicated
- grad_up: float32 [512, 2048], replicated
- grad_down: float32 [2048, 512], replicated
The draws below stay inside these ranges and needn't reach their ends.
Inputs may be any that keep to these rules, and one draw needn't show every extreme that they name: `lengths`: some sequence has exactly 256 valid tokens and some has exactly 40.
All inputs are finite; a program needn't handle non-finite values.
Results may differ from the reference program's by a relative error of at most 0.017.
Values may be sent and summed in bfloat16 or wider, within the bound.
No kernel may reach another device: no remote copies, remote signals or barrier semaphores. Data moves between devices by JAX's collectives and lax.ppermute only.
A program may use at most 192 MiB of HBM per device.

```python
import math
import jax
import jax.numpy as jnp
from jax import lax

D = 512
HEADS = 8
HD = 64
FF = 2048
BL = 32
ITERS = 8
LMAX = 256
MINLEN = 40
NB = 8
SEQUENCES = 128
TOKENS = 32768


def draw_lengths(key, part):
    key_values, key_order = jax.random.split(key)
    drawn_values = jax.random.randint(key_values, (SEQUENCES,), MINLEN, LMAX + 1, dtype=jnp.int32)
    shuffled = jax.random.permutation(key_order, SEQUENCES)
    placed = jnp.arange(SEQUENCES, dtype=jnp.int32)
    drawn_values = jnp.where(placed == shuffled[0], LMAX, drawn_values)
    return jnp.where(placed == shuffled[1], MINLEN, drawn_values)


def block_levels(key, extent, shards, least, high):
    def one(position, parts):
        draws = jax.random.uniform(jax.random.fold_in(jax.random.fold_in(key, 6), position), (parts,), jnp.float32, least / len(shards), high / len(shards))
        return jnp.repeat(jnp.exp(draws), extent[position] // parts).reshape((-1,) + (1,) * (len(extent) - position - 1))

    factor_of = one(*shards[0])
    for cut in shards[1:]:
        factor_of = factor_of * one(*cut)
    return factor_of


def gaussian(own_key, extent, scale, reach, cuts=(), kind=jnp.bfloat16):
    drawn = scale * jax.random.normal(own_key, extent, jnp.float32)
    if cuts:
        drawn = drawn * block_levels(own_key, extent, cuts, -0.22, 0.18)
    return jnp.clip(drawn, -reach, reach).astype(kind)


def setup_inputs(seed: int = 0) -> dict:
    key_of = jax.random.split(jax.random.key(seed), 16)
    tokens = gaussian(key_of[0], (TOKENS, D), 1.0, 6.0, ((0, 32),))
    lengths = draw_lengths(jax.random.fold_in(key_of[15], 71), 0)
    ln1_gain = jnp.clip(1.0 + 0.1 * jax.random.normal(key_of[2], (D,), jnp.float32), 0.5, 1.5)
    ln1_bias = gaussian(key_of[3], (D,), 0.2, 1.0, (), jnp.float32)
    w_query = gaussian(key_of[4], (D, D), D ** -0.5, 0.25, ((1, 2),))
    w_key = gaussian(key_of[5], (D, D), D ** -0.5, 0.25, ((1, 2),))
    w_value = gaussian(key_of[6], (D, D), D ** -0.5, 0.25, ((1, 2),))
    w_out = gaussian(key_of[7], (D, D), (D // 16) ** -0.5, 1.0, ((0, 2),))
    sort_first = gaussian(key_of[8], (D, D), D ** -0.5, 0.25)
    sort_second = gaussian(key_of[9], (D, NB), (D // 4) ** -0.5, 0.5)
    ln2_gain = jnp.clip(1.0 + 0.1 * jax.random.normal(key_of[10], (D,), jnp.float32), 0.5, 1.5)
    ln2_bias = gaussian(key_of[11], (D,), 0.2, 1.0, (), jnp.float32)
    w_up = gaussian(key_of[12], (D, FF), D ** -0.5, 0.25)
    w_down = gaussian(key_of[13], (FF, D), FF ** -0.5, 0.125)
    cotangent = gaussian(key_of[14], (TOKENS, D), 1.0, 6.0, ((0, 32),))
    return dict(tokens=tokens, lengths=lengths, ln1_gain=ln1_gain, ln1_bias=ln1_bias, w_query=w_query, w_key=w_key, w_value=w_value, w_out=w_out, sort_first=sort_first, sort_second=sort_second, ln2_gain=ln2_gain, ln2_bias=ln2_bias, w_up=w_up, w_down=w_down, cotangent=cotangent)


@jax.custom_vjp
def low(v):
    return lax.optimization_barrier(v.astype(jnp.bfloat16)).astype(jnp.float32)

@jax.custom_vjp
def low_back(v):
    return v

def low_keep(v):
    return (low(v), None)

def low_pass(kept, grad):
    return (grad,)

def back_keep(v):
    return (v, None)

def back_low(kept, grad):
    return (low(grad),)
low.defvjp(low_keep, low_pass)
low_back.defvjp(back_keep, back_low)
precise = lax.Precision.HIGHEST

def smooth_gate(values):
    return jax.nn.gelu(values, approximate=False)

def layer_norm(values, gain_vec, bias_vec):
    center = values - lax.optimization_barrier(jnp.mean(values, axis=-1, keepdims=True))
    spread = lax.optimization_barrier(jnp.mean(center * center, axis=-1, keepdims=True))
    return center * lax.rsqrt(spread + 1e-05) * gain_vec + bias_vec

def log_total(values, along):
    row_top = lax.optimization_barrier(jnp.max(values, axis=along, keepdims=True))
    return row_top + jnp.log(lax.optimization_barrier(jnp.sum(jnp.exp(values - row_top), axis=along, keepdims=True)))

def sort_plan(summary, sort_one, sort_two, block_ok):
    hidden = smooth_gate(jnp.einsum('cid,de->cie', summary, sort_one, precision=precise))
    logits = jnp.einsum('cie,ej->cij', hidden, sort_two, precision=precise)
    diagonal = jnp.eye(logits.shape[1], dtype=jnp.bool_)[None]
    allowed = block_ok[:, :, None] & block_ok[:, None, :] | diagonal & ~block_ok[:, :, None]
    plan_log = jnp.where(allowed, logits, -1e+30)
    for sweep_index in range(ITERS):
        plan_log = plan_log - log_total(plan_log, 2)
        plan_log = plan_log - log_total(plan_log, 1)
    return jnp.exp(plan_log)

def matmul(left, right):
    return jnp.dot(left, right, precision=precise)

def attend(queries, key_rows, value_rows, soft_plan, tok_ok, block_ok):
    tok_mask = tok_ok[..., None, None].astype(jnp.float32)
    key_kept = key_rows * tok_mask
    value_kept = value_rows * tok_mask
    sorted_keys = low(jnp.einsum('cij,cjthd->cithd', soft_plan, key_kept, precision=precise))
    sorted_values = low(jnp.einsum('cij,cjthd->cithd', soft_plan, value_kept, precision=precise))
    all_keys = jnp.concatenate([key_kept, sorted_keys], axis=2)
    all_values = jnp.concatenate([value_kept, sorted_values], axis=2)
    scores = low_back(jnp.einsum('cibhd,cikhd->cihbk', queries, all_keys, precision=precise) * HD ** (-0.5))
    key_ok = jnp.concatenate([tok_ok, jnp.broadcast_to(block_ok[:, :, None], tok_ok.shape)], axis=2)
    allowed = key_ok[:, :, None, None, :] | ~tok_ok[:, :, None, :, None]
    scores = jnp.where(allowed, scores, -1e+30)
    weights = low(jnp.exp(scores - log_total(scores, 4)))
    mixed_rows = jnp.einsum('cihbk,cikhd->cibhd', weights, all_values, precision=precise)
    return mixed_rows * tok_mask

def forward(values, weights_all, span_list):
    gain_one, bias_one, w_q, w_k, w_v, w_o, sort_one, sort_two, gain_two, bias_two, w_u, w_d = weights_all
    seq_count = span_list.shape[0]
    nblocks = LMAX // BL
    positions = jnp.arange(LMAX, dtype=jnp.int32)
    tok_ok = (positions[None, :] < span_list[:, None]).reshape(seq_count, nblocks, BL)
    block_ok = (jnp.arange(nblocks, dtype=jnp.int32) * BL)[None, :] < span_list[:, None]
    normed = low(layer_norm(values, gain_one, bias_one))
    block_shape = (seq_count, nblocks, BL, HEADS, HD)
    queries = low_back(low(matmul(normed, w_q))).reshape(block_shape)
    key_rows = low_back(low(matmul(normed, w_k))).reshape(block_shape)
    value_rows = low_back(low(matmul(normed, w_v))).reshape(block_shape)
    summary = lax.optimization_barrier(jnp.sum(normed.reshape(seq_count, nblocks, BL, D) * tok_ok[..., None], axis=2)) * BL ** (-0.5)
    soft_plan = sort_plan(summary, sort_one, sort_two, block_ok)
    mixed_rows = attend(queries, key_rows, value_rows, soft_plan, tok_ok, block_ok).reshape(seq_count * LMAX, D)
    mixed_rows = low_back(low(mixed_rows))
    attention = low_back(matmul(mixed_rows, w_o))
    middle = values + attention
    normed_two = low(layer_norm(middle, gain_two, bias_two))
    up_value = low_back(matmul(normed_two, w_u))
    hidden = low_back(low(smooth_gate(up_value)))
    return middle + matmul(hidden, w_d)

def add_pair(first_one, second_one):
    return first_one + second_one

def reference(tokens, lengths, ln1_gain, ln1_bias, w_query, w_key, w_value, w_out, sort_first, sort_second, ln2_gain, ln2_bias, w_up, w_down, cotangent):
    params = (ln1_gain, ln1_bias, w_query.astype(jnp.float32), w_key.astype(jnp.float32), w_value.astype(jnp.float32), w_out.astype(jnp.float32), sort_first.astype(jnp.float32), sort_second.astype(jnp.float32), ln2_gain, ln2_bias, w_up.astype(jnp.float32), w_down.astype(jnp.float32))
    group_size = math.gcd(SEQUENCES, 16)
    rounds = SEQUENCES // group_size
    row_total = group_size * LMAX
    inputs = tokens.astype(jnp.float32).reshape(rounds, row_total, D)
    cotans = cotangent.astype(jnp.float32).reshape(rounds, row_total, D)
    span_sets = lengths.reshape(rounds, group_size)

    def advance(totals, scan_item):
        block_in, block_cot, block_len = scan_item

        def run_layer(values, weights_all):
            return forward(values, weights_all, block_len)
        result, pull_back = jax.vjp(run_layer, block_in, params)
        grad_in, grad_params = pull_back(block_cot)
        totals = jax.tree.map(add_pair, totals, grad_params)
        return (totals, (result.astype(jnp.bfloat16), grad_in.astype(jnp.bfloat16)))
    start_sums = jax.tree.map(jnp.zeros_like, params)
    totals, (outputs, input_grads) = lax.scan(advance, start_sums, (inputs, cotans, span_sets))
    return (outputs.reshape(TOKENS, D), input_grads.reshape(TOKENS, D), totals[0], totals[1], totals[2], totals[3], totals[4], totals[5], totals[6], totals[7], totals[8], totals[9], totals[10], totals[11])
```

```python
import functools

import jax
import jax.numpy as jnp
from jax import lax
from jax.sharding import PartitionSpec as P

HD = 64
BL = 32
ITERS = 8
LMAX = 256


precise = lax.Precision.HIGHEST


def smooth_gate(values):
    return jax.nn.gelu(values, approximate=False)


def layer_norm(values, gain_vec, bias_vec):
    center = values - jnp.mean(values, axis=-1, keepdims=True)
    spread = jnp.mean(center * center, axis=-1, keepdims=True)
    return center * lax.rsqrt(spread + 1e-05) * gain_vec + bias_vec


def log_total(values, along):
    row_top = jnp.max(values, axis=along, keepdims=True)
    return row_top + jnp.log(jnp.sum(jnp.exp(values - row_top), axis=along, keepdims=True))


def sort_plan(summary, sort_one, sort_two, block_ok):
    hidden = smooth_gate(jnp.einsum("cid,de->cie", summary, sort_one, precision=precise))
    logits = jnp.einsum("cie,ej->cij", hidden, sort_two, precision=precise)
    diagonal = jnp.eye(logits.shape[1], dtype=jnp.bool_)[None]
    allowed = block_ok[:, :, None] & block_ok[:, None, :] | diagonal & ~block_ok[:, :, None]
    plan_log = jnp.where(allowed, logits, -1e30)
    for sweep_index in range(ITERS):
        plan_log = plan_log - log_total(plan_log, 2)
        plan_log = plan_log - log_total(plan_log, 1)
    return jnp.exp(plan_log)


def outer_product(left, right):
    return lax.dot_general(
        left, right, (((0,), (0,)), ((), ())), preferred_element_type=jnp.float32
    )


def attend_forward(queries, key_rows, value_rows, soft_plan, tok_ok, block_ok):
    tok_mask = tok_ok[..., None, None].astype(jnp.bfloat16)
    key_kept = key_rows * tok_mask
    value_kept = value_rows * tok_mask
    sorted_keys = jnp.einsum(
        "cij,cjthd->cithd", soft_plan, key_kept.astype(jnp.float32), precision=precise
    ).astype(jnp.bfloat16)
    sorted_values = jnp.einsum(
        "cij,cjthd->cithd", soft_plan, value_kept.astype(jnp.float32), precision=precise
    ).astype(jnp.bfloat16)
    all_keys = jnp.concatenate([key_kept, sorted_keys], axis=2)
    all_values = jnp.concatenate([value_kept, sorted_values], axis=2)
    score_scale = queries.shape[-1] ** (-0.5)
    scores = (
        jnp.einsum("cibhd,cikhd->cihbk", queries, all_keys, preferred_element_type=jnp.float32)
        * score_scale
    )
    key_ok = jnp.concatenate([tok_ok, jnp.broadcast_to(block_ok[:, :, None], tok_ok.shape)], axis=2)
    allowed = key_ok[:, :, None, None, :] | ~tok_ok[:, :, None, :, None]
    scores = jnp.where(allowed, scores, -1e30)
    weights = jnp.exp(scores - log_total(scores, 4))
    weights_low = weights.astype(jnp.bfloat16)
    mixed_rows = jnp.einsum(
        "cihbk,cikhd->cibhd", weights_low, all_values, preferred_element_type=jnp.float32
    )
    mixed_rows = mixed_rows * tok_ok[..., None, None].astype(jnp.float32)
    return (mixed_rows, (key_kept, all_keys, all_values, weights, weights_low))


def attend_backward(grad_mixed, queries, soft_plan, tok_ok, saved_state):
    key_kept, all_keys, all_values, weights, weights_low = saved_state
    block_len = key_kept.shape[2]
    score_scale = queries.shape[-1] ** (-0.5)
    value_kept = all_values[:, :, :block_len]
    grad_rows = grad_mixed * tok_ok[..., None, None].astype(jnp.bfloat16)
    grad_weights = jnp.einsum(
        "cibhd,cikhd->cihbk", grad_rows, all_values, preferred_element_type=jnp.float32
    )
    grad_all_values = jnp.einsum(
        "cihbk,cibhd->cikhd", weights_low, grad_rows, preferred_element_type=jnp.float32
    )
    weighted = jnp.sum(weights * grad_weights, axis=4, keepdims=True)
    grad_scores = (weights * (grad_weights - weighted)).astype(jnp.bfloat16)
    grad_queries = (
        jnp.einsum("cihbk,cikhd->cibhd", grad_scores, all_keys, preferred_element_type=jnp.float32)
        * score_scale
    )
    grad_all_keys = (
        jnp.einsum("cihbk,cibhd->cikhd", grad_scores, queries, preferred_element_type=jnp.float32)
        * score_scale
    )
    grad_sorted_keys = grad_all_keys[:, :, block_len:]
    grad_sorted_values = grad_all_values[:, :, block_len:]
    grad_plan = jnp.einsum(
        "cithd,cjthd->cij", grad_sorted_keys, key_kept.astype(jnp.float32), precision=precise
    )
    grad_plan = grad_plan + jnp.einsum(
        "cithd,cjthd->cij", grad_sorted_values, value_kept.astype(jnp.float32), precision=precise
    )
    key_total = grad_all_keys[:, :, :block_len] + jnp.einsum(
        "cij,cithd->cjthd", soft_plan, grad_sorted_keys, precision=precise
    )
    value_total = grad_all_values[:, :, :block_len] + jnp.einsum(
        "cij,cithd->cjthd", soft_plan, grad_sorted_values, precision=precise
    )
    tok_mask = tok_ok[..., None, None].astype(jnp.float32)
    return (
        grad_queries.astype(jnp.bfloat16),
        (key_total * tok_mask).astype(jnp.bfloat16),
        (value_total * tok_mask).astype(jnp.bfloat16),
        grad_plan,
    )


def run_attention(normed_here, span_list, query_cols, key_cols, value_cols, sort_one, sort_two):
    seq_count = span_list.shape[0]
    nblocks = LMAX // BL
    heads_here = query_cols.shape[1] // HD
    positions = jnp.arange(LMAX, dtype=jnp.int32)
    tok_ok = (positions[None, :] < span_list[:, None]).reshape(seq_count, nblocks, BL)
    block_ok = (jnp.arange(nblocks, dtype=jnp.int32) * BL)[None, :] < span_list[:, None]
    block_shape = (seq_count, nblocks, BL, heads_here, HD)
    queries = (
        jnp.dot(normed_here, query_cols, preferred_element_type=jnp.float32)
        .astype(jnp.bfloat16)
        .reshape(block_shape)
    )
    key_rows = (
        jnp.dot(normed_here, key_cols, preferred_element_type=jnp.float32)
        .astype(jnp.bfloat16)
        .reshape(block_shape)
    )
    value_rows = (
        jnp.dot(normed_here, value_cols, preferred_element_type=jnp.float32)
        .astype(jnp.bfloat16)
        .reshape(block_shape)
    )
    summary = jnp.sum(
        normed_here.reshape(seq_count, nblocks, BL, -1).astype(jnp.float32) * tok_ok[..., None],
        axis=2,
    ) * BL ** (-0.5)

    def plan_of(summary_in, first_in, second_in):
        return sort_plan(summary_in, first_in, second_in, block_ok)

    soft_plan, plan_back = jax.vjp(plan_of, summary, sort_one, sort_two)
    mixed_rows, saved_state = attend_forward(
        queries, key_rows, value_rows, soft_plan, tok_ok, block_ok
    )
    mixed_rows = mixed_rows.reshape(normed_here.shape[0], -1).astype(jnp.bfloat16)
    return (mixed_rows, queries, tok_ok, soft_plan, plan_back, saved_state)


AXES = ("dp", "head")


def swap(values, bit, dp_size):
    if bit == "head":
        pairs = [(d * 2 + h, d * 2 + (1 - h)) for d in range(dp_size) for h in range(2)]
    else:
        pairs = [(d * 2 + h, (d ^ bit) * 2 + h) for d in range(dp_size) for h in range(2)]
    return lax.ppermute(values, AXES, pairs)


def side_of(bit):
    if bit == "head":
        return lax.axis_index("head")
    return (lax.axis_index("dp") // bit) % 2


def scatter_sum(values, bits, dp_size):
    for bit in bits:
        halves = values.reshape((2, values.shape[0] // 2) + values.shape[1:])
        side = side_of(bit)
        sent = lax.dynamic_index_in_dim(halves, 1 - side, 0, keepdims=False)
        kept = lax.dynamic_index_in_dim(halves, side, 0, keepdims=False)
        got = swap(sent, bit, dp_size)
        values = (kept.astype(jnp.float32) + got.astype(jnp.float32)).astype(jnp.bfloat16)
    return values


def gather_all(values, bits, dp_size):
    for bit in reversed(bits):
        got = swap(values, bit, dp_size)
        side = side_of(bit)
        pair = jnp.stack([jnp.where(side == 0, values, got), jnp.where(side == 0, got, values)])
        values = pair.reshape((2 * values.shape[0],) + values.shape[1:])
    return values


def total_over(values, first_bits, dp_size, keep_head):
    spread = list(first_bits)
    rest = []
    bit = 4
    while bit < dp_size:
        (spread if bit <= 8 else rest).append(bit)
        bit *= 2
    shard = scatter_sum(values, spread, dp_size)
    for bit in rest:
        got = swap(shard, bit, dp_size)
        shard = (shard.astype(jnp.float32) + got.astype(jnp.float32)).astype(jnp.bfloat16)
    back = [bit for bit in spread if not (keep_head and bit == "head")]
    return gather_all(shard, back, dp_size)


def gather_weights(weights, dp_size):
    side = lax.axis_index("dp") % 2
    head_side = lax.axis_index("head")
    half = weights.shape[1] // 2
    mine = lax.dynamic_slice_in_dim(weights, side * half, half, 1)
    first = swap(mine, "head", dp_size)
    second = swap(first, 1, dp_size)
    other = jnp.where(
        side == 0, jnp.concatenate([first, second], 1), jnp.concatenate([second, first], 1)
    )
    return jnp.where(
        head_side == 0,
        jnp.concatenate([weights, other], 1),
        jnp.concatenate([other, weights], 1),
    )


def on_device(
    dp_size,
    tokens,
    lengths,
    ln1_gain,
    ln1_bias,
    w_query,
    w_key,
    w_value,
    w_out,
    sort_first,
    sort_second,
    ln2_gain,
    ln2_bias,
    w_up,
    w_down,
    cotangent,
):
    head_side = lax.axis_index("head")
    inputs = tokens.astype(jnp.float32)
    sort_one = sort_first.astype(jnp.float32)
    sort_two = sort_second.astype(jnp.float32)
    normed_f, norm_back = jax.vjp(layer_norm, inputs, ln1_gain, ln1_bias)
    normed = normed_f.astype(jnp.bfloat16)
    packed = gather_weights(jnp.concatenate([w_query, w_key, w_value, w_out.T], 0), dp_size)
    w_query, w_key, w_value = packed[:512], packed[512:1024], packed[1024:1536]
    w_out = packed[1536:].T
    here = lengths.shape[0] // 2
    lengths = lax.dynamic_slice_in_dim(lengths, head_side * here, here, 0)
    normed_here = normed
    mixed_rows, queries, tok_ok, soft_plan, plan_back, saved_state = run_attention(
        normed_here, lengths, w_query, w_key, w_value, sort_one, sort_two
    )
    attention = jnp.dot(mixed_rows, w_out, preferred_element_type=jnp.float32)
    middle = inputs + attention
    normed_two_f, norm_two_back = jax.vjp(layer_norm, middle, ln2_gain, ln2_bias)
    normed_two = normed_two_f.astype(jnp.bfloat16)
    up_value = jnp.dot(normed_two, w_up, preferred_element_type=jnp.float32)
    hidden_f, gate_back = jax.vjp(smooth_gate, up_value)
    hidden = hidden_f.astype(jnp.bfloat16)
    output = (middle + jnp.dot(hidden, w_down, preferred_element_type=jnp.float32)).astype(
        jnp.bfloat16
    )
    grad_hidden = jnp.dot(cotangent, w_down.T, preferred_element_type=jnp.float32).astype(
        jnp.bfloat16
    )
    grad_upin = gate_back(grad_hidden.astype(jnp.float32))[0].astype(jnp.bfloat16)
    grad_down = outer_product(hidden, cotangent)
    grad_up = outer_product(normed_two, grad_upin)
    grad_middle_norm, grad_gain_two, grad_bias_two = norm_two_back(
        jnp.dot(grad_upin, w_up.T, preferred_element_type=jnp.float32)
    )
    grad_middle = cotangent.astype(jnp.float32) + grad_middle_norm
    grad_attention = grad_middle.astype(jnp.bfloat16)
    grad_attention_here = grad_attention
    grad_w_out = outer_product(mixed_rows, grad_attention_here)
    grad_mixed = jnp.dot(
        grad_attention_here, w_out.T, preferred_element_type=jnp.float32
    ).astype(jnp.bfloat16)
    grad_queries, grad_keys, grad_values, grad_plan = attend_backward(
        grad_mixed.reshape(queries.shape), queries, soft_plan, tok_ok, saved_state
    )
    grad_summary, grad_first, grad_second = plan_back(grad_plan)
    rows_here = normed_here.shape[0]
    grad_queries = grad_queries.reshape(rows_here, -1)
    grad_keys = grad_keys.reshape(rows_here, -1)
    grad_values = grad_values.reshape(rows_here, -1)
    grad_spread = (grad_summary[:, :, None, :] * tok_ok[..., None] * BL ** (-0.5)).reshape(
        rows_here, -1
    )
    grad_w_query = outer_product(normed_here, grad_queries)
    grad_w_key = outer_product(normed_here, grad_keys)
    grad_w_value = outer_product(normed_here, grad_values)
    total_term = jnp.dot(grad_queries, w_query.T, preferred_element_type=jnp.float32)
    total_term = total_term + jnp.dot(grad_keys, w_key.T, preferred_element_type=jnp.float32)
    grad_normed = total_term + jnp.dot(grad_values, w_value.T, preferred_element_type=jnp.float32)
    grad_normed = grad_normed + grad_spread
    grad_inputs_norm, grad_gain_one, grad_bias_one = norm_back(grad_normed)
    input_grad = (grad_middle + grad_inputs_norm).astype(jnp.bfloat16)
    low = jnp.bfloat16
    packed_ffn = jnp.concatenate([grad_up.astype(low).reshape(2048, 512), grad_down.astype(low)], 0)
    small = jnp.concatenate(
        [grad_second.T, jnp.stack([grad_gain_one, grad_bias_one, grad_gain_two, grad_bias_two])], 0
    )
    small = jnp.pad(small, ((0, 512 - small.shape[0]), (0, 0)))
    packed_sort = jnp.concatenate([grad_first, small], 0).astype(low)
    heads = jnp.concatenate([grad_w_query.T, grad_w_key.T, grad_w_value.T, grad_w_out], 0).astype(low)
    heads = heads.reshape(4, 2, 256, 512).transpose(1, 0, 2, 3)
    y_first, x_first = [1, "head", 2], [1, 2, "head"]
    ffn = jnp.concatenate(
        [total_over(packed_ffn[:2048], y_first, dp_size, False), total_over(packed_ffn[2048:], x_first, dp_size, False)], 0
    ).astype(jnp.float32)
    sort = total_over(packed_sort, x_first, dp_size, False).astype(jnp.float32)
    heads = total_over(heads.reshape(2048, 512), ["head", 1, 2], dp_size, True).astype(jnp.float32)
    heads = heads.reshape(4, 256, 512)
    return (
        output,
        input_grad,
        sort[520],
        sort[521],
        heads[0].T,
        heads[1].T,
        heads[2].T,
        heads[3],
        sort[:512],
        sort[512:520].T,
        sort[522],
        sort[523],
        ffn[:2048].reshape(512, 2048),
        ffn[2048:],
    )


def solution(mesh):
    return jax.shard_map(
        functools.partial(on_device, mesh.shape["dp"]),
        mesh=mesh,
        in_specs=(
            P(("dp", "head"), None),
            P("dp"),
            P(),
            P(),
            P(None, "head"),
            P(None, "head"),
            P(None, "head"),
            P("head", None),
            P(),
            P(),
            P(),
            P(),
            P(),
            P(),
            P(("dp", "head"), None),
        ),
        out_specs=(
            P(("dp", "head"), None),
            P(("dp", "head"), None),
            P(),
            P(),
            P(None, "head"),
            P(None, "head"),
            P(None, "head"),
            P("head", None),
            P(),
            P(),
            P(),
            P(),
            P(),
            P(),
        ),
        check_vma=False,
    )
```

```python
import functools

import jax
import jax.numpy as jnp
from jax import lax
from jax.experimental import pallas as pl
from jax.experimental.pallas import tpu as pltpu
from jax.sharding import PartitionSpec as P

HD = 64
BL = 32
ITERS = 8
LMAX = 256
NB = LMAX // BL
SUMMARY_SCALE = BL**-0.5
F32 = jnp.float32
LOW = jnp.bfloat16
AXES = ("dp", "head")
VMEM_LIMIT = 56 * 1024 * 1024

ERF_P = 0.3875
ERF_C = (
    0.23607149955804155,
    0.07450957017858355,
    0.6926085194492264,
    -0.6975625302575207,
    0.9269567150083973,
    -0.23258376165572045,
)


def normal_parts(v):
    size = jnp.abs(v)
    bell = jnp.exp(v * v * -0.5)
    t = 1.0 / (1.0 + size * (ERF_P * 0.5**0.5))
    poly = ERF_C[5]
    for coef in ERF_C[4::-1]:
        poly = poly * t + coef
    tail = (0.5 * t) * poly * bell
    return jnp.where(v >= 0, 1.0 - tail, tail), bell * 0.3989422804014327


def dot_nn(a, b):
    return lax.dot_general(a, b, (((1,), (0,)), ((), ())), preferred_element_type=F32)


def dot_nt(a, b):
    return lax.dot_general(a, b, (((1,), (1,)), ((), ())), preferred_element_type=F32)


def dot_tn(a, b):
    return lax.dot_general(a, b, (((0,), (0,)), ((), ())), preferred_element_type=F32)


def split3(v):
    high = v.astype(LOW)
    left = v - high.astype(F32)
    mid = left.astype(LOW)
    return high, mid, (left - mid.astype(F32)).astype(LOW)


def split2(v):
    high = v.astype(LOW)
    return high, (v - high.astype(F32)).astype(LOW)


def exact_right(dot, v, w):
    a, b, c = split3(v)
    return dot(a, w) + dot(b, w) + dot(c, w)


def exact_both(dot, v, w):
    a, b, c = split3(v)
    d, e, f = split3(w)
    return dot(a, d) + (dot(a, e) + dot(b, d)) + (dot(b, e) + dot(a, f) + dot(c, d))


def row_norm(x):
    center = x - jnp.mean(x, axis=-1, keepdims=True)
    spread = jnp.mean(center * center, axis=-1, keepdims=True)
    scale = lax.rsqrt(spread + 1e-05)
    return center * scale, scale


def norm_pull(grad, unit, scale):
    return scale * (
        grad
        - jnp.mean(grad, axis=-1, keepdims=True)
        - unit * jnp.mean(grad * unit, axis=-1, keepdims=True)
    )


def iota(shape, axis):
    return lax.broadcasted_iota(jnp.int32, shape, axis)


def plan_allowed(count, spans):
    shape = (count, NB, NB)
    seq = iota(shape, 0)
    span = jnp.zeros(shape, jnp.int32)
    for s in range(count):
        span = jnp.where(seq == s, spans[s], span)
    row, col = iota(shape, 1), iota(shape, 2)
    row_ok, col_ok = row * BL < span, col * BL < span
    return (row_ok & col_ok) | ((row == col) & ~row_ok)


def prepare_kernel(
    count, lens, side, tokens, vecs, first, second, normed, normed_t, summary, pre, steps, plan
):
    spans = [lens[side[0] * count + s] for s in range(count)]
    gain, bias = vecs[0:1, :], vecs[1:2, :]
    for s in range(count):
        rows = pl.ds(s * LMAX, LMAX)
        unit, _ = row_norm(tokens[rows, :].astype(F32))
        low = (unit * gain + bias).astype(LOW)
        normed[rows, :] = low
        normed_t[:, rows] = low.T
        token, block = iota((NB, LMAX), 1), iota((NB, LMAX), 0)
        member = (token // BL == block) & (token < spans[s])
        picked = jnp.where(member, 1.0, 0.0).astype(LOW)
        summary[pl.ds(s * NB, NB), :] = dot_nn(picked, low) * SUMMARY_SCALE
    before = exact_right(dot_nn, summary[...], first[...])
    pre[...] = before
    gate, _ = normal_parts(before)
    logits = exact_right(dot_nn, before * gate, second[...])
    logits = logits.reshape(count, NB, NB)
    x = jnp.where(plan_allowed(count, spans), logits, -1e30)
    for k in range(2 * ITERS):
        axis = 2 - k % 2
        top = jnp.max(x, axis=axis, keepdims=True)
        x = x - (top + jnp.log(jnp.sum(jnp.exp(x - top), axis=axis, keepdims=True)))
        steps[k] = x
    plan[...] = jnp.exp(x)


def head_mask(value):
    row, lane = iota((LMAX, 8 * HD), 0), iota((LMAX, 8 * HD), 1)
    return jnp.where(row // BL == lane // HD, value, 0.0).astype(LOW)


def spread_plan(plan, flip):
    pick = jnp.where(iota((LMAX, NB), 0) // BL == iota((LMAX, NB), 1), 1.0, 0.0).astype(LOW)
    same = (iota((LMAX, LMAX), 0) % BL) == (iota((LMAX, LMAX), 1) % BL)
    parts = []
    for part in split2(plan):
        tall = (dot_nt if flip else dot_nn)(pick, part).astype(LOW)
        parts.append(jnp.where(same, dot_nt(tall, pick), 0.0).astype(LOW))
    return parts


def pair_rows(left_t, right, m, lane_low):
    both = dot_nn(left_t[2 * BL * m : 2 * BL * (m + 1), :], right[:, 2 * HD * m : 2 * HD * (m + 1)])
    return jnp.where(lane_low, both[:BL], both[BL:])


def forward_kernel(
    count, lens, side, normed, tokens, cotangent, plan, w_q, w_k, w_v, w_o, vecs,
    q_out, k_out, v_out, sk_out, sv_out, p_out, mixed, mixed_t, middle, normed2, normed2_t, cot_t,
    mask,
):
    s = pl.program_id(0)
    span = lens[side[0] * count + s]

    @pl.when(s == 0)
    def _():
        mask[...] = head_mask(HD**-0.5)

    cot_t[...] = cotangent[...].T
    n = normed[...]
    keep = iota((LMAX, 8 * HD), 0) < span
    q_out[...] = dot_nn(n, w_q[...]).astype(LOW)
    key = jnp.where(keep, dot_nn(n, w_k[...]), 0.0).astype(LOW)
    value = jnp.where(keep, dot_nn(n, w_v[...]), 0.0).astype(LOW)
    k_out[...] = key
    v_out[...] = value
    high, low = spread_plan(plan[0], False)
    sk_out[...] = (dot_nn(high, key) + dot_nn(low, key)).astype(LOW)
    sv_out[...] = (dot_nn(high, value) + dot_nn(low, value)).astype(LOW)
    key_row = iota((2 * BL, 8 * BL), 0)
    query = iota((2 * BL, 8 * BL), 1) % BL
    lane_low = iota((BL, 2 * HD), 1) < HD
    for i in range(NB):
        rows = pl.ds(i * BL, BL)
        keys = jnp.concatenate([k_out[rows, :], sk_out[rows, :]], 0)
        values = jnp.concatenate([v_out[rows, :], sv_out[rows, :]], 0)
        wide = jnp.concatenate([q_out[rows, :]] * 8, 0) * mask[...]
        scores = dot_nt(keys, wide)
        valid = jnp.where(key_row < BL, i * BL + key_row, i * BL) < span
        scores = jnp.where(valid | (i * BL + query >= span), scores, -1e30)
        top = jnp.max(scores, axis=0, keepdims=True)
        grown = jnp.exp(scores - top)
        weights = grown * (1.0 / jnp.sum(grown, axis=0, keepdims=True))
        p_out[pl.ds(i * 2 * BL, 2 * BL), :] = weights.astype(LOW)
        weights_t = weights.T.astype(LOW)
        outs = [pair_rows(weights_t, values, m, lane_low) for m in range(4)]
        out = jnp.concatenate(outs, 1)
        out = jnp.where(iota((BL, 8 * HD), 0) + i * BL < span, out, 0.0)
        mixed[rows, :] = out.astype(LOW)
    blended = mixed[...]
    mixed_t[...] = blended.T
    mid = tokens[...].astype(F32) + dot_nn(blended, w_o[...])
    middle[...] = mid
    unit, _ = row_norm(mid)
    low2 = (unit * vecs[2:3, :] + vecs[3:4, :]).astype(LOW)
    normed2[...] = low2
    normed2_t[...] = low2.T


def ffn_kernel(
    steps, rows_all, middle, normed2, normed2_t, cotangent, cot_t, up, down,
    output, grad_norm2, grad_up, grad_down_t,
    up_s, gh_s, hid_s, gup_s, out_s,
):
    f = pl.program_id(0)
    up_s[...] = dot_nn(normed2[...], up[...])
    gh_s[...] = dot_nt(cotangent[...], down[...]).astype(LOW)
    piece = 64

    def gate(r, carry):
        rows = pl.ds(pl.multiple_of(r * piece, piece), piece)
        v = up_s[rows, :]
        share, bell = normal_parts(v)
        hid_s[rows, :] = (v * share).astype(LOW)
        gup_s[rows, :] = (gh_s[rows, :].astype(F32) * (share + v * bell)).astype(LOW)
        return carry

    lax.fori_loop(0, rows_all // piece, gate, 0)
    hidden, gup = hid_s[...], gup_s[...]
    grad_up[0] = dot_nn(normed2_t[...], gup).astype(LOW)
    grad_down_t[0] = dot_nn(cot_t[...], hidden).astype(LOW)

    @pl.when(f == 0)
    def _():
        out_s[...] = dot_nn(hidden, down[...])
        grad_norm2[...] = dot_nt(gup, up[...])

    @pl.when(f > 0)
    def _():
        out_s[...] += dot_nn(hidden, down[...])
        grad_norm2[...] += dot_nt(gup, up[...])

    @pl.when(f == steps - 1)
    def _():
        output[...] = (middle[...] + out_s[...]).astype(LOW)


def backward_kernel(
    count, lens, side, grad_norm2, middle, cotangent, normed_t, mixed_t, plan,
    q_in, k_in, v_in, sk_in, sv_in, p_in, w_o, vecs,
    grad_middle, grad_q, grad_k, grad_v, grad_plan, grad_w, grad_wo, grad_vecs,
    mask, go_s, dks, dvs, dk_own, dv_own, acc_w, acc_o,
):
    s = pl.program_id(0)
    span = lens[side[0] * count + s]

    @pl.when(s == 0)
    def _():
        mask[...] = head_mask(1.0)
        acc_w[...] = jnp.zeros_like(acc_w)
        acc_o[...] = jnp.zeros_like(acc_o)
        grad_vecs[...] = jnp.zeros_like(grad_vecs)

    unit, scale = row_norm(middle[...])
    gn = grad_norm2[...]
    grad_vecs[2:3, :] += jnp.sum(gn * unit, axis=0, keepdims=True)
    grad_vecs[3:4, :] += jnp.sum(gn, axis=0, keepdims=True)
    gmid = cotangent[...].astype(F32) + norm_pull(gn * vecs[2:3, :], unit, scale)
    grad_middle[...] = gmid
    gatt = gmid.astype(LOW)
    acc_o[...] += dot_nn(mixed_t[...], gatt)
    gmixed = dot_nt(gatt, w_o[...]).astype(LOW)
    keep = iota((LMAX, 8 * HD), 0) < span
    go_s[...] = jnp.where(keep, gmixed, jnp.zeros_like(gmixed))
    lane_low = iota((BL, 2 * HD), 1) < HD
    for i in range(NB):
        rows = pl.ds(i * BL, BL)
        keys = jnp.concatenate([k_in[rows, :], sk_in[rows, :]], 0)
        values = jnp.concatenate([v_in[rows, :], sv_in[rows, :]], 0)
        gwide = jnp.concatenate([go_s[rows, :]] * 8, 0) * mask[...]
        qwide = jnp.concatenate([q_in[rows, :]] * 8, 0) * mask[...]
        weights = p_in[pl.ds(i * 2 * BL, 2 * BL), :]
        wide = weights.astype(F32)
        gweights = dot_nt(values, gwide)
        dv = dot_nn(weights, gwide)
        total = jnp.sum(wide * gweights, axis=0, keepdims=True)
        gscores = wide * (gweights - total)
        dk = dot_nn(gscores.astype(LOW), qwide) * HD**-0.5
        gscores_t = gscores.T.astype(LOW)
        dq = jnp.concatenate([pair_rows(gscores_t, keys, m, lane_low) for m in range(4)], 1)
        grad_q[rows, :] = (dq * HD**-0.5).astype(LOW)
        dk_own[rows, :] = dk[:BL]
        dks[rows, :] = dk[BL:]
        dv_own[rows, :] = dv[:BL]
        dvs[rows, :] = dv[BL:]
    same = (iota((LMAX, LMAX), 0) % BL) == (iota((LMAX, LMAX), 1) % BL)
    high, low = spread_plan(plan[0], True)
    cross = jnp.zeros((LMAX, LMAX), F32)
    for own, sorted_part, kept, target in (
        (dk_own, dks, k_in, grad_k),
        (dv_own, dvs, v_in, grad_v),
    ):
        g_high, g_low = split2(sorted_part[...])
        kept_rows = kept[...]
        cross += dot_nt(g_high, kept_rows) + dot_nt(g_low, kept_rows)
        total = own[...] + (dot_nn(high, g_high) + (dot_nn(high, g_low) + dot_nn(low, g_high)))
        target[...] = jnp.where(keep, total, 0.0).astype(LOW)
    cross = jnp.where(same, cross, 0.0)
    rows8 = jnp.sum(cross.reshape(NB, BL, LMAX), axis=1)
    pick = jnp.where(iota((LMAX, NB), 0) // BL == iota((LMAX, NB), 1), 1.0, 0.0).astype(LOW)
    grad_plan[0] = exact_right(dot_nn, rows8, pick)
    nt = normed_t[...]
    for slot, grads in enumerate((grad_q, grad_k, grad_v)):
        acc_w[slot] += dot_nn(nt, grads[...])

    @pl.when(s == count - 1)
    def _():
        grad_w[...] = acc_w[...].astype(LOW)
        grad_wo[...] = acc_o[...].astype(LOW)


def finish_kernel(
    count, lens, side, tokens, grad_middle, grad_q, grad_k, grad_v, w_q, w_k, w_v, vecs,
    grad_plan, plan, steps, pre, summary, first, second,
    input_grad, grad_first, grad_second, grad_vecs,
    gsum,
):
    s = pl.program_id(0)
    span = lens[side[0] * count + s]

    @pl.when(s == 0)
    def _():
        grad_vecs[...] = jnp.zeros_like(grad_vecs)
        spans = [lens[side[0] * count + c] for c in range(count)]
        g = grad_plan[...] * plan[...]
        for k in range(2 * ITERS - 1, -1, -1):
            axis = 2 - k % 2
            g = g - jnp.exp(steps[k]) * jnp.sum(g, axis=axis, keepdims=True)
        g = jnp.where(plan_allowed(count, spans), g, 0.0).reshape(count * NB, NB)
        before = pre[...]
        share, bell = normal_parts(before)
        grad_second[...] = exact_both(dot_tn, before * share, g)
        ghid = exact_right(dot_nt, g, second[...])
        gpre = ghid * (share + before * bell)
        grad_first[...] = exact_both(dot_tn, summary[...], gpre).astype(LOW)
        gsum[...] = exact_right(dot_nt, gpre, first[...]) * SUMMARY_SCALE

    unit, scale = row_norm(tokens[...].astype(F32))
    token, block = iota((LMAX, NB), 0), iota((LMAX, NB), 1)
    member = (token // BL == block) & (token < span)
    picked = jnp.where(member, 1.0, 0.0).astype(LOW)
    part = gsum[pl.ds(pl.multiple_of(s * NB, NB), NB), :]
    high, mid, low = split3(part)
    gn = dot_nn(picked, high) + dot_nn(picked, mid) + dot_nn(picked, low)
    gn += dot_nt(grad_q[...], w_q[...]) + dot_nt(grad_k[...], w_k[...])
    gn += dot_nt(grad_v[...], w_v[...])
    grad_vecs[0:1, :] += jnp.sum(gn * unit, axis=0, keepdims=True)
    grad_vecs[1:2, :] += jnp.sum(gn, axis=0, keepdims=True)
    pulled = norm_pull(gn * vecs[0:1, :], unit, scale)
    input_grad[...] = (grad_middle[...] + pulled).astype(LOW)


def swap(values, bit, dp_size):
    if bit == "head":
        pairs = [(d * 2 + h, d * 2 + (1 - h)) for d in range(dp_size) for h in range(2)]
    else:
        pairs = [(d * 2 + h, (d ^ bit) * 2 + h) for d in range(dp_size) for h in range(2)]
    return lax.ppermute(values, AXES, pairs)


def side_of(bit):
    if bit == "head":
        return lax.axis_index("head")
    return (lax.axis_index("dp") // bit) % 2


def add_low(a, b):
    return (a.astype(F32) + b.astype(F32)).astype(LOW)


def dp_bits(first_bits, dp_size):
    spread, rest = list(first_bits), []
    bit = 4
    while bit < dp_size:
        (spread if bit <= 8 else rest).append(bit)
        bit *= 2
    return spread, rest


def scatter_sum(values, bits, dp_size):
    for bit in bits:
        halves = values.reshape((2, values.shape[0] // 2) + values.shape[1:])
        side = side_of(bit)
        sent = lax.dynamic_index_in_dim(halves, 1 - side, 0, keepdims=False)
        kept = lax.dynamic_index_in_dim(halves, side, 0, keepdims=False)
        values = add_low(kept, swap(sent, bit, dp_size))
    return values


def gather_all(values, bits, dp_size):
    for bit in reversed(bits):
        got = swap(values, bit, dp_size)
        side = side_of(bit)
        pair = jnp.stack([jnp.where(side == 0, values, got), jnp.where(side == 0, got, values)])
        values = pair.reshape((2 * values.shape[0],) + values.shape[1:])
    return values


def total_over(values, first_bits, dp_size, keep_head=False, turn=None):
    spread, rest = dp_bits(first_bits, dp_size)
    shard = scatter_sum(values, spread, dp_size)
    for bit in rest:
        shard = add_low(shard, swap(shard, bit, dp_size))
    if turn is not None:
        shard = turn(shard)
    return gather_all(shard, [b for b in spread if not (keep_head and b == "head")], dp_size)


def total_small(values, dp_size):
    spread, rest = dp_bits([1, "head", 2], dp_size)
    for bit in spread + rest:
        values = values + swap(values, bit, dp_size)
    return values


def gather_weights(weights, dp_size):
    side = lax.axis_index("dp") % 2
    head_side = lax.axis_index("head")
    half = weights.shape[1] // 2
    mine = lax.dynamic_slice_in_dim(weights, side * half, half, 1)
    first = swap(mine, "head", dp_size)
    second = swap(first, 1, dp_size)
    other = jnp.where(
        side == 0, jnp.concatenate([first, second], 1), jnp.concatenate([second, first], 1)
    )
    return jnp.where(
        head_side == 0,
        jnp.concatenate([weights, other], 1),
        jnp.concatenate([other, weights], 1),
    )


def whole(shape):
    return pl.BlockSpec(shape, lambda s, *_: (0,) * len(shape))


def by_seq(rows, lanes):
    return pl.BlockSpec((rows, lanes), lambda s, *_: (s, 0))


def across(rows, lanes):
    return pl.BlockSpec((rows, lanes), lambda s, *_: (0, s))


def shaped(shape, kind):
    return jax.ShapeDtypeStruct(shape, kind)


def call(body, grid, prefetch, in_specs, outs, scratch, flops):
    spec = pltpu.PrefetchScalarGridSpec(
        num_scalar_prefetch=prefetch,
        grid=(grid,),
        in_specs=in_specs,
        out_specs=[o[0] for o in outs],
        scratch_shapes=scratch,
    )
    return pl.pallas_call(
        body,
        grid_spec=spec,
        out_shape=[o[1] for o in outs],
        compiler_params=pltpu.CompilerParams(
            dimension_semantics=("arbitrary",), vmem_limit_bytes=VMEM_LIMIT
        ),
        cost_estimate=pl.CostEstimate(flops=flops, bytes_accessed=8 << 20, transcendentals=0),
    )


def on_device(
    dp_size,
    tokens,
    lengths,
    ln1_gain,
    ln1_bias,
    w_query,
    w_key,
    w_value,
    w_out,
    sort_first,
    sort_second,
    ln2_gain,
    ln2_bias,
    w_up,
    w_down,
    cotangent,
):
    rows_all, d = tokens.shape
    count = rows_all // LMAX
    ff = w_up.shape[1]
    side = lax.axis_index("head").astype(jnp.int32).reshape(1)
    vecs = jnp.stack([ln1_gain, ln1_bias, ln2_gain, ln2_bias])
    packed = gather_weights(jnp.concatenate([w_query, w_key, w_value, w_out.T], 0), dp_size)
    w_q, w_k, w_v, w_o = packed[:d], packed[d : 2 * d], packed[2 * d : 3 * d], packed[3 * d :].T

    square, tile, tall = whole((d, d)), by_seq(LMAX, d), across(d, LMAX)
    low_rows, wide_rows = shaped((rows_all, d), LOW), shaped((rows_all, d), F32)
    low_cols = shaped((d, rows_all), LOW)
    plan_tile = pl.BlockSpec((1, NB, NB), lambda s, *_: (s, 0, 0))
    small_plan = shaped((count, NB, NB), F32)

    normed, normed_t, summary, pre, steps, plan = call(
        functools.partial(prepare_kernel, count), 1, 2,
        [whole((rows_all, d)), whole((4, d)), square, whole((d, NB))],
        [
            (whole((rows_all, d)), low_rows),
            (whole((d, rows_all)), low_cols),
            (whole((count * NB, d)), shaped((count * NB, d), F32)),
            (whole((count * NB, d)), shaped((count * NB, d), F32)),
            (whole((2 * ITERS, count, NB, NB)), shaped((2 * ITERS, count, NB, NB), F32)),
            (whole((count, NB, NB)), small_plan),
        ],
        [], 1 << 28,
    )(lengths, side, tokens, vecs, sort_first, sort_second)

    p_tile = by_seq(2 * LMAX, LMAX)
    p_shape = shaped((count * 2 * LMAX, LMAX), LOW)
    q, k, v, sk, sv, p, mixed, mixed_t, middle, normed2, normed2_t, cot_t = call(
        functools.partial(forward_kernel, count), count, 2,
        [tile, tile, tile, plan_tile] + [square] * 4 + [whole((4, d))],
        [(tile, low_rows)] * 5
        + [(p_tile, p_shape), (tile, low_rows), (tall, low_cols), (tile, wide_rows)]
        + [(tile, low_rows), (tall, low_cols), (tall, low_cols)],
        [pltpu.VMEM((LMAX, d), LOW)], 4 << 30,
    )(lengths, side, normed, tokens, cotangent, plan, w_q, w_k, w_v, w_o, vecs)

    part = 256
    pieces = ff // part
    all_rows = whole((rows_all, d))
    chunk = pl.BlockSpec((1, d, part), lambda f: (f, 0, 0))
    chunks = shaped((pieces, d, part), LOW)
    output, grad_norm2, grad_up, grad_down_t = call(
        functools.partial(ffn_kernel, pieces, rows_all), pieces, 0,
        [all_rows, all_rows, whole((d, rows_all)), all_rows, whole((d, rows_all))]
        + [pl.BlockSpec((d, part), lambda f: (0, f)), pl.BlockSpec((part, d), lambda f: (f, 0))],
        [(all_rows, low_rows), (all_rows, wide_rows), (chunk, chunks), (chunk, chunks)],
        [
            pltpu.VMEM((rows_all, part), F32),
            pltpu.VMEM((rows_all, part), LOW),
            pltpu.VMEM((rows_all, part), LOW),
            pltpu.VMEM((rows_all, part), LOW),
            pltpu.VMEM((rows_all, d), F32),
        ],
        12 * rows_all * d * ff,
    )(middle, normed2, normed2_t, cotangent, cot_t, w_up, w_down)

    wide_part = pltpu.VMEM((LMAX, d), F32)
    grad_middle, grad_q, grad_k, grad_v, grad_plan, grad_w, grad_wo, vecs2 = call(
        functools.partial(backward_kernel, count), count, 2,
        [tile, tile, tile, tall, tall, plan_tile] + [tile] * 5 + [p_tile, square, whole((4, d))],
        [(tile, wide_rows)] + [(tile, low_rows)] * 3
        + [(plan_tile, small_plan), (whole((3, d, d)), shaped((3, d, d), LOW))]
        + [(square, shaped((d, d), LOW)), (whole((4, d)), shaped((4, d), F32))],
        [pltpu.VMEM((LMAX, d), LOW)] * 2 + [wide_part] * 4
        + [pltpu.VMEM((3, d, d), F32), pltpu.VMEM((d, d), F32)],
        8 << 30,
    )(
        lengths, side, grad_norm2, middle, cotangent, normed_t, mixed_t, plan,
        q, k, v, sk, sv, p, w_o, vecs,
    )

    input_grad, grad_first, grad_second, vecs1 = call(
        functools.partial(finish_kernel, count), count, 2,
        [tile, tile, tile, tile, tile, square, square, square, whole((4, d))]
        + [whole((count, NB, NB))] * 2
        + [whole((2 * ITERS, count, NB, NB)), whole((count * NB, d)), whole((count * NB, d))]
        + [square, whole((d, NB))],
        [
            (tile, low_rows),
            (square, shaped((d, d), LOW)),
            (whole((d, NB)), shaped((d, NB), F32)),
            (whole((4, d)), shaped((4, d), F32)),
        ],
        [pltpu.VMEM((count * NB, d), F32)], 2 << 30,
    )(
        lengths, side, tokens, grad_middle, grad_q, grad_k, grad_v, w_q, w_k, w_v, vecs,
        grad_plan, plan, steps, pre, summary, sort_first, sort_second,
    )

    y_first, x_first = [1, "head", 2], [1, 2, "head"]
    quarter = d // 4
    up_sum = total_over(grad_up.reshape(pieces * d, part), y_first, dp_size)
    down_sum = total_over(
        grad_down_t.reshape(pieces * d, part), x_first, dp_size, turn=lambda shard: shard.T
    )
    half = d // 2
    heads = jnp.concatenate(
        [
            grad_w.reshape(3, d, 2, half).transpose(2, 0, 1, 3).reshape(2, 3 * d, half),
            grad_wo.reshape(2, half, 2, half).transpose(0, 2, 1, 3).reshape(2, d, half),
        ],
        1,
    )
    heads = total_over(heads.reshape(8 * d, half), ["head", 1, 2], dp_size, keep_head=True)
    heads = heads.astype(F32).reshape(4, d, half)
    first_sum = total_over(grad_first, x_first, dp_size).astype(F32)
    small = jnp.concatenate([vecs1[:2], vecs2[2:4], grad_second.T], 0)
    small = total_small(jnp.pad(small, ((0, 4), (0, 0))), dp_size)
    return (
        output,
        input_grad,
        small[0],
        small[1],
        heads[0],
        heads[1],
        heads[2],
        heads[3].reshape(2, half, half).transpose(1, 0, 2).reshape(half, d),
        first_sum,
        small[4 : 4 + NB].T,
        small[2],
        small[3],
        up_sum.astype(F32).reshape(pieces, d, part).transpose(1, 0, 2).reshape(d, ff),
        down_sum.astype(F32).reshape(pieces, 4, part, quarter).transpose(0, 2, 1, 3).reshape(ff, d),
    )


def solution(mesh):
    tokens, copied, columns = P(AXES, None), P(), P(None, "head")
    return jax.shard_map(
        functools.partial(on_device, mesh.shape["dp"]),
        mesh=mesh,
        in_specs=(tokens, P("dp"), copied, copied, columns, columns, columns, P("head", None))
        + (copied,) * 6
        + (tokens,),
        out_specs=(tokens, tokens, copied, copied, columns, columns, columns, P("head", None))
        + (copied,) * 6,
        check_vma=False,
    )
```

```python
import functools

import jax
import jax.numpy as jnp
from jax import lax
from jax.experimental import pallas as pl
from jax.experimental.pallas import tpu as pltpu
from jax.sharding import PartitionSpec as P

HD = 64
BL = 32
ITERS = 8
LMAX = 256
NB = LMAX // BL
SUMMARY_SCALE = BL**-0.5
F32 = jnp.float32
LOW = jnp.bfloat16
AXES = ("dp", "head")
VMEM_LIMIT = 56 * 1024 * 1024
TURNS = ["last", "ffn"] * 3 + ["last"] + ["last", "ffn"] * 2 + ["last"] + ["ffn", "last"]

ERF_P = 0.3875
ERF_C = (
    0.23607149955804155,
    0.07450957017858355,
    0.6926085194492264,
    -0.6975625302575207,
    0.9269567150083973,
    -0.23258376165572045,
)


def normal_parts(v):
    size = jnp.abs(v)
    bell = jnp.exp(v * v * -0.5)
    t = 1.0 / (1.0 + size * (ERF_P * 0.5**0.5))
    poly = ERF_C[5]
    for coef in ERF_C[4::-1]:
        poly = poly * t + coef
    tail = (0.5 * t) * poly * bell
    return jnp.where(v >= 0, 1.0 - tail, tail), bell * 0.3989422804014327


def dot_nn(a, b):
    return lax.dot_general(a, b, (((1,), (0,)), ((), ())), preferred_element_type=F32)


def dot_nt(a, b):
    return lax.dot_general(a, b, (((1,), (1,)), ((), ())), preferred_element_type=F32)


def dot_tn(a, b):
    return lax.dot_general(a, b, (((0,), (0,)), ((), ())), preferred_element_type=F32)


def split3(v):
    high = v.astype(LOW)
    left = v - high.astype(F32)
    mid = left.astype(LOW)
    return high, mid, (left - mid.astype(F32)).astype(LOW)


def split2(v):
    high = v.astype(LOW)
    return high, (v - high.astype(F32)).astype(LOW)


def exact_right(dot, v, w):
    a, b, c = split3(v)
    return dot(a, w) + dot(b, w) + dot(c, w)


def exact_both(dot, v, w):
    a, b, c = split3(v)
    d, e, f = split3(w)
    return dot(a, d) + (dot(a, e) + dot(b, d)) + (dot(b, e) + dot(a, f) + dot(c, d))


def row_norm(x):
    center = x - jnp.mean(x, axis=-1, keepdims=True)
    spread = jnp.mean(center * center, axis=-1, keepdims=True)
    scale = lax.rsqrt(spread + 1e-05)
    return center * scale, scale


def norm_pull(grad, unit, scale):
    return scale * (
        grad
        - jnp.mean(grad, axis=-1, keepdims=True)
        - unit * jnp.mean(grad * unit, axis=-1, keepdims=True)
    )


def iota(shape, axis):
    return lax.broadcasted_iota(jnp.int32, shape, axis)


def plan_allowed(count, spans):
    shape = (count, NB, NB)
    seq = iota(shape, 0)
    span = jnp.zeros(shape, jnp.int32)
    for s in range(count):
        span = jnp.where(seq == s, spans[s], span)
    row, col = iota(shape, 1), iota(shape, 2)
    row_ok, col_ok = row * BL < span, col * BL < span
    return (row_ok & col_ok) | ((row == col) & ~row_ok)


def head_mask(value):
    row, lane = iota((LMAX, 8 * HD), 0), iota((LMAX, 8 * HD), 1)
    return jnp.where(row // BL == lane // HD, value, 0.0).astype(LOW)


def spread_plan(plan, flip):
    pick = jnp.where(iota((LMAX, NB), 0) // BL == iota((LMAX, NB), 1), 1.0, 0.0).astype(LOW)
    same = (iota((LMAX, LMAX), 0) % BL) == (iota((LMAX, LMAX), 1) % BL)
    parts = []
    for part in split2(plan):
        tall = (dot_nt if flip else dot_nn)(pick, part).astype(LOW)
        parts.append(jnp.where(same, dot_nt(tall, pick), 0.0).astype(LOW))
    return parts


def pair_rows(left_t, right, m, lane_low):
    both = dot_nn(left_t[2 * BL * m : 2 * BL * (m + 1), :], right[:, 2 * HD * m : 2 * HD * (m + 1)])
    return jnp.where(lane_low, both[:BL], both[BL:])


PART = 256
PIECE = 64


def prepare_kernel(
    count, lens, ids, tokens, ln_gain, ln_bias, first, second, cotangent, down,
    normed, normed_t, summary, pre, steps, plan, cot_t, grad_hidden,
):
    spans = [lens[ids[2] * count + s] for s in range(count)]
    tokens.wait()
    ln_gain.wait()
    ln_bias.wait()
    gain, bias = ln_gain[...], ln_bias[...]
    for s in range(count):
        rows = pl.ds(s * LMAX, LMAX)
        unit, _ = row_norm(tokens[rows, :].astype(F32))
        low = (unit * gain + bias).astype(LOW)
        normed[rows, :] = low
        normed_t[:, rows] = low.T
        token, block = iota((NB, LMAX), 1), iota((NB, LMAX), 0)
        member = (token // BL == block) & (token < spans[s])
        picked = jnp.where(member, 1.0, 0.0).astype(LOW)
        summary[pl.ds(s * NB, NB), :] = dot_nn(picked, low) * SUMMARY_SCALE
    for out in (normed, normed_t, summary):
        out.send()
    for value in (first, second, cotangent, down):
        value.wait()
    before = exact_right(dot_nn, summary[...], first[...])
    pre[...] = before
    gate, _ = normal_parts(before)
    logits = exact_right(dot_nt, before * gate, second[...])
    logits = logits.reshape(count, NB, NB)
    x = jnp.where(plan_allowed(count, spans), logits, -1e30)
    for k in range(2 * ITERS):
        axis = 2 - k % 2
        top = jnp.max(x, axis=axis, keepdims=True)
        x = x - (top + jnp.log(jnp.sum(jnp.exp(x - top), axis=axis, keepdims=True)))
        steps[k] = x
    plan[...] = jnp.exp(x)
    for out in (pre, steps, plan):
        out.send()
    rows = cotangent[...]
    for s in range(count):
        seq = slice(s * LMAX, (s + 1) * LMAX)
        cot_t[:, seq] = cotangent[seq, :].T
    cot_t.send()
    for at in range(0, down.shape[0], PART):
        grad_hidden[:, at : at + PART] = dot_nt(rows, down[at : at + PART, :]).astype(LOW)


def forward_kernel(
    count, lens, ids, w_q, w_k, w_v, w_o, near_w, far_w, normed, plan, tokens, ln_gain, ln_bias,
    up, grad_hidden, cot_t, down, cotangent,
    q_out, k_out, v_out, sk_out, sv_out, p_out, w_all, sent, kept, output, grad_middle, grad_att,
    grad_vecs,
    mask, mixed, mixed_t, middle, normed2, normed2_t, up0, up1, hid0, hid1, gup0, gup1, out_s, gn_s,
    grad_s, part_sems,
):
    mask[...] = head_mask(HD**-0.5)
    for value in (w_q, w_k, w_v, w_o, near_w, far_w, normed, plan):
        value.wait()
    core, head = ids[0], ids[2]
    half, quarter = 4 * HD, 2 * HD
    own = pl.ds(pl.multiple_of(head * half, half), half)
    near = pl.ds(pl.multiple_of((1 - head) * half + core * quarter, quarter), quarter)
    far = pl.ds(pl.multiple_of((1 - head) * half + (1 - core) * quarter, quarter), quarter)
    for slot, w in enumerate((w_q, w_k, w_v)):
        w_all[slot, :, own] = w[...]
        w_all[slot, :, near] = near_w[512 * slot : 512 * (slot + 1), :]
        w_all[slot, :, far] = far_w[512 * slot : 512 * (slot + 1), :]
    w_all[3, own, :] = w_o[...]
    for m in range(4):
        lanes, rows = slice(128 * m, 128 * (m + 1)), slice(1536 + 128 * m, 1664 + 128 * m)
        w_all[3, near, lanes] = near_w[rows, :]
        w_all[3, far, lanes] = far_w[rows, :]
    w_all.send()
    keep_row = iota((LMAX, 8 * HD), 0)
    key_row = iota((2 * BL, 8 * BL), 0)
    query = iota((2 * BL, 8 * BL), 1) % BL
    lane_low = iota((BL, 2 * HD), 1) < HD

    def one(s, carry):
        span = lens[ids[2] * count + s]
        seq = pl.ds(pl.multiple_of(s * LMAX, LMAX), LMAX)
        n = normed[seq, :]
        keep = keep_row < span
        q_out[seq, :] = dot_nn(n, w_all[0]).astype(LOW)
        key = jnp.where(keep, dot_nn(n, w_all[1]), 0.0).astype(LOW)
        value = jnp.where(keep, dot_nn(n, w_all[2]), 0.0).astype(LOW)
        k_out[seq, :] = key
        v_out[seq, :] = value
        high, low = spread_plan(plan[s], False)
        sk_out[seq, :] = (dot_nn(high, key) + dot_nn(low, key)).astype(LOW)
        sv_out[seq, :] = (dot_nn(high, value) + dot_nn(low, value)).astype(LOW)
        for i in range(NB):
            rows = pl.ds(pl.multiple_of(s * LMAX + i * BL, BL), BL)
            keys = jnp.concatenate([k_out[rows, :], sk_out[rows, :]], 0)
            values = jnp.concatenate([v_out[rows, :], sv_out[rows, :]], 0)
            wide = jnp.concatenate([q_out[rows, :]] * 8, 0) * mask[...]
            scores = dot_nt(keys, wide)
            valid = jnp.where(key_row < BL, i * BL + key_row, i * BL) < span
            scores = jnp.where(valid | (i * BL + query >= span), scores, -1e30)
            top = jnp.max(scores, axis=0, keepdims=True)
            grown = jnp.exp(scores - top)
            weights = grown * (1.0 / jnp.sum(grown, axis=0, keepdims=True))
            at = pl.multiple_of(s * 2 * LMAX + i * 2 * BL, 2 * BL)
            p_out[pl.ds(at, 2 * BL), :] = weights.astype(LOW)
            weights_t = weights.T.astype(LOW)
            outs = [pair_rows(weights_t, values, m, lane_low) for m in range(4)]
            out = jnp.concatenate(outs, 1)
            out = jnp.where(iota((BL, 8 * HD), 0) + i * BL < span, out, 0.0)
            mixed[i * BL : (i + 1) * BL, :] = out.astype(LOW)
        blended = mixed[...]
        mixed_t[:, seq] = blended.T

        @pl.when(s == 0)
        def _():
            tokens.wait()
            ln_gain.wait()
            ln_bias.wait()

        mid = tokens[seq, :].astype(F32) + dot_nn(blended, w_all[3])
        middle[seq, :] = mid
        unit, _ = row_norm(mid)
        low2 = (unit * ln_gain[...] + ln_bias[...]).astype(LOW)
        normed2[seq, :] = low2
        normed2_t[:, seq] = low2.T
        return carry

    lax.fori_loop(0, count, one, 0)
    for out in (q_out, k_out, v_out, sk_out, sv_out, p_out):
        out.send()
    for value in (up, grad_hidden, cot_t, down, cotangent):
        value.wait()
    units = up.shape[1] // PART // 2
    quarter = normed.shape[1] // 4
    ups, hids, gups = (up0, up1), (hid0, hid1), (gup0, gup1)

    def columns(c):
        unit = ((c // units) ^ (1 - core)) * units + c % units
        return pl.ds(pl.multiple_of(unit * PART, PART), PART)

    def expand(c, side):
        ups[side][...] = dot_nn(normed2[...], up[:, columns(c)])

    def gate(c, side):
        for r in range(up0.shape[0] // PIECE):
            rows = slice(r * PIECE, (r + 1) * PIECE)
            v = ups[side][rows, :]
            share, bell = normal_parts(v)
            hids[side][rows, :] = (v * share).astype(LOW)
            gh = grad_hidden[rows, columns(c)].astype(F32)
            gups[side][rows, :] = (gh * (share + v * bell)).astype(LOW)

    def reduce(c, side, target):
        hidden, gup = hids[side][...], gups[side][...]
        for color, (left, right) in enumerate(((normed2_t, gup), (cot_t, hidden))):
            grad = dot_nn(left[...], right).astype(LOW)
            for j in range(PART // 128):
                for i in range(4):
                    tile = grad[quarter * i : quarter * (i + 1), 128 * j : 128 * (j + 1)]
                    target.buffer[color, c % units, i, quarter * j : quarter * (j + 1), :] = tile
        out_s[...] += dot_nn(hidden, down[columns(c), :])
        gn_s[...] += dot_nt(gup, up[:, columns(c)])

    def part_copy(n, c, target):
        at = (slice(None), c % units, slice(None), slice(0, PART))
        return pltpu.make_async_copy(target.buffer.at[at], target.target.at[at], part_sems.at[n])

    out_s[...] = jnp.zeros_like(out_s)
    gn_s[...] = jnp.zeros_like(gn_s)
    expand(0, 0)
    expand(1, 1)
    gate(0, 0)
    for c in range(1, 2 * units):
        side = c % 2
        if c + 1 < 2 * units:
            expand(c + 1, 1 - side)
        gate(c, side)
        reduce(c - 1, 1 - side, sent if c - 1 < units else kept)
        if c >= 2:
            part_copy(c - 2, c - 2, sent if c - 2 < units else kept).start()
    c = 2 * units - 1
    reduce(c, c % 2, kept)
    part_copy(c - 1, c - 1, kept).start()
    gain = jnp.zeros((1, middle.shape[1]), F32)
    bias = jnp.zeros((1, middle.shape[1]), F32)
    for s in range(count):
        seq = slice(s * LMAX, (s + 1) * LMAX)
        gn, mid = gn_s[seq, :], middle[seq, :]
        unit, scale = row_norm(mid)
        gain += jnp.sum(gn * unit, axis=0, keepdims=True)
        bias += jnp.sum(gn, axis=0, keepdims=True)
        gmid = cotangent[seq, :].astype(F32) + norm_pull(gn * ln_gain[...], unit, scale)
        grad_middle[seq, :] = gmid
        grad_att[seq, :] = gmid.astype(LOW)
        output[seq, :] = (mid + out_s[seq, :]).astype(LOW)
    for out in (grad_att, grad_middle, output):
        out.send()
    grad_vecs[0:1, :] = gain
    grad_vecs[1:2, :] = bias
    part_copy(c, c, kept).start()
    grad_s[...] = dot_nn(mixed_t[...], grad_att[...])
    tails = []
    for n, target in enumerate((sent, kept)):
        base = (core ^ (1 - n)) * units
        for j in range(units):
            for m in range(4):
                for h in range(2):
                    at = pl.multiple_of((base + j) * 64 + 32 * h, 32)
                    tile = grad_s[pl.ds(at, 32), 128 * m : 128 * (m + 1)].astype(LOW)
                    target.buffer[m // 2, j, 2 * (m % 2) + h, PART : PART + 32, :] = tile
        at = (slice(None), slice(None), slice(None), slice(PART, PART + 32))
        tail = pltpu.make_async_copy(
            target.buffer.at[at], target.target.at[at], part_sems.at[2 * units + n]
        )
        tail.start()
        tails.append(tail)
    for n in range(2 * units):
        part_copy(n, n, sent if n < units else kept).wait()
    for tail in tails:
        tail.wait()


def scatter_tiles(core, sent, kept, wide, base):
    for n, target in enumerate((sent, kept)):
        for color in range(2):
            for u in range(4):
                at = (color * 8 + (core ^ (1 - n)) * 4 + u) * 32
                tile = wide[pl.ds(pl.multiple_of(at, 32), 32), :].astype(LOW)
                for p in range(4):
                    for m in range(4):
                        part = tile[8 * p : 8 * (p + 1), 128 * m : 128 * (m + 1)]
                        low = slice(base + 8 * m, base + 8 * (m + 1))
                        target[color, u, p, low, :] = part


def backward_one(
    local, plan_at, span, grad_att, w_o, q_in, k_in, v_in, sk_in, sv_in, p_in, plan,
    grad_q, grad_k, grad_v, grad_plan, mask, go_s, dks, dvs, dk_own, dv_own,
):
    base = local * LMAX
    seq = pl.ds(pl.multiple_of(base, LMAX), LMAX)
    gmixed = dot_nt(grad_att[seq, :], w_o[...]).astype(LOW)
    keep = iota((LMAX, 8 * HD), 0) < span
    go_s[...] = jnp.where(keep, gmixed, jnp.zeros_like(gmixed))
    lane_low = iota((BL, 2 * HD), 1) < HD
    for i in range(NB):
        rows = pl.ds(pl.multiple_of(base + i * BL, BL), BL)
        own_rows = slice(i * BL, (i + 1) * BL)
        keys = jnp.concatenate([k_in[rows, :], sk_in[rows, :]], 0)
        values = jnp.concatenate([v_in[rows, :], sv_in[rows, :]], 0)
        gwide = jnp.concatenate([go_s[own_rows, :]] * 8, 0) * mask[...]
        qwide = jnp.concatenate([q_in[rows, :]] * 8, 0) * mask[...]
        weights = p_in[pl.ds(pl.multiple_of(2 * base + i * 2 * BL, 2 * BL), 2 * BL), :]
        wide = weights.astype(F32)
        gweights = dot_nt(values, gwide)
        dv = dot_nn(weights, gwide)
        total = jnp.sum(wide * gweights, axis=0, keepdims=True)
        gscores = wide * (gweights - total)
        dk = dot_nn(gscores.astype(LOW), qwide) * HD**-0.5
        gscores_t = gscores.T.astype(LOW)
        dq = jnp.concatenate([pair_rows(gscores_t, keys, m, lane_low) for m in range(4)], 1)
        grad_q[rows, :] = (dq * HD**-0.5).astype(LOW)
        dk_own[own_rows, :] = dk[:BL]
        dks[own_rows, :] = dk[BL:]
        dv_own[own_rows, :] = dv[:BL]
        dvs[own_rows, :] = dv[BL:]
    same = (iota((LMAX, LMAX), 0) % BL) == (iota((LMAX, LMAX), 1) % BL)
    high, low = spread_plan(plan[plan_at], True)
    cross = jnp.zeros((LMAX, LMAX), F32)
    for own, sorted_part, kept, target in (
        (dk_own, dks, k_in, grad_k),
        (dv_own, dvs, v_in, grad_v),
    ):
        g_high, g_low = split2(sorted_part[...])
        kept_rows = kept[seq, :]
        cross += dot_nt(g_high, kept_rows) + dot_nt(g_low, kept_rows)
        total = own[...] + (dot_nn(high, g_high) + (dot_nn(high, g_low) + dot_nn(low, g_high)))
        target[seq, :] = jnp.where(keep, total, 0.0).astype(LOW)
    cross = jnp.where(same, cross, 0.0)
    rows8 = jnp.sum(cross.reshape(NB, BL, LMAX), axis=1)
    pick = jnp.where(iota((LMAX, NB), 0) // BL == iota((LMAX, NB), 1), 1.0, 0.0).astype(LOW)
    grad_plan[local] = exact_right(dot_nn, rows8, pick)


def backward_kernel(
    first, count, lens, ids, grad_att, w_all, q_in, k_in, v_in, sk_in, sv_in, p_in, plan,
    grad_q, grad_k, grad_v, grad_plan, mask, *own,
):
    mask[...] = head_mask(1.0)
    ins = (grad_att, w_all, q_in, k_in, v_in, sk_in, sv_in, p_in, plan)
    for value in ins:
        value.wait()
    ins = (grad_att, w_all.buffer.at[0], *ins[2:])

    def one(n, carry):
        span = lens[ids[2] * count + first + n]
        backward_one(
            n, first + n, span, *ins, grad_q, grad_k, grad_v, grad_plan, mask, *own
        )
        return carry

    lax.fori_loop(0, grad_q.shape[0] // LMAX, one, 0)


def last_kernel(cuts, count, lens, ids, grad_att, w_all, q_in, k_in, v_in, sk_in, sv_in, p_in, plan, *refs):
    first, groups = cuts[-2], len(cuts) - 2
    early, refs = refs[: 4 * groups], refs[4 * groups :]
    normed_t, steps, pre, summary, sort_one, sort_two, ln_gain, vecs2, tokens, grad_middle = refs[:10]
    sent, kept, input_grad, mask, go_s, dks, dvs, dk_own, dv_own = refs[10:19]
    grad_q, grad_k, grad_v, grad_plan, gsum, small, grad_s = refs[19:]
    mask[...] = head_mask(1.0)
    ins = (grad_att, w_all, q_in, k_in, v_in, sk_in, sv_in, p_in, plan)
    for value in ins:
        value.wait()
    ins = (grad_att, w_all.buffer.at[3], *ins[2:])
    own = (mask, go_s, dks, dvs, dk_own, dv_own)

    def one(n, carry):
        span = lens[ids[2] * count + first + n]
        backward_one(n, first + n, span, *ins, grad_q, grad_k, grad_v, grad_plan, *own)
        return carry

    lax.fori_loop(0, count - first, one, 0)
    for value in (*early, normed_t, steps):
        value.wait()
    kinds = [list(early[n::4]) + [late] for n, late in enumerate((grad_q, grad_k, grad_v, grad_plan))]
    spans = [lens[ids[2] * count + c] for c in range(count)]
    g = jnp.concatenate([r[...] for r in kinds[3]], 0) * plan[...]
    for k in range(2 * ITERS - 1, -1, -1):
        axis = 2 - k % 2
        g = g - jnp.exp(steps[k]) * jnp.sum(g, axis=axis, keepdims=True)
    g = jnp.where(plan_allowed(count, spans), g, 0.0).reshape(count * NB, NB)
    d = normed_t.shape[0]
    for slot in range(3):
        grad = jnp.zeros((d, d), F32)
        for n, rows in enumerate(kinds[slot]):
            grad += dot_nn(normed_t[:, cuts[n] * LMAX : cuts[n + 1] * LMAX], rows[...])
        grad_s[...] = grad
        scatter_tiles(ids[0], sent, kept, grad_s, 32 * slot)
    for value in (pre, summary, sort_one, sort_two, ln_gain, vecs2, tokens, grad_middle):
        value.wait()
    before = pre[...]
    share, bell = normal_parts(before)
    small[...] = jnp.zeros_like(small)
    small[0:NB, :] = exact_both(dot_tn, g, before * share)
    small[10:12, :] = vecs2[...]
    gpre = exact_right(dot_nn, g, sort_two[...]) * (share + before * bell)
    grad_s[...] = exact_both(dot_tn, summary[...], gpre)
    scatter_tiles(ids[0], sent, kept, grad_s, 96)
    gsum[...] = exact_right(dot_nt, gpre, sort_one[...]) * SUMMARY_SCALE
    gain, bias = jnp.zeros((1, d), F32), jnp.zeros((1, d), F32)
    token, block = iota((LMAX, NB), 0), iota((LMAX, NB), 1)
    for s in range(count):
        seq = slice(s * LMAX, (s + 1) * LMAX)
        unit, scale = row_norm(tokens[seq, :].astype(F32))
        member = (token // BL == block) & (token < spans[s])
        picked = jnp.where(member, 1.0, 0.0).astype(LOW)
        high, mid, low = split3(gsum[s * NB : (s + 1) * NB, :])
        gn = dot_nn(picked, high) + dot_nn(picked, mid) + dot_nn(picked, low)
        for slot in range(3):
            group = max(n for n in range(groups + 1) if cuts[n] <= s)
            at = (s - cuts[group]) * LMAX
            gn += dot_nt(kinds[slot][group][at : at + LMAX, :], w_all[slot])
        gain += jnp.sum(gn * unit, axis=0, keepdims=True)
        bias += jnp.sum(gn, axis=0, keepdims=True)
        pulled = norm_pull(gn * ln_gain[...], unit, scale)
        input_grad[seq, :] = (grad_middle[seq, :] + pulled).astype(LOW)
    small[8:9, :] = gain
    small[9:10, :] = bias
    zeros = jnp.zeros((8, 128), LOW)
    for n, target in enumerate((sent, kept)):
        at = pl.ds(pl.multiple_of((ids[0] ^ (1 - n)) * 8, 8), 8)
        for u in range(4):
            tile = small[at, 128 * u : 128 * (u + 1)].astype(LOW)
            for color in range(2):
                for i in range(4):
                    target[color, u, i, 128:136, :] = tile if color == 0 and i == 0 else zeros


def pieces_of(ids, near, far):
    core, x, head = ids[0], ids[1], ids[2]
    for color in range(2):
        one, two = ((head, x), (x, head))[color]
        for r in range(8):
            unit = (core ^ (r // 4)) * 4 + (one ^ (r // 2 % 2)) * 2 + (two ^ (r % 2))
            for i in range(4):
                part = (ids[3] ^ (i // 2)) * 2 + (ids[4] ^ (i % 2))
                yield color, unit, part, (near, far)[r // 4].buffer.at[color, r % 4, i // 2, i % 2]


def place_ffn_kernel(ids, near, far, grad_up, grad_down, grad_o, o_s):
    near.wait()
    far.wait()
    for color, unit, part, source in pieces_of(ids, near, far):
        quarter = pl.ds(pl.multiple_of(part * 128, 128), 128)
        for j in range(2):
            at = pl.ds(pl.multiple_of(unit * PART + 128 * j, 128), 128)
            block = source[128 * j : 128 * (j + 1), :].astype(F32)
            if color == 0:
                grad_up[quarter, at] = block
            else:
                grad_down[at, quarter] = block.T
        rows = pl.ds(pl.multiple_of(unit * 64 + (part % 2) * 32, 32), 32)
        lanes = pl.ds(pl.multiple_of(256 * color + (part // 2) * 128, 128), 128)
        o_s[rows, lanes] = source[PART : PART + 32, :].astype(F32)
    grad_o[...] = o_s[pl.ds(pl.multiple_of(ids[2] * 256, 256), 256), :]


def place_last_kernel(
    ids, near, far, grad_q, grad_k, grad_v, grad_first, second, gain1, bias1, gain2, bias2, wide, small
):
    near.wait()
    far.wait()
    head = ids[2]
    for color, unit, part, source in pieces_of(ids, near, far):
        rows = pl.ds(pl.multiple_of(color * 256 + unit * 32 + part * 8, 8), 8)
        wide[...] = source[...].astype(F32)
        for slot, out in enumerate((grad_q, grad_k, grad_v)):
            for t in range(2):
                at = pl.ds(pl.multiple_of((4 * slot + 2 * head + t) * 8, 8), 8)
                out[rows, 128 * t : 128 * (t + 1)] = wide[at, :]
        for m in range(4):
            grad_first[rows, 128 * m : 128 * (m + 1)] = wide[96 + 8 * m : 104 + 8 * m, :]
        if color == 0:
            high = pl.ds(pl.multiple_of((unit // 4) * 8, 8), 8)
            lanes = pl.ds(pl.multiple_of((unit % 4) * 128, 128), 128)
            small[part, high, lanes] = wide[128:136, :]
    second[...] = small[0, 0:NB, :]
    for n, out in enumerate((gain1, bias1, gain2, bias2)):
        out[...] = small[0, 8 + n : 9 + n, :]


def slice_kernel(ids, w_q, w_k, w_v, w_o, mine):
    core = ids[0]
    lanes = pl.ds(pl.multiple_of(core * 2 * HD, 2 * HD), 2 * HD)
    for slot, w in enumerate((w_q, w_k, w_v)):
        w.wait()
        mine[512 * slot : 512 * (slot + 1), :] = w[:, lanes]
    w_o.wait()
    for m in range(4):
        mine[1536 + 128 * m : 1664 + 128 * m, :] = w_o[lanes, 128 * m : 128 * (m + 1)]


def swap(values, bit, dp_size):
    if bit == "head":
        pairs = [(d * 2 + h, d * 2 + (1 - h)) for d in range(dp_size) for h in range(2)]
    else:
        pairs = [(d * 2 + h, (d ^ bit) * 2 + h) for d in range(dp_size) for h in range(2)]
    return lax.ppermute(values, AXES, pairs)


def side_of(bit):
    if bit == "head":
        return lax.axis_index("head")
    return (lax.axis_index("dp") // bit) % 2


def pick(values, index, axis=0):
    return lax.dynamic_index_in_dim(values, index, axis, keepdims=False)


def halves(kept, got, bit, axis):
    side = side_of(bit)
    mine = pick(kept, side, axis).astype(F32) + pick(got, side, axis).astype(F32)
    other = pick(kept, 1 - side, axis).astype(F32) + pick(got, 1 - side, axis).astype(F32)
    return mine, other.astype(LOW)


def line_bits(dp_size):
    bits, bit = [], 4
    while bit < dp_size:
        bits.append(bit)
        bit *= 2
    return bits


def sum_chain(sent, kept, dp_size):
    order = (("head", 2), (2, "head"))
    line = line_bits(dp_size)
    got = swap(sent, 1, dp_size)
    got, = yield [sent], [got]
    shape = (2, 2, 2, 2) + kept.shape[3:]
    sums = [(kept[c].reshape(shape), got[c].reshape(shape)) for c in range(2)]
    for turn in range(2):
        parts = [halves(*sums[c], order[c][turn], 0) for c in range(2)]
        gots = [swap(parts[c][1], order[c][turn], dp_size) for c in range(2)]
        gots = yield [part[1] for part in parts], gots
        sums = [(parts[c][0], gots[c]) for c in range(2)]
    kept, got = (jnp.stack([pair[n].astype(F32) for pair in sums]) for n in range(2))
    for turn, bit in enumerate(line[:2]):
        kept, sent = halves(kept, got, bit, 1)
        got = swap(sent, bit, dp_size)
        got, = yield [sent], [got]
    near = (kept + got.astype(F32)).astype(LOW)
    for bit in line[2:]:
        got = swap(near, bit, dp_size)
        got, = yield [near], [got]
        near = (near.astype(F32) + got.astype(F32)).astype(LOW)
    near = near[:, None]
    got = swap(near, line[1], dp_size)
    got, = yield [near], [got]
    near = jnp.concatenate([near, got], 1)[:, None]
    got = swap(near, line[0], dp_size)
    got, = yield [near], [got]
    near = jnp.concatenate([near, got], 1)
    near = [near[c][None] for c in range(2)]
    for turn in (1, 0):
        gots = [swap(near[c], order[c][turn], dp_size) for c in range(2)]
        gots = yield near, gots
        near = [jnp.concatenate([near[c], gots[c]], 0) for c in range(2)]
    near = jnp.stack(near)
    far = swap(near, 1, dp_size)
    far, = yield [near], [far]
    return near, far


class Slots:
    def __init__(self):
        self.running, self.done, self.got = {}, {}, {}

    def start(self, name, chain):
        self.running[name], self.got[name] = chain, None

    def step(self):
        sent = []
        for name, chain in list(self.running.items()):
            try:
                new, self.got[name] = chain.send(self.got[name])
                sent += new
            except StopIteration as end:
                self.done[name] = end.value
                del self.running[name], self.got[name]
        return sent

    def before(self, value):
        return lax.optimization_barrier((value, *self.step()))[0]

    def after(self, value):
        names = list(self.running)
        sizes = [len(self.got[n]) for n in names]
        flat = [g for n in names for g in self.got[n]]
        flat = lax.optimization_barrier((value, *flat))[1:]
        for name, size in zip(names, sizes):
            self.got[name], flat = list(flat[:size]), flat[size:]

    def turn(self, name, last):
        if name not in self.running:
            return last
        got = self.got[name]
        if got is not None:
            self.got[name] = list(lax.optimization_barrier((*got, *last))[: len(got)])
        try:
            sent, self.got[name] = self.running[name].send(self.got[name])
            return sent
        except StopIteration as end:
            self.done[name] = end.value
            del self.running[name]
            return last


def shaped(shape, kind):
    return jax.ShapeDtypeStruct(shape, kind)


class Staged:
    def __init__(self, buffer, copy, target=None, by_parts=False):
        self.buffer, self.copy, self.target = buffer, copy, target
        self.sent, self.by_parts = by_parts, by_parts

    def wait(self):
        self.copy.wait()

    def send(self):
        if not self.sent:
            self.copy.start()
            self.sent = True

    shape = property(lambda self: self.buffer.shape)
    dtype = property(lambda self: self.buffer.dtype)

    def __getitem__(self, at):
        return self.buffer[at]

    def __setitem__(self, at, value):
        self.buffer[at] = value


def call(body, scalars, args, outs, scratch, flops, by_parts=()):
    args = [a if isinstance(a, tuple) else (a, None) for a in args]
    views = [jax.eval_shape(lambda v, i=i: v if i is None else v[i], a) for a, i in args]
    n_scalars, n_in, n_out = len(scalars), len(args), len(outs)

    def kernel(*refs):
        head, refs = refs[:n_scalars], refs[n_scalars:]
        sources, refs = refs[:n_in], refs[n_in:]
        targets, refs = refs[:n_out], refs[n_out:]
        taken, refs = refs[:n_in], refs[n_in:]
        made, refs = refs[:n_out], refs[n_out:]
        sems, own = refs[-1], refs[:-1]
        ins, results = [], []
        for n, (source, (_, index)) in enumerate(zip(sources, args)):
            source = source if index is None else source.at[index]
            copy = pltpu.make_async_copy(source, taken[n], sems.at[n])
            copy.start()
            ins.append(Staged(taken[n], copy))
        for n, target in enumerate(targets):
            copy = pltpu.make_async_copy(made[n], target, sems.at[n_in + n])
            results.append(Staged(made[n], copy, target, n in by_parts))
        body(*head, *ins, *results, *own)
        for result in results:
            result.send()
        for result in results:
            if not result.by_parts:
                result.wait()

    smem, hbm = pl.BlockSpec(memory_space=pltpu.SMEM), pl.BlockSpec(memory_space=pltpu.HBM)
    buffers = [pltpu.VMEM(v.shape, v.dtype) for v in (*views, *outs)]
    moved = sum(v.size * v.dtype.itemsize for v in (*views, *outs))
    return pl.pallas_call(
        kernel,
        in_specs=[smem] * n_scalars + [hbm] * n_in,
        out_specs=[hbm] * n_out,
        out_shape=outs,
        scratch_shapes=buffers + scratch + [pltpu.SemaphoreType.DMA((n_in + n_out,))],
        compiler_params=pltpu.CompilerParams(vmem_limit_bytes=VMEM_LIMIT),
        cost_estimate=pl.CostEstimate(flops=flops, bytes_accessed=moved, transcendentals=0),
    )(*scalars, *[a for a, _ in args])


def on_device(
    dp_size,
    tokens,
    lengths,
    ln1_gain,
    ln1_bias,
    w_query,
    w_key,
    w_value,
    w_out,
    sort_first,
    sort_second,
    ln2_gain,
    ln2_bias,
    w_up,
    w_down,
    cotangent,
):
    rows_all, d = tokens.shape
    count = rows_all // LMAX
    ff = w_up.shape[1]
    core = side_of(1)
    ids = jnp.stack([core, side_of(2), side_of("head"), side_of(4), side_of(8)]).astype(jnp.int32)

    gain1, bias1, gain2, bias2 = (v.reshape(1, d) for v in (ln1_gain, ln1_bias, ln2_gain, ln2_bias))
    second_t = sort_second.T
    mine = call(
        slice_kernel, (ids,), (w_query, w_key, w_value, w_out), [shaped((4 * d, 2 * HD), LOW)], [],
        1 << 20,
    )[0]
    near_w = swap(mine, "head", dp_size)

    low_rows, wide_rows = shaped((rows_all, d), LOW), shaped((rows_all, d), F32)
    low_cols = shaped((d, rows_all), LOW)
    small_plan = shaped((count, NB, NB), F32)
    blocks = shaped((count * NB, d), F32)

    normed, normed_t, summary, pre, steps, plan, cot_t, grad_hidden = call(
        functools.partial(prepare_kernel, count), (lengths, ids),
        (tokens, gain1, bias1, sort_first, second_t, cotangent, w_down),
        [low_rows, low_cols, blocks, blocks, shaped((2 * ITERS, count, NB, NB), F32), small_plan]
        + [low_cols, shaped((rows_all, ff), LOW)],
        [], 2 * rows_all * d * ff,
    )
    near_w, normed = lax.optimization_barrier((near_w, normed))
    far_w = swap(near_w, 1, dp_size)

    (
        q, k, v, sk, sv, p, w_all, sent, kept, output, grad_middle, grad_att, vecs2
    ) = call(
        functools.partial(forward_kernel, count), (lengths, ids),
        (w_query, w_key, w_value, w_out, near_w, far_w, normed, plan, tokens, gain2, bias2)
        + (w_up, grad_hidden, cot_t, w_down, cotangent),
        [low_rows] * 5 + [shaped((count * 2 * LMAX, LMAX), LOW), shaped((4, d, d), LOW)]
        + [shaped((2, 4, 4, PART + 32, 128), LOW)] * 2 + [low_rows, wide_rows, low_rows, shaped((2, d), F32)],
        [pltpu.VMEM((LMAX, d), LOW)] * 2
        + [pltpu.VMEM((d, rows_all), LOW), pltpu.VMEM((rows_all, d), F32)]
        + [pltpu.VMEM((rows_all, d), LOW), pltpu.VMEM((d, rows_all), LOW)]
        + [pltpu.VMEM((rows_all, PART), F32)] * 2 + [pltpu.VMEM((rows_all, PART), LOW)] * 4
        + [pltpu.VMEM((rows_all, d), F32)] * 2 + [pltpu.VMEM((d, d), F32)]
        + [pltpu.SemaphoreType.DMA((ff // PART + 2,))],
        24 * rows_all * d * d, by_parts=(7, 8),
    )
    slots = Slots()
    slots.start("ffn", sum_chain(sent, kept, dp_size))
    work = [pltpu.VMEM((LMAX, d), LOW)] * 2 + [pltpu.VMEM((LMAX, d), F32)] * 4
    cuts = (0, 1, 3, count)

    def inputs_of(first, end, w):
        rows, probs = slice(first * LMAX, end * LMAX), slice(first * 2 * LMAX, end * 2 * LMAX)
        args = ((slots.before(grad_att), rows), w) + tuple((a, rows) for a in (q, k, v, sk, sv))
        return args + ((p, probs), plan)

    grads = []
    for first, end in zip(cuts[:-2], cuts[1:-1]):
        out = call(
            functools.partial(backward_kernel, first, count), (lengths, ids),
            inputs_of(first, end, (w_all, slice(3, 4))),
            [shaped(((end - first) * LMAX, d), LOW)] * 3 + [shaped((end - first, NB, NB), F32)],
            work, 4 << 30,
        )
        slots.after(out[-1])
        grads.append(out)
    first, late = cuts[-2], count - cuts[-2]
    sent, kept, input_grad = call(
        functools.partial(last_kernel, cuts, count), (lengths, ids),
        inputs_of(first, count, w_all)
        + (*(g for out in grads for g in out), normed_t, steps, pre, summary, sort_first, second_t)
        + (gain1, vecs2, tokens, grad_middle),
        [shaped((2, 4, 4, 136, 128), LOW)] * 2 + [low_rows],
        work + [pltpu.VMEM((late * LMAX, d), LOW)] * 3 + [pltpu.VMEM((late, NB, NB), F32)]
        + [pltpu.VMEM((count * NB, d), F32), pltpu.VMEM((16, d), F32), pltpu.VMEM((d, d), F32)],
        16 << 30,
    )
    slots.after(sent)
    slots.start("last", sum_chain(sent, kept, dp_size))
    last = [input_grad]
    for name in TURNS:
        last = slots.turn(name, last)
    while "ffn" in slots.running:
        last = slots.turn("ffn", last)
    up_sum, down_sum, o_sum = call(
        place_ffn_kernel, (ids,), slots.done["ffn"],
        [shaped(s, F32) for s in ((d, ff), (ff, d), w_out.shape)],
        [pltpu.VMEM((d, d), F32)], 1 << 28,
    )
    last = [o_sum]
    while "last" in slots.running:
        last = slots.turn("last", last)
    q_sum, k_sum, v_sum, first_sum, second_sum, *vec_sums = call(
        place_last_kernel, (ids,), slots.done["last"],
        [shaped(w_query.shape, F32)] * 3 + [shaped((d, d), F32), shaped((NB, d), F32)]
        + [shaped((1, d), F32)] * 4,
        [pltpu.VMEM((136, 128), F32), pltpu.VMEM((4, 16, d), F32)], 1 << 26,
    )
    vec_sums = [v.reshape(d) for v in vec_sums]
    return (
        output,
        input_grad,
        vec_sums[0],
        vec_sums[1],
        q_sum,
        k_sum,
        v_sum,
        o_sum,
        first_sum,
        second_sum.T,
        vec_sums[2],
        vec_sums[3],
        up_sum,
        down_sum,
    )


def solution(mesh):
    tokens, copied, columns = P(AXES, None), P(), P(None, "head")
    return jax.shard_map(
        functools.partial(on_device, mesh.shape["dp"]),
        mesh=mesh,
        in_specs=(tokens, P("dp"), copied, copied, columns, columns, columns, P("head", None))
        + (copied,) * 6
        + (tokens,),
        out_specs=(tokens, tokens, copied, copied, columns, columns, columns, P("head", None))
        + (copied,) * 6,
        check_vma=False,
    )
```

```python
import functools

import jax
import jax.numpy as jnp
from jax import lax
from jax.experimental import pallas as pl
from jax.experimental.pallas import tpu as pltpu
from jax.sharding import PartitionSpec as P

HD = 64
BL = 32
ITERS = 8
LMAX = 256
NB = LMAX // BL
SUMMARY_SCALE = BL**-0.5
F32 = jnp.float32
LOW = jnp.bfloat16
AXES = ("dp", "head")
VMEM_LIMIT = 56 * 1024 * 1024
TURNS = ["ffn", "last", "last", "ffn", "last", "ffn", "last", "last", "ffn", "last", "ffn", "last", "last", "ffn", "last", "ffn"]

ERF_P = 0.3875
ERF_C = (
    0.23607149955804155,
    0.07450957017858355,
    0.6926085194492264,
    -0.6975625302575207,
    0.9269567150083973,
    -0.23258376165572045,
)


def normal_parts(v):
    size = jnp.abs(v)
    bell = jnp.exp(v * v * -0.5)
    t = 1.0 / (1.0 + size * (ERF_P * 0.5**0.5))
    poly = ERF_C[5]
    for coef in ERF_C[4::-1]:
        poly = poly * t + coef
    tail = (0.5 * t) * poly * bell
    return jnp.where(v >= 0, 1.0 - tail, tail), bell * 0.3989422804014327


def dot_nn(a, b):
    return lax.dot_general(a, b, (((1,), (0,)), ((), ())), preferred_element_type=F32)


def dot_nt(a, b):
    return lax.dot_general(a, b, (((1,), (1,)), ((), ())), preferred_element_type=F32)


def dot_tn(a, b):
    return lax.dot_general(a, b, (((0,), (0,)), ((), ())), preferred_element_type=F32)


def split3(v):
    high = v.astype(LOW)
    left = v - high.astype(F32)
    mid = left.astype(LOW)
    return high, mid, (left - mid.astype(F32)).astype(LOW)


def split2(v):
    high = v.astype(LOW)
    return high, (v - high.astype(F32)).astype(LOW)


def exact_right(dot, v, w):
    a, b, c = split3(v)
    return dot(a, w) + dot(b, w) + dot(c, w)


def exact_both(dot, v, w):
    a, b, c = split3(v)
    d, e, f = split3(w)
    return dot(a, d) + (dot(a, e) + dot(b, d)) + (dot(b, e) + dot(a, f) + dot(c, d))


def row_norm(x):
    center = x - jnp.mean(x, axis=-1, keepdims=True)
    spread = jnp.mean(center * center, axis=-1, keepdims=True)
    scale = lax.rsqrt(spread + 1e-05)
    return center * scale, scale


def norm_pull(grad, unit, scale):
    return scale * (
        grad
        - jnp.mean(grad, axis=-1, keepdims=True)
        - unit * jnp.mean(grad * unit, axis=-1, keepdims=True)
    )


def iota(shape, axis):
    return lax.broadcasted_iota(jnp.int32, shape, axis)


def plan_allowed(count, spans):
    shape = (count, NB, NB)
    seq = iota(shape, 0)
    span = jnp.zeros(shape, jnp.int32)
    for s in range(count):
        span = jnp.where(seq == s, spans[s], span)
    row, col = iota(shape, 1), iota(shape, 2)
    row_ok, col_ok = row * BL < span, col * BL < span
    return (row_ok & col_ok) | ((row == col) & ~row_ok)


def head_mask(value):
    row, lane = iota((LMAX, 8 * HD), 0), iota((LMAX, 8 * HD), 1)
    return jnp.where(row // BL == lane // HD, value, 0.0).astype(LOW)


def spread_plan(plan, flip):
    pick = jnp.where(iota((LMAX, NB), 0) // BL == iota((LMAX, NB), 1), 1.0, 0.0).astype(LOW)
    same = (iota((LMAX, LMAX), 0) % BL) == (iota((LMAX, LMAX), 1) % BL)
    parts = []
    for part in split2(plan):
        tall = (dot_nt if flip else dot_nn)(pick, part).astype(LOW)
        parts.append(jnp.where(same, dot_nt(tall, pick), 0.0).astype(LOW))
    return parts


def pair_rows(left_t, right, m, lane_low):
    both = dot_nn(left_t[2 * BL * m : 2 * BL * (m + 1), :], right[:, 2 * HD * m : 2 * HD * (m + 1)])
    return jnp.where(lane_low, both[:BL], both[BL:])


PART = 256
PIECE = 64


def prepare_kernel(
    count, lens, ids, tokens, ln_gain, ln_bias, first, second, cotangent, down,
    normed, normed_t, summary, pre, steps, plan, cot_t, grad_hidden,
):
    spans = [lens[ids[2] * count + s] for s in range(count)]
    tokens.wait()
    ln_gain.wait()
    ln_bias.wait()
    gain, bias = ln_gain[...], ln_bias[...]
    token, block = iota((NB, LMAX), 1), iota((NB, LMAX), 0)

    def norm(s, carry):
        rows = pl.ds(pl.multiple_of(s * LMAX, LMAX), LMAX)
        unit, _ = row_norm(tokens[rows, :].astype(F32))
        low = (unit * gain + bias).astype(LOW)
        normed[rows, :] = low
        normed_t[:, rows] = low.T
        member = (token // BL == block) & (token < lens[ids[2] * count + s])
        picked = jnp.where(member, 1.0, 0.0).astype(LOW)
        blocks = pl.ds(pl.multiple_of(s * NB, NB), NB)
        summary[blocks, :] = dot_nn(picked, low) * SUMMARY_SCALE
        return carry

    lax.fori_loop(0, count, norm, 0)
    for out in (normed, normed_t, summary):
        out.send()
    for value in (first, second, cotangent, down):
        value.wait()
    before = exact_right(dot_nn, summary[...], first[...])
    pre[...] = before
    gate, _ = normal_parts(before)
    logits = exact_right(dot_nt, before * gate, second[...])
    logits = logits.reshape(count, NB, NB)
    x = jnp.where(plan_allowed(count, spans), logits, -1e30)
    for k in range(2 * ITERS):
        axis = 2 - k % 2
        top = jnp.max(x, axis=axis, keepdims=True)
        x = x - (top + jnp.log(jnp.sum(jnp.exp(x - top), axis=axis, keepdims=True)))
        steps[k] = x
    plan[...] = jnp.exp(x)
    for out in (pre, steps, plan):
        out.send()
    rows = cotangent[...]
    for s in range(count):
        seq = slice(s * LMAX, (s + 1) * LMAX)
        cot_t[:, seq] = cotangent[seq, :].T
    cot_t.send()

    def expand(c, carry):
        at = pl.ds(pl.multiple_of(c * PART, PART), PART)
        grad_hidden[:, at] = dot_nt(rows, down[at, :]).astype(LOW)
        return carry

    lax.fori_loop(0, down.shape[0] // PART, expand, 0)


def forward_kernel(
    count, lens, ids, w_q, w_k, w_v, w_o, near_w, far_w, normed, plan, tokens, ln_gain, ln_bias,
    up, grad_hidden, cot_t, down, cotangent,
    q_out, k_out, v_out, sk_out, sv_out, p_out, w_all, sent, kept, output, grad_middle, grad_att,
    grad_vecs,
    mask, mixed, mixed_t, middle, normed2, normed2_t, up0, up1, hid0, hid1, gup0, gup1, out_s, gn_s,
    grad_s, parts, part_sems,
):
    mask[...] = head_mask(HD**-0.5)
    for value in (w_q, w_k, w_v, w_o, near_w, far_w, normed, plan):
        value.wait()
    core, head = ids[0], ids[2]
    half, quarter = 4 * HD, 2 * HD
    own = pl.ds(pl.multiple_of(head * half, half), half)
    near = pl.ds(pl.multiple_of((1 - head) * half + core * quarter, quarter), quarter)
    far = pl.ds(pl.multiple_of((1 - head) * half + (1 - core) * quarter, quarter), quarter)
    for slot, w in enumerate((w_q, w_k, w_v)):
        w_all[slot, :, own] = w[...]
        w_all[slot, :, near] = near_w[512 * slot : 512 * (slot + 1), :]
        w_all[slot, :, far] = far_w[512 * slot : 512 * (slot + 1), :]
    w_all[3, own, :] = w_o[...]
    for m in range(4):
        lanes, rows = slice(128 * m, 128 * (m + 1)), slice(1536 + 128 * m, 1664 + 128 * m)
        w_all[3, near, lanes] = near_w[rows, :]
        w_all[3, far, lanes] = far_w[rows, :]
    w_all.send()
    keep_row = iota((LMAX, 8 * HD), 0)
    key_row = iota((2 * BL, 8 * BL), 0)
    query = iota((2 * BL, 8 * BL), 1) % BL
    lane_low = iota((BL, 2 * HD), 1) < HD

    def one(s, carry):
        span = lens[ids[2] * count + s]
        seq = pl.ds(pl.multiple_of(s * LMAX, LMAX), LMAX)
        n = normed[seq, :]
        keep = keep_row < span
        q_out[seq, :] = dot_nn(n, w_all[0]).astype(LOW)
        key = jnp.where(keep, dot_nn(n, w_all[1]), 0.0).astype(LOW)
        value = jnp.where(keep, dot_nn(n, w_all[2]), 0.0).astype(LOW)
        k_out[seq, :] = key
        v_out[seq, :] = value
        high, low = spread_plan(plan[s], False)
        sk_out[seq, :] = (dot_nn(high, key) + dot_nn(low, key)).astype(LOW)
        sv_out[seq, :] = (dot_nn(high, value) + dot_nn(low, value)).astype(LOW)
        rows = [pl.ds(pl.multiple_of(s * LMAX + i * BL, BL), BL) for i in range(NB)]
        scores = []
        for r in rows:
            keys = jnp.concatenate([k_out[r, :], sk_out[r, :]], 0)
            wide = jnp.concatenate([q_out[r, :]] * 8, 0) * mask[...]
            scores.append(dot_nt(keys, wide))
        weights = []
        for i, score in enumerate(scores):
            valid = jnp.where(key_row < BL, i * BL + key_row, i * BL) < span
            score = jnp.where(valid | (i * BL + query >= span), score, -1e30)
            grown = jnp.exp(score - jnp.max(score, axis=0, keepdims=True))
            weights.append(grown * (1.0 / jnp.sum(grown, axis=0, keepdims=True)))
        for i, weight in enumerate(weights):
            at = pl.multiple_of(s * 2 * LMAX + i * 2 * BL, 2 * BL)
            p_out[pl.ds(at, 2 * BL), :] = weight.astype(LOW)
        turned = [weight.T.astype(LOW) for weight in weights]
        for i, (r, weight_t) in enumerate(zip(rows, turned)):
            values = jnp.concatenate([v_out[r, :], sv_out[r, :]], 0)
            out = jnp.concatenate([pair_rows(weight_t, values, m, lane_low) for m in range(4)], 1)
            out = jnp.where(iota((BL, 8 * HD), 0) + i * BL < span, out, 0.0)
            mixed[i * BL : (i + 1) * BL, :] = out.astype(LOW)
        blended = mixed[...]
        mixed_t[:, seq] = blended.T

        @pl.when(s == 0)
        def _():
            tokens.wait()
            ln_gain.wait()
            ln_bias.wait()

        mid = tokens[seq, :].astype(F32) + dot_nn(blended, w_all[3])
        middle[seq, :] = mid
        unit, _ = row_norm(mid)
        low2 = (unit * ln_gain[...] + ln_bias[...]).astype(LOW)
        normed2[seq, :] = low2
        normed2_t[:, seq] = low2.T
        return carry

    lax.fori_loop(0, count, one, 0)
    for out in (q_out, k_out, v_out, sk_out, sv_out, p_out):
        out.send()
    for value in (up, grad_hidden, cot_t, down, cotangent):
        value.wait()
    units = up.shape[1] // PART // 2
    quarter = normed.shape[1] // 4
    ups, hids, gups = (up0, up1), (hid0, hid1), (gup0, gup1)

    def columns(c):
        unit = ((c // units) ^ (1 - core)) * units + c % units
        return pl.ds(pl.multiple_of(unit * PART, PART), PART)

    def expand(c, side):
        ups[side][...] = dot_nn(normed2[...], up[:, columns(c)])

    def gate_rows(c, side, rows):
        v = ups[side][rows, :]
        share, bell = normal_parts(v)
        hids[side][rows, :] = (v * share).astype(LOW)
        gh = grad_hidden[rows, columns(c)].astype(F32)
        gups[side][rows, :] = (gh * (share + v * bell)).astype(LOW)

    def gate(c, side):
        for r in range(up0.shape[0] // PIECE):
            gate_rows(c, side, slice(r * PIECE, (r + 1) * PIECE))

    def gate_alone(c, side):
        def piece(r, carry):
            gate_rows(c, side, pl.ds(pl.multiple_of(r * PIECE, PIECE), PIECE))
            return carry

        lax.fori_loop(0, up0.shape[0] // PIECE, piece, 0)

    def reduce(c, side):
        hidden, gup = hids[side][...], gups[side][...]
        for color, (left, right) in enumerate(((normed2_t, gup), (cot_t, hidden))):
            grad = dot_nn(left[...], right).astype(LOW)
            for j in range(PART // 128):
                for i in range(4):
                    tile = grad[quarter * i : quarter * (i + 1), 128 * j : 128 * (j + 1)]
                    at = slice(quarter * j, quarter * (j + 1))
                    parts[c // units, color, c % units, i, at, :] = tile
        out_s[...] += dot_nn(hidden, down[columns(c), :])
        gn_s[...] += dot_nt(gup, up[:, columns(c)])

    def part_copy(n, u):
        at = (slice(None), u, slice(None), slice(0, PART))
        return pltpu.make_async_copy(
            parts.at[n].at[at], (sent, kept)[n].at[at], part_sems.at[n * units + u]
        )

    out_s[...] = jnp.zeros_like(out_s)
    gn_s[...] = jnp.zeros_like(gn_s)
    last = 2 * units - 1
    expand(0, 0)
    expand(1, 1)
    gate_alone(0, 0)

    def steps(i, carry):
        for h in range(2):
            c = 2 * i + 1 + h
            expand(c + 1, h)
            gate(c, 1 - h)
            reduce(c - 1, h)
        return carry

    lax.fori_loop(0, units - 1, steps, 0)
    for u in range(units):
        part_copy(0, u).start()
    gate(last, 1)
    reduce(last - 1, 0)
    reduce(last, 1)

    def pull(s, carry):
        gain, bias = carry
        seq = pl.ds(pl.multiple_of(s * LMAX, LMAX), LMAX)
        gn, mid = gn_s[seq, :], middle[seq, :]
        unit, scale = row_norm(mid)
        gmid = cotangent[seq, :].astype(F32) + norm_pull(gn * ln_gain[...], unit, scale)
        grad_middle[seq, :] = gmid
        grad_att[seq, :] = gmid.astype(LOW)
        output[seq, :] = (mid + out_s[seq, :]).astype(LOW)
        gain = gain + jnp.sum(gn * unit, axis=0, keepdims=True)
        return gain, bias + jnp.sum(gn, axis=0, keepdims=True)

    zero = jnp.zeros((1, middle.shape[1]), F32)
    gain, bias = lax.fori_loop(0, count, pull, (zero, zero))
    for out in (grad_att, grad_middle, output):
        out.send()
    grad_vecs[0:1, :] = gain
    grad_vecs[1:2, :] = bias
    for u in range(units):
        part_copy(1, u).start()
    grad_s[...] = dot_nn(mixed_t[...], grad_att[...])
    tails = []
    for n, target in enumerate((sent, kept)):
        base = (core ^ (1 - n)) * units
        for j in range(units):
            for m in range(4):
                for h in range(2):
                    at = pl.multiple_of((base + j) * 64 + 32 * h, 32)
                    tile = grad_s[pl.ds(at, 32), 128 * m : 128 * (m + 1)].astype(LOW)
                    parts[n, m // 2, j, 2 * (m % 2) + h, PART : PART + 32, :] = tile
        at = (slice(None), slice(None), slice(None), slice(PART, PART + 32))
        tail = pltpu.make_async_copy(
            parts.at[n].at[at], target.at[at], part_sems.at[2 * units + n]
        )
        tail.start()
        tails.append(tail)
    for u in range(units):
        part_copy(0, u).wait()
        part_copy(1, u).wait()
    for tail in tails:
        tail.wait()


def scatter_tiles(core, sent, kept, wide, base):
    for n, target in enumerate((sent, kept)):

        def unit(k, carry, n=n, target=target):
            color, u = k // 4, k % 4
            at = (color * 8 + (core ^ (1 - n)) * 4 + u) * 32
            tile = wide[pl.ds(pl.multiple_of(at, 32), 32), :].astype(LOW)
            for p in range(4):
                for m in range(4):
                    part = tile[8 * p : 8 * (p + 1), 128 * m : 128 * (m + 1)]
                    target[color, u, p, base + 8 * m : base + 8 * (m + 1), :] = part
            return carry

        lax.fori_loop(0, 8, unit, 0)


def backward_one(
    local, plan_at, span, grad_att, w_o, q_in, k_in, v_in, sk_in, sv_in, p_in, plan,
    grad_q, grad_k, grad_v, grad_plan, mask, go_s, dks, dvs, dk_own, dv_own,
):
    base = local * LMAX
    seq = pl.ds(pl.multiple_of(base, LMAX), LMAX)
    gmixed = dot_nt(grad_att[seq, :], w_o[...]).astype(LOW)
    keep = iota((LMAX, 8 * HD), 0) < span
    go_s[...] = jnp.where(keep, gmixed, jnp.zeros_like(gmixed))
    lane_low = iota((BL, 2 * HD), 1) < HD
    rows = [pl.ds(pl.multiple_of(base + i * BL, BL), BL) for i in range(NB)]
    probs = [pl.ds(pl.multiple_of(2 * base + i * 2 * BL, 2 * BL), 2 * BL) for i in range(NB)]
    own_rows = [slice(i * BL, (i + 1) * BL) for i in range(NB)]
    grads, scores = [], []
    for r, at, mine in zip(rows, probs, own_rows):
        values = jnp.concatenate([v_in[r, :], sv_in[r, :]], 0)
        gwide = jnp.concatenate([go_s[mine, :]] * 8, 0) * mask[...]
        grads.append(dot_nt(values, gwide))
        dv = dot_nn(p_in[at, :], gwide)
        dv_own[mine, :] = dv[:BL]
        dvs[mine, :] = dv[BL:]
    for at, gweights in zip(probs, grads):
        wide = p_in[at, :].astype(F32)
        total = jnp.sum(wide * gweights, axis=0, keepdims=True)
        scores.append(wide * (gweights - total))
    turned = [gscores.T.astype(LOW) for gscores in scores]
    for r, mine, gscores in zip(rows, own_rows, scores):
        qwide = jnp.concatenate([q_in[r, :]] * 8, 0) * mask[...]
        dk = dot_nn(gscores.astype(LOW), qwide) * HD**-0.5
        dk_own[mine, :] = dk[:BL]
        dks[mine, :] = dk[BL:]
    for r, gscores_t in zip(rows, turned):
        keys = jnp.concatenate([k_in[r, :], sk_in[r, :]], 0)
        dq = jnp.concatenate([pair_rows(gscores_t, keys, m, lane_low) for m in range(4)], 1)
        grad_q[r, :] = (dq * HD**-0.5).astype(LOW)
    same = (iota((LMAX, LMAX), 0) % BL) == (iota((LMAX, LMAX), 1) % BL)
    high, low = spread_plan(plan[plan_at], True)
    cross = jnp.zeros((LMAX, LMAX), F32)
    for own, sorted_part, kept, target in (
        (dk_own, dks, k_in, grad_k),
        (dv_own, dvs, v_in, grad_v),
    ):
        g_high, g_low = split2(sorted_part[...])
        kept_rows = kept[seq, :]
        cross += dot_nt(g_high, kept_rows) + dot_nt(g_low, kept_rows)
        total = own[...] + (dot_nn(high, g_high) + (dot_nn(high, g_low) + dot_nn(low, g_high)))
        target[seq, :] = jnp.where(keep, total, 0.0).astype(LOW)
    cross = jnp.where(same, cross, 0.0)
    rows8 = jnp.sum(cross.reshape(NB, BL, LMAX), axis=1)
    pick = jnp.where(iota((LMAX, NB), 0) // BL == iota((LMAX, NB), 1), 1.0, 0.0).astype(LOW)
    grad_plan[local] = exact_right(dot_nn, rows8, pick)


def backward_kernel(
    first, count, lens, ids, grad_att, w_all, q_in, k_in, v_in, sk_in, sv_in, p_in, plan,
    grad_q, grad_k, grad_v, grad_plan, mask, *own,
):
    mask[...] = head_mask(1.0)
    ins = (grad_att, w_all, q_in, k_in, v_in, sk_in, sv_in, p_in, plan)
    for value in ins:
        value.wait()
    ins = (grad_att, w_all.buffer.at[0], *ins[2:])

    def one(n, carry):
        span = lens[ids[2] * count + first + n]
        backward_one(
            n, first + n, span, *ins, grad_q, grad_k, grad_v, grad_plan, mask, *own
        )
        return carry

    lax.fori_loop(0, grad_q.shape[0] // LMAX, one, 0)


def last_kernel(cuts, count, lens, ids, grad_att, w_all, q_in, k_in, v_in, sk_in, sv_in, p_in, plan, *refs):
    first, groups = cuts[-2], len(cuts) - 2
    early, refs = refs[: 4 * groups], refs[4 * groups :]
    normed_t, steps, pre, summary, sort_one, sort_two, ln_gain, vecs2, tokens, grad_middle = refs[:10]
    sent, kept, input_grad, mask, go_s, dks, dvs, dk_own, dv_own = refs[10:19]
    grad_q, grad_k, grad_v, grad_plan, gsum, small, grad_s = refs[19:]
    mask[...] = head_mask(1.0)
    ins = (grad_att, w_all, q_in, k_in, v_in, sk_in, sv_in, p_in, plan)
    for value in ins:
        value.wait()
    ins = (grad_att, w_all.buffer.at[3], *ins[2:])
    own = (mask, go_s, dks, dvs, dk_own, dv_own)

    def one(n, carry):
        span = lens[ids[2] * count + first + n]
        backward_one(n, first + n, span, *ins, grad_q, grad_k, grad_v, grad_plan, *own)
        return carry

    lax.fori_loop(0, count - first, one, 0)
    for value in (*early, normed_t, steps):
        value.wait()
    kinds = [list(early[n::4]) + [late] for n, late in enumerate((grad_q, grad_k, grad_v, grad_plan))]
    spans = [lens[ids[2] * count + c] for c in range(count)]
    g = jnp.concatenate([r[...] for r in kinds[3]], 0) * plan[...]
    for k in range(2 * ITERS - 1, -1, -1):
        axis = 2 - k % 2
        g = g - jnp.exp(steps[k]) * jnp.sum(g, axis=axis, keepdims=True)
    g = jnp.where(plan_allowed(count, spans), g, 0.0).reshape(count * NB, NB)
    d = normed_t.shape[0]
    for slot in range(3):
        grad = jnp.zeros((d, d), F32)
        for n, rows in enumerate(kinds[slot]):
            grad += dot_nn(normed_t[:, cuts[n] * LMAX : cuts[n + 1] * LMAX], rows[...])
        grad_s[...] = grad
        scatter_tiles(ids[0], sent, kept, grad_s, 32 * slot)
    for value in (pre, summary, sort_one, sort_two, ln_gain, vecs2, tokens, grad_middle):
        value.wait()
    before = pre[...]
    share, bell = normal_parts(before)
    small[...] = jnp.zeros_like(small)
    small[0:NB, :] = exact_both(dot_tn, g, before * share)
    small[10:12, :] = vecs2[...]
    gpre = exact_right(dot_nn, g, sort_two[...]) * (share + before * bell)
    grad_s[...] = exact_both(dot_tn, summary[...], gpre)
    scatter_tiles(ids[0], sent, kept, grad_s, 96)
    gsum[...] = exact_right(dot_nt, gpre, sort_one[...]) * SUMMARY_SCALE
    gain, bias = jnp.zeros((1, d), F32), jnp.zeros((1, d), F32)
    token, block = iota((LMAX, NB), 0), iota((LMAX, NB), 1)
    for s in range(count):
        seq = slice(s * LMAX, (s + 1) * LMAX)
        unit, scale = row_norm(tokens[seq, :].astype(F32))
        member = (token // BL == block) & (token < spans[s])
        picked = jnp.where(member, 1.0, 0.0).astype(LOW)
        high, mid, low = split3(gsum[s * NB : (s + 1) * NB, :])
        gn = dot_nn(picked, high) + dot_nn(picked, mid) + dot_nn(picked, low)
        for slot in range(3):
            group = max(n for n in range(groups + 1) if cuts[n] <= s)
            at = (s - cuts[group]) * LMAX
            gn += dot_nt(kinds[slot][group][at : at + LMAX, :], w_all[slot])
        gain += jnp.sum(gn * unit, axis=0, keepdims=True)
        bias += jnp.sum(gn, axis=0, keepdims=True)
        pulled = norm_pull(gn * ln_gain[...], unit, scale)
        input_grad[seq, :] = (grad_middle[seq, :] + pulled).astype(LOW)
    small[8:9, :] = gain
    small[9:10, :] = bias
    zeros = jnp.zeros((8, 128), LOW)
    for n, target in enumerate((sent, kept)):
        at = pl.ds(pl.multiple_of((ids[0] ^ (1 - n)) * 8, 8), 8)
        for u in range(4):
            tile = small[at, 128 * u : 128 * (u + 1)].astype(LOW)
            for color in range(2):
                for i in range(4):
                    target[color, u, i, 128:136, :] = tile if color == 0 and i == 0 else zeros


def each_piece(ids, near, far, place, looped):
    core, x, head = ids[0], ids[1], ids[2]
    for color in range(2):
        one, two = ((head, x), (x, head))[color]
        for n, source in enumerate((near, far)):

            def pieces(r, carry, color=color, one=one, two=two, n=n, source=source):
                unit = (core ^ n) * 4 + (one ^ (r // 2)) * 2 + (two ^ (r % 2))
                for i in range(4):
                    part = (ids[3] ^ (i // 2)) * 2 + (ids[4] ^ (i % 2))
                    place(color, unit, part, source.buffer.at[color, r, i // 2, i % 2])
                return carry

            if looped:
                lax.fori_loop(0, 4, pieces, 0)
            else:
                for r in range(4):
                    pieces(r, 0)


def place_ffn_kernel(ids, near, far, grad_up, grad_down, grad_o, o_s):
    near.wait()
    far.wait()

    def place(color, unit, part, source):
        quarter = pl.ds(pl.multiple_of(part * 128, 128), 128)
        for j in range(2):
            at = pl.ds(pl.multiple_of(unit * PART + 128 * j, 128), 128)
            block = source[128 * j : 128 * (j + 1), :].astype(F32)
            if color == 0:
                grad_up[quarter, at] = block
            else:
                grad_down[at, quarter] = block.T
        rows = pl.ds(pl.multiple_of(unit * 64 + (part % 2) * 32, 32), 32)
        lanes = pl.ds(pl.multiple_of(256 * color + (part // 2) * 128, 128), 128)
        o_s[rows, lanes] = source[PART : PART + 32, :].astype(F32)

    each_piece(ids, near, far, place, True)
    grad_o[...] = o_s[pl.ds(pl.multiple_of(ids[2] * 256, 256), 256), :]


def place_last_kernel(
    ids, near, far, grad_q, grad_k, grad_v, grad_first, second, gain1, bias1, gain2, bias2, wide, small
):
    near.wait()
    far.wait()
    head = ids[2]

    def place(color, unit, part, source):
        rows = pl.ds(pl.multiple_of(color * 256 + unit * 32 + part * 8, 8), 8)
        wide[...] = source[...].astype(F32)
        for slot, out in enumerate((grad_q, grad_k, grad_v)):
            for t in range(2):
                at = pl.ds(pl.multiple_of((4 * slot + 2 * head + t) * 8, 8), 8)
                out[rows, 128 * t : 128 * (t + 1)] = wide[at, :]
        for m in range(4):
            grad_first[rows, 128 * m : 128 * (m + 1)] = wide[96 + 8 * m : 104 + 8 * m, :]
        if color == 0:
            high = pl.ds(pl.multiple_of((unit // 4) * 8, 8), 8)
            lanes = pl.ds(pl.multiple_of((unit % 4) * 128, 128), 128)
            small[part, high, lanes] = wide[128:136, :]

    each_piece(ids, near, far, place, False)
    second[...] = small[0, 0:NB, :]
    for n, out in enumerate((gain1, bias1, gain2, bias2)):
        out[...] = small[0, 8 + n : 9 + n, :]


def slice_kernel(ids, w_q, w_k, w_v, w_o, mine):
    core = ids[0]
    lanes = pl.ds(pl.multiple_of(core * 2 * HD, 2 * HD), 2 * HD)
    for slot, w in enumerate((w_q, w_k, w_v)):
        w.wait()
        mine[512 * slot : 512 * (slot + 1), :] = w[:, lanes]
    w_o.wait()
    for m in range(4):
        mine[1536 + 128 * m : 1664 + 128 * m, :] = w_o[lanes, 128 * m : 128 * (m + 1)]


def swap(values, bit, dp_size):
    if bit == "head":
        pairs = [(d * 2 + h, d * 2 + (1 - h)) for d in range(dp_size) for h in range(2)]
    else:
        pairs = [(d * 2 + h, (d ^ bit) * 2 + h) for d in range(dp_size) for h in range(2)]
    return lax.ppermute(values, AXES, pairs)


def side_of(bit):
    if bit == "head":
        return lax.axis_index("head")
    return (lax.axis_index("dp") // bit) % 2


def pick(values, index, axis=0):
    return lax.dynamic_index_in_dim(values, index, axis, keepdims=False)


def pick_all(arrays, index):
    return [pick(a, index) for a in arrays]


def low_sum(arrays):
    total = arrays[0].astype(F32)
    for a in arrays[1:]:
        total = total + a.astype(F32)
    return total.astype(LOW)


def line_bits(dp_size):
    bits, bit = [], 4
    while bit < dp_size:
        bits.append(bit)
        bit *= 2
    return bits


def sum_chain(sent, kept, dp_size):
    order = (("head", 2), (2, "head"))
    line = line_bits(dp_size)
    got = swap(sent, 1, dp_size)
    got, = yield [sent], [got]
    shape = (2, 2, 2, 2) + kept.shape[3:]
    sums = [[kept[c].reshape(shape), got[c].reshape(shape)] for c in range(2)]
    for turn in range(2):
        sides = [side_of(order[c][turn]) for c in range(2)]
        sents = [low_sum(pick_all(sums[c], 1 - sides[c])) for c in range(2)]
        gots = [swap(sents[c], order[c][turn], dp_size) for c in range(2)]
        gots = yield sents, gots
        sums = [pick_all(sums[c], sides[c]) + [gots[c]] for c in range(2)]
    for bit in line[:2]:
        side = side_of(bit)
        sent = jnp.stack([low_sum(pick_all(sums[c], 1 - side)) for c in range(2)])
        got = swap(sent, bit, dp_size)
        got, = yield [sent], [got]
        sums = [pick_all(sums[c], side) + [got[c]] for c in range(2)]
    near = jnp.stack([low_sum(sums[c]) for c in range(2)])
    for bit in line[2:]:
        got = swap(near, bit, dp_size)
        got, = yield [near], [got]
        near = (near.astype(F32) + got.astype(F32)).astype(LOW)
    near = near[:, None]
    got = swap(near, line[1], dp_size)
    got, = yield [near], [got]
    near = jnp.concatenate([near, got], 1)[:, None]
    got = swap(near, line[0], dp_size)
    got, = yield [near], [got]
    near = jnp.concatenate([near, got], 1)
    near = [near[c][None] for c in range(2)]
    for turn in (1, 0):
        gots = [swap(near[c], order[c][turn], dp_size) for c in range(2)]
        gots = yield near, gots
        near = [jnp.concatenate([near[c], gots[c]], 0) for c in range(2)]
    near = jnp.stack(near)
    far = swap(near, 1, dp_size)
    far, = yield [near], [far]
    return near, far


class Slots:
    def __init__(self):
        self.running, self.done, self.got = {}, {}, {}

    def start(self, name, chain):
        self.running[name], self.got[name] = chain, None

    def step(self):
        sent = []
        for name, chain in list(self.running.items()):
            try:
                new, self.got[name] = chain.send(self.got[name])
                sent += new
            except StopIteration as end:
                self.done[name] = end.value
                del self.running[name], self.got[name]
        return sent

    def before(self, value):
        return lax.optimization_barrier((value, *self.step()))[0]

    def after(self, value):
        names = list(self.running)
        sizes = [len(self.got[n]) for n in names]
        flat = [g for n in names for g in self.got[n]]
        flat = lax.optimization_barrier((value, *flat))[1:]
        for name, size in zip(names, sizes):
            self.got[name], flat = list(flat[:size]), flat[size:]

    def turn(self, name, last):
        if name not in self.running:
            return last
        got = self.got[name]
        if got is not None:
            self.got[name] = list(lax.optimization_barrier((*got, *last))[: len(got)])
        try:
            sent, self.got[name] = self.running[name].send(self.got[name])
            return sent
        except StopIteration as end:
            self.done[name] = end.value
            del self.running[name]
            return last


def shaped(shape, kind):
    return jax.ShapeDtypeStruct(shape, kind)


class Staged:
    def __init__(self, buffer, copy):
        self.buffer, self.copy, self.sent = buffer, copy, False

    def wait(self):
        self.copy.wait()

    def send(self):
        if not self.sent:
            self.copy.start()
            self.sent = True

    shape = property(lambda self: self.buffer.shape)
    dtype = property(lambda self: self.buffer.dtype)

    def __getitem__(self, at):
        return self.buffer[at]

    def __setitem__(self, at, value):
        self.buffer[at] = value


def call(body, scalars, args, outs, scratch, flops, by_parts=(), limit=VMEM_LIMIT):
    args = [a if isinstance(a, tuple) else (a, None) for a in args]
    views = [jax.eval_shape(lambda v, i=i: v if i is None else v[i], a) for a, i in args]
    n_scalars, n_in, n_out = len(scalars), len(args), len(outs)

    def kernel(*refs):
        head, refs = refs[:n_scalars], refs[n_scalars:]
        sources, refs = refs[:n_in], refs[n_in:]
        targets, refs = refs[:n_out], refs[n_out:]
        taken, refs = refs[:n_in], refs[n_in:]
        made, refs = refs[: n_out - len(by_parts)], refs[n_out - len(by_parts) :]
        sems, own = refs[-1], refs[:-1]
        ins, results = [], []
        for n, (source, (_, index)) in enumerate(zip(sources, args)):
            source = source if index is None else source.at[index]
            copy = pltpu.make_async_copy(source, taken[n], sems.at[n])
            copy.start()
            ins.append(Staged(taken[n], copy))
        made = list(made)
        for n, target in enumerate(targets):
            if n in by_parts:
                results.append(target)
            else:
                buffer = made.pop(0)
                copy = pltpu.make_async_copy(buffer, target, sems.at[n_in + n])
                results.append(Staged(buffer, copy))
        body(*head, *ins, *results, *own)
        results = [r for n, r in enumerate(results) if n not in by_parts]
        for result in results:
            result.send()
        for result in results:
            result.wait()

    space = pltpu.HBM if limit == VMEM_LIMIT else pl.ANY
    smem, hbm = pl.BlockSpec(memory_space=pltpu.SMEM), pl.BlockSpec(memory_space=pltpu.HBM)
    whole = [v for n, v in enumerate(outs) if n not in by_parts]
    buffers = [pltpu.VMEM(v.shape, v.dtype) for v in (*views, *whole)]
    return pl.pallas_call(
        kernel,
        in_specs=[smem] * n_scalars + [pl.BlockSpec(memory_space=space)] * n_in,
        out_specs=[hbm] * n_out,
        out_shape=outs,
        scratch_shapes=buffers + scratch + [pltpu.SemaphoreType.DMA((n_in + n_out,))],
        compiler_params=pltpu.CompilerParams(vmem_limit_bytes=limit),
        cost_estimate=pl.CostEstimate(flops=1 << 34, bytes_accessed=1 << 24, transcendentals=0),
    )(*scalars, *[a for a, _ in args])


def on_device(
    dp_size,
    tokens,
    lengths,
    ln1_gain,
    ln1_bias,
    w_query,
    w_key,
    w_value,
    w_out,
    sort_first,
    sort_second,
    ln2_gain,
    ln2_bias,
    w_up,
    w_down,
    cotangent,
):
    rows_all, d = tokens.shape
    count = rows_all // LMAX
    ff = w_up.shape[1]
    core = side_of(1)
    ids = jnp.stack([core, side_of(2), side_of("head"), side_of(4), side_of(8)]).astype(jnp.int32)

    gain1, bias1, gain2, bias2 = (v.reshape(1, d) for v in (ln1_gain, ln1_bias, ln2_gain, ln2_bias))
    second_t = sort_second.T
    mine = call(
        slice_kernel, (ids,), (w_query, w_key, w_value, w_out), [shaped((4 * d, 2 * HD), LOW)], [],
        1 << 20,
    )[0]
    near_w = swap(mine, "head", dp_size)

    low_rows, wide_rows = shaped((rows_all, d), LOW), shaped((rows_all, d), F32)
    low_cols = shaped((d, rows_all), LOW)
    small_plan = shaped((count, NB, NB), F32)
    blocks = shaped((count * NB, d), F32)

    normed, normed_t, summary, pre, steps, plan, cot_t, grad_hidden = call(
        functools.partial(prepare_kernel, count), (lengths, ids),
        (tokens, gain1, bias1, sort_first, second_t, cotangent, w_down),
        [low_rows, low_cols, blocks, blocks, shaped((2 * ITERS, count, NB, NB), F32), small_plan]
        + [low_cols, shaped((rows_all, ff), LOW)],
        [], 2 * rows_all * d * ff,
    )
    near_w, normed = lax.optimization_barrier((near_w, normed))
    far_w = swap(near_w, 1, dp_size)

    (
        q, k, v, sk, sv, p, w_all, sent, kept, output, grad_middle, grad_att, vecs2
    ) = call(
        functools.partial(forward_kernel, count), (lengths, ids),
        (w_query, w_key, w_value, w_out, near_w, far_w, normed, plan, tokens, gain2, bias2)
        + (w_up, grad_hidden, cot_t, w_down, cotangent),
        [low_rows] * 5 + [shaped((count * 2 * LMAX, LMAX), LOW), shaped((4, d, d), LOW)]
        + [shaped((2, 4, 4, PART + 32, 128), LOW)] * 2 + [low_rows, wide_rows, low_rows, shaped((2, d), F32)],
        [pltpu.VMEM((LMAX, d), LOW)] * 2
        + [pltpu.VMEM((d, rows_all), LOW), pltpu.VMEM((rows_all, d), F32)]
        + [pltpu.VMEM((rows_all, d), LOW), pltpu.VMEM((d, rows_all), LOW)]
        + [pltpu.VMEM((rows_all, PART), F32)] * 2 + [pltpu.VMEM((rows_all, PART), LOW)] * 4
        + [pltpu.VMEM((rows_all, d), F32)] * 2 + [pltpu.VMEM((d, d), F32)]
        + [pltpu.VMEM((2, 2, 4, 4, PART + 32, 128), LOW)]
        + [pltpu.SemaphoreType.DMA((ff // PART + 2,))],
        24 * rows_all * d * d, by_parts=(7, 8),
    )
    slots = Slots()
    slots.start("ffn", sum_chain(sent, kept, dp_size))
    work = [pltpu.VMEM((LMAX, d), LOW)] * 2 + [pltpu.VMEM((LMAX, d), F32)] * 4
    cuts = (0, 1, 3, count)

    def inputs_of(first, end, w):
        rows, probs = slice(first * LMAX, end * LMAX), slice(first * 2 * LMAX, end * 2 * LMAX)
        args = ((slots.before(grad_att), rows), w) + tuple((a, rows) for a in (q, k, v, sk, sv))
        return args + ((p, probs), plan)

    grads = []
    for first, end in zip(cuts[:-2], cuts[1:-1]):
        out = call(
            functools.partial(backward_kernel, first, count), (lengths, ids),
            inputs_of(first, end, (w_all, slice(3, 4))),
            [shaped(((end - first) * LMAX, d), LOW)] * 3 + [shaped((end - first, NB, NB), F32)],
            work, 4 << 30,
        )
        slots.after(out[-1])
        grads.append(out)
    first, late = cuts[-2], count - cuts[-2]
    sent, kept, input_grad = call(
        functools.partial(last_kernel, cuts, count), (lengths, ids),
        inputs_of(first, count, w_all)
        + (*(g for out in grads for g in out), normed_t, steps, pre, summary, sort_first, second_t)
        + (gain1, vecs2, tokens, grad_middle),
        [shaped((2, 4, 4, 136, 128), LOW)] * 2 + [low_rows],
        work + [pltpu.VMEM((late * LMAX, d), LOW)] * 3 + [pltpu.VMEM((late, NB, NB), F32)]
        + [pltpu.VMEM((count * NB, d), F32), pltpu.VMEM((16, d), F32), pltpu.VMEM((d, d), F32)],
        16 << 30,
    )
    slots.after(sent)
    slots.start("last", sum_chain(sent, kept, dp_size))
    last = [input_grad]
    for name in TURNS:
        last = slots.turn(name, last)
    while "ffn" in slots.running:
        last = slots.turn("ffn", last)
    up_sum, down_sum, o_sum = call(
        place_ffn_kernel, (ids,), slots.done["ffn"],
        [shaped(s, F32) for s in ((d, ff), (ff, d), w_out.shape)],
        [pltpu.VMEM((d, d), F32)], 1 << 28, limit=20 << 20,
    )
    last = [o_sum]
    while "last" in slots.running:
        last = slots.turn("last", last)
    q_sum, k_sum, v_sum, first_sum, second_sum, *vec_sums = call(
        place_last_kernel, (ids,), slots.done["last"],
        [shaped(w_query.shape, F32)] * 3 + [shaped((d, d), F32), shaped((NB, d), F32)]
        + [shaped((1, d), F32)] * 4,
        [pltpu.VMEM((136, 128), F32), pltpu.VMEM((4, 16, d), F32)], 1 << 26, limit=8 << 20,
    )
    vec_sums = [v.reshape(d) for v in vec_sums]
    return (
        output,
        input_grad,
        vec_sums[0],
        vec_sums[1],
        q_sum,
        k_sum,
        v_sum,
        o_sum,
        first_sum,
        second_sum.T,
        vec_sums[2],
        vec_sums[3],
        up_sum,
        down_sum,
    )


def solution(mesh):
    tokens, copied, columns = P(AXES, None), P(), P(None, "head")
    return jax.shard_map(
        functools.partial(on_device, mesh.shape["dp"]),
        mesh=mesh,
        in_specs=(tokens, P("dp"), copied, copied, columns, columns, columns, P("head", None))
        + (copied,) * 6
        + (tokens,),
        out_specs=(tokens, tokens, copied, copied, columns, columns, columns, P("head", None))
        + (copied,) * 6,
        check_vma=False,
    )
```

```python
import functools

import jax
import jax.numpy as jnp
from jax import lax
from jax.experimental import pallas as pl
from jax.experimental.pallas import tpu as pltpu
from jax.sharding import PartitionSpec as P

HD = 64
BL = 32
ITERS = 8
LMAX = 256
NB = LMAX // BL
SUMMARY_SCALE = BL**-0.5
F32 = jnp.float32
LOW = jnp.bfloat16
AXES = ("dp", "head")
VMEM_LIMIT = 56 * 1024 * 1024
TURNS = ["last", "last", "ffn", "output", "last", "ffn", "input", "last", "ffn", "ffn", "last"]
LAST_HALVED = False

ERF_P = 0.3875
ERF_C = (
    0.23607149955804155,
    0.07450957017858355,
    0.6926085194492264,
    -0.6975625302575207,
    0.9269567150083973,
    -0.23258376165572045,
)


def normal_parts(v):
    size = jnp.abs(v)
    bell = jnp.exp(v * v * -0.5)
    t = 1.0 / (1.0 + size * (ERF_P * 0.5**0.5))
    poly = ERF_C[5]
    for coef in ERF_C[4::-1]:
        poly = poly * t + coef
    tail = (0.5 * t) * poly * bell
    return jnp.where(v >= 0, 1.0 - tail, tail), bell * 0.3989422804014327


def dot_nn(a, b):
    return lax.dot_general(a, b, (((1,), (0,)), ((), ())), preferred_element_type=F32)


def dot_nt(a, b):
    return lax.dot_general(a, b, (((1,), (1,)), ((), ())), preferred_element_type=F32)


def dot_tn(a, b):
    return lax.dot_general(a, b, (((0,), (0,)), ((), ())), preferred_element_type=F32)


def split3(v):
    high = v.astype(LOW)
    left = v - high.astype(F32)
    mid = left.astype(LOW)
    return high, mid, (left - mid.astype(F32)).astype(LOW)


def split2(v):
    high = v.astype(LOW)
    return high, (v - high.astype(F32)).astype(LOW)


def exact_right(dot, v, w):
    a, b, c = split3(v)
    return dot(a, w) + dot(b, w) + dot(c, w)


def exact_both(dot, v, w):
    a, b, c = split3(v)
    d, e, f = split3(w)
    return dot(a, d) + (dot(a, e) + dot(b, d)) + (dot(b, e) + dot(a, f) + dot(c, d))


def row_norm(x):
    center = x - jnp.mean(x, axis=-1, keepdims=True)
    spread = jnp.mean(center * center, axis=-1, keepdims=True)
    scale = lax.rsqrt(spread + 1e-05)
    return center * scale, scale


def norm_pull(grad, unit, scale):
    return scale * (
        grad
        - jnp.mean(grad, axis=-1, keepdims=True)
        - unit * jnp.mean(grad * unit, axis=-1, keepdims=True)
    )


def iota(shape, axis):
    return lax.broadcasted_iota(jnp.int32, shape, axis)


def plan_allowed(count, spans):
    shape = (count, NB, NB)
    seq = iota(shape, 0)
    span = jnp.zeros(shape, jnp.int32)
    for s in range(count):
        span = jnp.where(seq == s, spans[s], span)
    row, col = iota(shape, 1), iota(shape, 2)
    row_ok, col_ok = row * BL < span, col * BL < span
    return (row_ok & col_ok) | ((row == col) & ~row_ok)


def head_mask(value):
    row, lane = iota((LMAX, 8 * HD), 0), iota((LMAX, 8 * HD), 1)
    return jnp.where(row // BL == lane // HD, value, 0.0).astype(LOW)


def spread_plan(plan, flip):
    pick = jnp.where(iota((LMAX, NB), 0) // BL == iota((LMAX, NB), 1), 1.0, 0.0).astype(LOW)
    same = (iota((LMAX, LMAX), 0) % BL) == (iota((LMAX, LMAX), 1) % BL)
    parts = []
    for part in split2(plan):
        tall = (dot_nt if flip else dot_nn)(pick, part).astype(LOW)
        parts.append(jnp.where(same, dot_nt(tall, pick), 0.0).astype(LOW))
    return parts


def pair_rows(left_t, right, m, lane_low):
    both = dot_nn(left_t[2 * BL * m : 2 * BL * (m + 1), :], right[:, 2 * HD * m : 2 * HD * (m + 1)])
    return jnp.where(lane_low, both[:BL], both[BL:])


PART = 256
PIECE = 64


def prepare_kernel(
    count, lens, ids, tokens, ln_gain, ln_bias, first, second, cotangent, down,
    normed, normed_t, summary, pre, steps, plan, cot_t, grad_hidden,
):
    spans = [lens[ids[2] * count + s] for s in range(count)]
    tokens.wait()
    ln_gain.wait()
    ln_bias.wait()
    gain, bias = ln_gain[...], ln_bias[...]
    token, block = iota((NB, LMAX), 1), iota((NB, LMAX), 0)

    def norm(s, carry):
        rows = pl.ds(pl.multiple_of(s * LMAX, LMAX), LMAX)
        unit, _ = row_norm(tokens[rows, :].astype(F32))
        low = (unit * gain + bias).astype(LOW)
        normed[rows, :] = low
        normed_t[:, rows] = low.T
        member = (token // BL == block) & (token < lens[ids[2] * count + s])
        picked = jnp.where(member, 1.0, 0.0).astype(LOW)
        blocks = pl.ds(pl.multiple_of(s * NB, NB), NB)
        summary[blocks, :] = dot_nn(picked, low) * SUMMARY_SCALE
        return carry

    lax.fori_loop(0, count, norm, 0)
    for out in (normed, normed_t, summary):
        out.send()
    for value in (first, second, cotangent, down):
        value.wait()
    before = exact_right(dot_nn, summary[...], first[...])
    pre[...] = before
    gate, _ = normal_parts(before)
    logits = exact_right(dot_nt, before * gate, second[...])
    logits = logits.reshape(count, NB, NB)
    x = jnp.where(plan_allowed(count, spans), logits, -1e30)
    for k in range(2 * ITERS):
        axis = 2 - k % 2
        top = jnp.max(x, axis=axis, keepdims=True)
        x = x - (top + jnp.log(jnp.sum(jnp.exp(x - top), axis=axis, keepdims=True)))
        steps[k] = x
    plan[...] = jnp.exp(x)
    for out in (pre, steps, plan):
        out.send()
    rows = cotangent[...]
    for s in range(count):
        seq = slice(s * LMAX, (s + 1) * LMAX)
        cot_t[:, seq] = cotangent[seq, :].T
    cot_t.send()

    def expand(c, carry):
        at = pl.ds(pl.multiple_of(c * PART, PART), PART)
        grad_hidden[:, at] = dot_nt(rows, down[at, :]).astype(LOW)
        return carry

    lax.fori_loop(0, down.shape[0] // PART, expand, 0)


def forward_kernel(
    count, lens, ids, w_q, w_k, w_v, w_o, near_w, far_w, normed, plan, tokens, ln_gain, ln_bias,
    up, grad_hidden, cot_t, cotangent,
    q_out, k_out, v_out, sk_out, sv_out, p_out, w_all, sent, kept, hidden_out, middle, grad_middle,
    grad_att, grad_vecs,
    mask, mixed, mixed_t, normed2, normed2_t, up0, up1, hid0, hid1, gup0, gup1, gn_s,
    grad_s, parts, part_sems,
):
    mask[...] = head_mask(HD**-0.5)
    for value in (w_q, w_k, w_v, w_o, near_w, far_w, normed, plan):
        value.wait()
    core, head = ids[0], ids[2]
    half, quarter = 4 * HD, 2 * HD
    own = pl.ds(pl.multiple_of(head * half, half), half)
    near = pl.ds(pl.multiple_of((1 - head) * half + core * quarter, quarter), quarter)
    far = pl.ds(pl.multiple_of((1 - head) * half + (1 - core) * quarter, quarter), quarter)
    for slot, w in enumerate((w_q, w_k, w_v)):
        w_all[slot, :, own] = w[...]
        w_all[slot, :, near] = near_w[512 * slot : 512 * (slot + 1), :]
        w_all[slot, :, far] = far_w[512 * slot : 512 * (slot + 1), :]
    w_all[3, own, :] = w_o[...]
    for m in range(4):
        lanes, rows = slice(128 * m, 128 * (m + 1)), slice(1536 + 128 * m, 1664 + 128 * m)
        w_all[3, near, lanes] = near_w[rows, :]
        w_all[3, far, lanes] = far_w[rows, :]
    w_all.send()
    keep_row = iota((LMAX, 8 * HD), 0)
    key_row = iota((2 * BL, 8 * BL), 0)
    query = iota((2 * BL, 8 * BL), 1) % BL
    lane_low = iota((BL, 2 * HD), 1) < HD

    def one(s, carry):
        span = lens[ids[2] * count + s]
        seq = pl.ds(pl.multiple_of(s * LMAX, LMAX), LMAX)
        n = normed[seq, :]
        keep = keep_row < span
        q_out[seq, :] = dot_nn(n, w_all[0]).astype(LOW)
        key = jnp.where(keep, dot_nn(n, w_all[1]), 0.0).astype(LOW)
        value = jnp.where(keep, dot_nn(n, w_all[2]), 0.0).astype(LOW)
        k_out[seq, :] = key
        v_out[seq, :] = value
        high, low = spread_plan(plan[s], False)
        sk_out[seq, :] = (dot_nn(high, key) + dot_nn(low, key)).astype(LOW)
        sv_out[seq, :] = (dot_nn(high, value) + dot_nn(low, value)).astype(LOW)
        rows = [pl.ds(pl.multiple_of(s * LMAX + i * BL, BL), BL) for i in range(NB)]
        scores = []
        for r in rows:
            keys = jnp.concatenate([k_out[r, :], sk_out[r, :]], 0)
            wide = jnp.concatenate([q_out[r, :]] * 8, 0) * mask[...]
            scores.append(dot_nt(keys, wide))
        weights = []
        for i, score in enumerate(scores):
            valid = jnp.where(key_row < BL, i * BL + key_row, i * BL) < span
            score = jnp.where(valid | (i * BL + query >= span), score, -1e30)
            grown = jnp.exp(score - jnp.max(score, axis=0, keepdims=True))
            weights.append(grown * (1.0 / jnp.sum(grown, axis=0, keepdims=True)))
        for i, weight in enumerate(weights):
            at = pl.multiple_of(s * 2 * LMAX + i * 2 * BL, 2 * BL)
            p_out[pl.ds(at, 2 * BL), :] = weight.astype(LOW)
        turned = [weight.T.astype(LOW) for weight in weights]
        for i, (r, weight_t) in enumerate(zip(rows, turned)):
            values = jnp.concatenate([v_out[r, :], sv_out[r, :]], 0)
            out = jnp.concatenate([pair_rows(weight_t, values, m, lane_low) for m in range(4)], 1)
            out = jnp.where(iota((BL, 8 * HD), 0) + i * BL < span, out, 0.0)
            mixed[i * BL : (i + 1) * BL, :] = out.astype(LOW)
        blended = mixed[...]
        mixed_t[:, seq] = blended.T

        @pl.when(s == 0)
        def _():
            tokens.wait()
            ln_gain.wait()
            ln_bias.wait()

        mid = tokens[seq, :].astype(F32) + dot_nn(blended, w_all[3])
        middle[seq, :] = mid
        unit, _ = row_norm(mid)
        low2 = (unit * ln_gain[...] + ln_bias[...]).astype(LOW)
        normed2[seq, :] = low2
        normed2_t[:, seq] = low2.T
        return carry

    lax.fori_loop(0, count, one, 0)
    for out in (q_out, k_out, v_out, sk_out, sv_out, p_out, middle):
        out.send()
    for value in (up, grad_hidden, cot_t, cotangent):
        value.wait()
    units = up.shape[1] // PART // 2
    quarter = normed.shape[1] // 4
    ups, hids, gups = (up0, up1), (hid0, hid1), (gup0, gup1)

    def columns(c):
        unit = ((c // units) ^ (1 - core)) * units + c % units
        return pl.ds(pl.multiple_of(unit * PART, PART), PART)

    def expand(c, side):
        ups[side][...] = dot_nn(normed2[...], up[:, columns(c)])

    def gate_rows(c, side, rows):
        v = ups[side][rows, :]
        share, bell = normal_parts(v)
        hidden = (v * share).astype(LOW)
        hids[side][rows, :] = hidden
        hidden_out[rows, columns(c)] = hidden
        gh = grad_hidden[rows, columns(c)].astype(F32)
        gups[side][rows, :] = (gh * (share + v * bell)).astype(LOW)

    def gate(c, side):
        for r in range(up0.shape[0] // PIECE):
            gate_rows(c, side, slice(r * PIECE, (r + 1) * PIECE))

    def gate_alone(c, side):
        def piece(r, carry):
            gate_rows(c, side, pl.ds(pl.multiple_of(r * PIECE, PIECE), PIECE))
            return carry

        lax.fori_loop(0, up0.shape[0] // PIECE, piece, 0)

    def reduce(c, side):
        hidden, gup = hids[side][...], gups[side][...]
        for color, (left, right) in enumerate(((normed2_t, gup), (cot_t, hidden))):
            grad = dot_nn(left[...], right).astype(LOW)
            for j in range(PART // 128):
                for i in range(4):
                    tile = grad[quarter * i : quarter * (i + 1), 128 * j : 128 * (j + 1)]
                    at = slice(quarter * j, quarter * (j + 1))
                    parts[c // units, c % units, i, color, at, :] = tile
        gn_s[...] += dot_nt(gup, up[:, columns(c)])

    def part_copy(n, u):
        at = (u, slice(None), slice(None), slice(0, PART))
        return pltpu.make_async_copy(
            parts.at[n].at[at], (sent, kept)[n].at[at], part_sems.at[n * units + u]
        )

    gn_s[...] = jnp.zeros_like(gn_s)
    last = 2 * units - 1
    expand(0, 0)
    expand(1, 1)
    gate_alone(0, 0)

    def steps(i, carry):
        for h in range(2):
            c = 2 * i + 1 + h
            expand(c + 1, h)
            gate(c, 1 - h)
            reduce(c - 1, h)
        return carry

    lax.fori_loop(0, units - 1, steps, 0)
    for u in range(units):
        part_copy(0, u).start()
    gate(last, 1)
    hidden_out.send()
    reduce(last - 1, 0)
    reduce(last, 1)

    def pull(s, carry):
        gain, bias = carry
        seq = pl.ds(pl.multiple_of(s * LMAX, LMAX), LMAX)
        gn, mid = gn_s[seq, :], middle[seq, :]
        unit, scale = row_norm(mid)
        gmid = cotangent[seq, :].astype(F32) + norm_pull(gn * ln_gain[...], unit, scale)
        grad_middle[seq, :] = gmid
        grad_att[seq, :] = gmid.astype(LOW)
        gain = gain + jnp.sum(gn * unit, axis=0, keepdims=True)
        return gain, bias + jnp.sum(gn, axis=0, keepdims=True)

    zero = jnp.zeros((1, middle.shape[1]), F32)
    gain, bias = lax.fori_loop(0, count, pull, (zero, zero))
    for out in (grad_att, grad_middle):
        out.send()
    grad_vecs[0:1, :] = gain
    grad_vecs[1:2, :] = bias
    for u in range(units):
        part_copy(1, u).start()
    grad_s[...] = dot_nn(mixed_t[...], grad_att[...])
    tails = []
    for n, target in enumerate((sent, kept)):
        base = (core ^ (1 - n)) * units
        for j in range(units):
            for m in range(4):
                for h in range(2):
                    at = pl.multiple_of((base + j) * 64 + 32 * h, 32)
                    tile = grad_s[pl.ds(at, 32), 128 * m : 128 * (m + 1)].astype(LOW)
                    parts[n, j, 2 * (m % 2) + h, m // 2, PART : PART + 32, :] = tile
        at = (slice(None), slice(None), slice(None), slice(PART, PART + 32))
        tail = pltpu.make_async_copy(
            parts.at[n].at[at], target.at[at], part_sems.at[2 * units + n]
        )
        tail.start()
        tails.append(tail)
    for u in range(units):
        part_copy(0, u).wait()
        part_copy(1, u).wait()
    for tail in tails:
        tail.wait()


def scatter_tiles(core, sent, kept, wide, base):
    for n, target in enumerate((sent, kept)):

        def unit(k, carry, n=n, target=target):
            color, u = k // 4, k % 4
            at = (color * 8 + (core ^ (1 - n)) * 4 + u) * 32
            tile = wide[pl.ds(pl.multiple_of(at, 32), 32), :].astype(LOW)
            for p in range(4):
                for m in range(4):
                    part = tile[8 * p : 8 * (p + 1), 128 * m : 128 * (m + 1)]
                    target[u, p, color, base + 8 * m : base + 8 * (m + 1), :] = part
            return carry

        lax.fori_loop(0, 8, unit, 0)


def backward_one(
    local, plan_at, span, grad_att, w_o, q_in, k_in, v_in, sk_in, sv_in, p_in, plan,
    grad_q, grad_k, grad_v, grad_plan, mask, go_s, dks, dvs, dk_own, dv_own,
):
    base = local * LMAX
    seq = pl.ds(pl.multiple_of(base, LMAX), LMAX)
    gmixed = dot_nt(grad_att[seq, :], w_o[...]).astype(LOW)
    keep = iota((LMAX, 8 * HD), 0) < span
    go_s[...] = jnp.where(keep, gmixed, jnp.zeros_like(gmixed))
    lane_low = iota((BL, 2 * HD), 1) < HD
    rows = [pl.ds(pl.multiple_of(base + i * BL, BL), BL) for i in range(NB)]
    probs = [pl.ds(pl.multiple_of(2 * base + i * 2 * BL, 2 * BL), 2 * BL) for i in range(NB)]
    own_rows = [slice(i * BL, (i + 1) * BL) for i in range(NB)]
    grads, scores = [], []
    for r, at, mine in zip(rows, probs, own_rows):
        values = jnp.concatenate([v_in[r, :], sv_in[r, :]], 0)
        gwide = jnp.concatenate([go_s[mine, :]] * 8, 0) * mask[...]
        grads.append(dot_nt(values, gwide))
        dv = dot_nn(p_in[at, :], gwide)
        dv_own[mine, :] = dv[:BL]
        dvs[mine, :] = dv[BL:]
    for at, gweights in zip(probs, grads):
        wide = p_in[at, :].astype(F32)
        total = jnp.sum(wide * gweights, axis=0, keepdims=True)
        scores.append(wide * (gweights - total))
    turned = [gscores.T.astype(LOW) for gscores in scores]
    for r, mine, gscores in zip(rows, own_rows, scores):
        qwide = jnp.concatenate([q_in[r, :]] * 8, 0) * mask[...]
        dk = dot_nn(gscores.astype(LOW), qwide) * HD**-0.5
        dk_own[mine, :] = dk[:BL]
        dks[mine, :] = dk[BL:]
    for r, gscores_t in zip(rows, turned):
        keys = jnp.concatenate([k_in[r, :], sk_in[r, :]], 0)
        dq = jnp.concatenate([pair_rows(gscores_t, keys, m, lane_low) for m in range(4)], 1)
        grad_q[r, :] = (dq * HD**-0.5).astype(LOW)
    same = (iota((LMAX, LMAX), 0) % BL) == (iota((LMAX, LMAX), 1) % BL)
    high, low = spread_plan(plan[plan_at], True)
    cross = jnp.zeros((LMAX, LMAX), F32)
    for own, sorted_part, kept, target in (
        (dk_own, dks, k_in, grad_k),
        (dv_own, dvs, v_in, grad_v),
    ):
        g_high, g_low = split2(sorted_part[...])
        kept_rows = kept[seq, :]
        cross += dot_nt(g_high, kept_rows) + dot_nt(g_low, kept_rows)
        total = own[...] + (dot_nn(high, g_high) + (dot_nn(high, g_low) + dot_nn(low, g_high)))
        target[seq, :] = jnp.where(keep, total, 0.0).astype(LOW)
    cross = jnp.where(same, cross, 0.0)
    rows8 = jnp.sum(cross.reshape(NB, BL, LMAX), axis=1)
    pick = jnp.where(iota((LMAX, NB), 0) // BL == iota((LMAX, NB), 1), 1.0, 0.0).astype(LOW)
    grad_plan[local] = exact_right(dot_nn, rows8, pick)


def backward_kernel(
    first, count, lens, ids, grad_att, w_all, q_in, k_in, v_in, sk_in, sv_in, p_in, plan,
    grad_q, grad_k, grad_v, grad_plan, mask, *own,
):
    mask[...] = head_mask(1.0)
    ins = (grad_att, w_all, q_in, k_in, v_in, sk_in, sv_in, p_in, plan)
    for value in ins:
        value.wait()
    ins = (grad_att, w_all.buffer.at[0], *ins[2:])

    def one(n, carry):
        span = lens[ids[2] * count + first + n]
        backward_one(
            n, first + n, span, *ins, grad_q, grad_k, grad_v, grad_plan, mask, *own
        )
        return carry

    lax.fori_loop(0, grad_q.shape[0] // LMAX, one, 0)


def last_kernel(cuts, count, lens, ids, grad_att, w_all, q_in, k_in, v_in, sk_in, sv_in, p_in, plan, *refs):
    first, groups = cuts[-2], len(cuts) - 2
    early, refs = refs[: 4 * groups], refs[4 * groups :]
    normed_t, steps, pre, summary, sort_one, sort_two, ln_gain, ln_bias, vecs2 = refs[:9]
    sent, kept, grad_q, grad_k, grad_v, gsum = refs[9:15]
    mask, go_s, dks, dvs, dk_own, dv_own, grad_plan, small, grad_s, prod_s = refs[15:]
    mask[...] = head_mask(1.0)
    ins = (grad_att, w_all, q_in, k_in, v_in, sk_in, sv_in, p_in, plan)
    for value in ins:
        value.wait()
    ins = (grad_att, w_all.buffer.at[3], *ins[2:])
    own = (mask, go_s, dks, dvs, dk_own, dv_own)

    def one(n, carry):
        span = lens[ids[2] * count + first + n]
        backward_one(n, first + n, span, *ins, grad_q, grad_k, grad_v, grad_plan, *own)
        return carry

    lax.fori_loop(0, count - first, one, 0)
    for value in (*early, normed_t, steps):
        value.wait()
    kinds = [list(early[n::4]) + [late] for n, late in enumerate((grad_q, grad_k, grad_v, grad_plan))]
    spans = [lens[ids[2] * count + c] for c in range(count)]
    g = jnp.concatenate([r[...] for r in kinds[3]], 0) * plan[...]
    for k in range(2 * ITERS - 1, -1, -1):
        axis = 2 - k % 2
        g = g - jnp.exp(steps[k]) * jnp.sum(g, axis=axis, keepdims=True)
    g = jnp.where(plan_allowed(count, spans), g, 0.0).reshape(count * NB, NB)
    for out in (grad_q, grad_k, grad_v):
        out.send()
    d = normed_t.shape[0]
    bias = jnp.zeros((8, d), F32)
    for slot in range(3):
        grad = jnp.zeros((d, d), F32)
        for n, rows in enumerate(kinds[slot]):
            grad += dot_nn(normed_t[:, cuts[n] * LMAX : cuts[n + 1] * LMAX], rows[...])
        grad_s[...] = grad
        scatter_tiles(ids[0], sent, kept, grad_s, 32 * slot)
        prod = grad * w_all[slot].astype(F32)
        prod_s[...] = prod if slot == 0 else prod_s[...] + prod
        rows = [dot_nn(jnp.ones((8, part.shape[0]), LOW), part[...]) for part in kinds[slot]]
        for part in split2(sum(rows[1:], rows[0])):
            bias += dot_nt(part, w_all[slot])
    for value in (pre, summary, sort_one, sort_two, ln_gain, ln_bias, vecs2):
        value.wait()
    before = pre[...]
    share, bell = normal_parts(before)
    small[...] = jnp.zeros_like(small)
    small[0:NB, :] = exact_both(dot_tn, g, before * share)
    small[10:12, :] = vecs2[...]
    gpre = exact_right(dot_nn, g, sort_two[...]) * (share + before * bell)
    grad_s[...] = exact_both(dot_tn, summary[...], gpre)
    scatter_tiles(ids[0], sent, kept, grad_s, 96)
    spread = exact_right(dot_nt, gpre, sort_one[...]) * SUMMARY_SCALE
    gsum[...] = spread
    gsum.send()
    block = iota((count * NB, 1), 0)
    valid = jnp.zeros((count * NB, 1), jnp.int32)
    for s in range(count):
        valid = jnp.where(block // NB == s, jnp.clip(spans[s] - block % NB * BL, 0, BL), valid)
    bias = bias[0:1] + jnp.sum(spread * valid.astype(F32), axis=0, keepdims=True)
    gain = jnp.sum(spread * summary[...], axis=0, keepdims=True) * (1.0 / SUMMARY_SCALE)
    for part in split2(prod_s[...]):
        gain += dot_nt(jnp.ones((8, d), LOW), part)[0:1]
    gain = (gain - ln_bias[...] * bias) / ln_gain[...]
    small[8:9, :] = gain
    small[9:10, :] = bias
    zeros = jnp.zeros((8, 128), LOW)
    for n, target in enumerate((sent, kept)):
        at = pl.ds(pl.multiple_of((ids[0] ^ (1 - n)) * 8, 8), 8)
        for u in range(4):
            tile = small[at, 128 * u : 128 * (u + 1)].astype(LOW)
            for color in range(2):
                for i in range(4):
                    target[u, i, color, 128:136, :] = tile if color == 0 and i == 0 else zeros


def input_kernel(cuts, count, lens, ids, gsum, w_all, ln_gain, *refs):
    groups = len(cuts) - 1
    kinds = [refs[n : 3 * groups : 3] for n in range(3)]
    tokens, grad_middle = refs[3 * groups : 3 * groups + count], refs[3 * groups + count : -1]
    input_grad = refs[-1]
    for value in (gsum, w_all, ln_gain):
        value.wait()
    token, block = iota((LMAX, NB), 0), iota((LMAX, NB), 1)
    for s in range(count):
        group = max(n for n in range(groups) if cuts[n] <= s)
        if cuts[group] == s:
            for slot in range(3):
                kinds[slot][group].wait()
        tokens[s].wait()
        grad_middle[s].wait()
        unit, scale = row_norm(tokens[s][...].astype(F32))
        member = (token // BL == block) & (token < lens[ids[2] * count + s])
        picked = jnp.where(member, 1.0, 0.0).astype(LOW)
        high, mid, low = split3(gsum[s * NB : (s + 1) * NB, :])
        gn = dot_nn(picked, high) + dot_nn(picked, mid) + dot_nn(picked, low)
        at = (s - cuts[group]) * LMAX
        for slot in range(3):
            gn += dot_nt(kinds[slot][group][at : at + LMAX, :], w_all[slot])
        pulled = norm_pull(gn * ln_gain[...], unit, scale)
        input_grad[s * LMAX : (s + 1) * LMAX, :] = (grad_middle[s][...] + pulled).astype(LOW)


def output_kernel(count, down, *refs):
    hidden, middle, output = refs[:count], refs[count:-1], refs[-1]
    down.wait()
    for s in range(count):
        hidden[s].wait()
        middle[s].wait()
        total = middle[s][...] + dot_nn(hidden[s][...], down[...])
        output[s * LMAX : (s + 1) * LMAX, :] = total.astype(LOW)


def each_piece(ids, near, far, place, halved):
    core, mine = ids[0], ids[1] * 2 + ids[2]
    for n, source in enumerate((near, far)):
        for color in range(2):

            def pieces(r, carry, n=n, source=source, color=color):
                unit = (core ^ n) * 4 + (mine ^ r)
                for i in range(4):
                    part = (ids[3] ^ (i // 2)) * 2 + (ids[4] ^ (i % 2)) if halved else i
                    place(color, unit, part, source.buffer.at[r, i // 2, i % 2, color])
                return carry

            if halved:
                lax.fori_loop(0, 4, pieces, 0)
            else:
                for r in range(4):
                    pieces(r, 0)


def place_ffn_kernel(ids, near, far, grad_up, grad_down, grad_o, o_s):
    near.wait()
    far.wait()

    def place(color, unit, part, source):
        quarter = pl.ds(pl.multiple_of(part * 128, 128), 128)
        for j in range(2):
            at = pl.ds(pl.multiple_of(unit * PART + 128 * j, 128), 128)
            block = source[128 * j : 128 * (j + 1), :].astype(F32)
            if color == 0:
                grad_up[quarter, at] = block
            else:
                grad_down[at, quarter] = block.T
        rows = pl.ds(pl.multiple_of(unit * 64 + (part % 2) * 32, 32), 32)
        lanes = pl.ds(pl.multiple_of(256 * color + (part // 2) * 128, 128), 128)
        o_s[rows, lanes] = source[PART : PART + 32, :].astype(F32)

    each_piece(ids, near, far, place, True)
    grad_o[...] = o_s[pl.ds(pl.multiple_of(ids[2] * 256, 256), 256), :]


def place_last_kernel(
    ids, near, far, grad_q, grad_k, grad_v, grad_first, second, gain1, bias1, gain2, bias2, wide, small
):
    near.wait()
    far.wait()
    head = ids[2]

    def place(color, unit, part, source):
        rows = pl.ds(pl.multiple_of(color * 256 + unit * 32 + part * 8, 8), 8)
        wide[...] = source[...].astype(F32)
        for slot, out in enumerate((grad_q, grad_k, grad_v)):
            for t in range(2):
                at = pl.ds(pl.multiple_of((4 * slot + 2 * head + t) * 8, 8), 8)
                out[rows, 128 * t : 128 * (t + 1)] = wide[at, :]
        for m in range(4):
            grad_first[rows, 128 * m : 128 * (m + 1)] = wide[96 + 8 * m : 104 + 8 * m, :]
        if color == 0:
            high = pl.ds(pl.multiple_of((unit // 4) * 8, 8), 8)
            lanes = pl.ds(pl.multiple_of((unit % 4) * 128, 128), 128)
            small[part, high, lanes] = wide[128:136, :]

    each_piece(ids, near, far, place, LAST_HALVED)
    second[...] = small[0, 0:NB, :]
    for n, out in enumerate((gain1, bias1, gain2, bias2)):
        out[...] = small[0, 8 + n : 9 + n, :]


def slice_kernel(ids, w_q, w_k, w_v, w_o, mine):
    core = ids[0]
    lanes = pl.ds(pl.multiple_of(core * 2 * HD, 2 * HD), 2 * HD)
    for slot, w in enumerate((w_q, w_k, w_v)):
        w.wait()
        mine[512 * slot : 512 * (slot + 1), :] = w[:, lanes]
    w_o.wait()
    for m in range(4):
        mine[1536 + 128 * m : 1664 + 128 * m, :] = w_o[lanes, 128 * m : 128 * (m + 1)]


def swap(values, bits, dp_size):
    dp_bits = sum(bit for bit in bits if bit != "head")
    flip = int("head" in bits)
    pairs = [(d * 2 + h, (d ^ dp_bits) * 2 + (h ^ flip)) for d in range(dp_size) for h in range(2)]
    return lax.ppermute(values, AXES, pairs)


def side_of(bit):
    if bit == "head":
        return lax.axis_index("head")
    return (lax.axis_index("dp") // bit) % 2


def pick(values, index, axis=0):
    return lax.dynamic_index_in_dim(values, index, axis, keepdims=False)


def pick_all(arrays, index):
    return [pick(a, index) for a in arrays]


def low_sum(arrays):
    total = arrays[0].astype(F32)
    for a in arrays[1:]:
        total = total + a.astype(F32)
    return total.astype(LOW)


def line_bits(dp_size):
    bits, bit = [], 4
    while bit < dp_size:
        bits.append(bit)
        bit *= 2
    return bits


PLANE = (["head"], [2], [2, "head"])


def sum_chain(sent, kept, dp_size, halve):
    line = line_bits(dp_size)
    got = swap(sent, [1], dp_size)
    got, = yield [sent], [got]
    shape = (4, 2, 2) + kept.shape[2:]
    sums = [kept.reshape(shape), got.reshape(shape)]
    mine = side_of(2) * 2 + side_of("head")
    sents = [low_sum(pick_all(sums, mine ^ (n + 1))) for n in range(3)]
    gots = [swap(v, bits, dp_size) for v, bits in zip(sents, PLANE)]
    gots = yield sents, gots
    sums = pick_all(sums, mine) + list(gots)
    if halve:
        for bit in line[:2]:
            side = side_of(bit)
            sent = low_sum(pick_all(sums, 1 - side))
            got = swap(sent, [bit], dp_size)
            got, = yield [sent], [got]
            sums = pick_all(sums, side) + [got]
    near = low_sum(sums)
    for bit in line[2:] if halve else line:
        got = swap(near, [bit], dp_size)
        got, = yield [near], [got]
        near = low_sum([near, got])
    if halve:
        for bit in (line[1], line[0]):
            got = swap(near, [bit], dp_size)
            got, = yield [near], [got]
            near = jnp.stack([near, got])
    gots = [swap(near, bits, dp_size) for bits in PLANE]
    gots = yield [near], gots
    near = jnp.stack([near, *gots])
    far = swap(near, [1], dp_size)
    far, = yield [near], [far]
    return near, far


class Slots:
    def __init__(self):
        self.running, self.done, self.got = {}, {}, {}

    def start(self, name, chain):
        self.running[name], self.got[name] = chain, None

    def step(self):
        sent = []
        for name, chain in list(self.running.items()):
            try:
                new, self.got[name] = chain.send(self.got[name])
                sent += new
            except StopIteration as end:
                self.done[name] = end.value
                del self.running[name], self.got[name]
        return sent

    def before(self, value):
        return lax.optimization_barrier((value, *self.step()))[0]

    def after(self, value):
        names = list(self.running)
        sizes = [len(self.got[n]) for n in names]
        flat = [g for n in names for g in self.got[n]]
        flat = lax.optimization_barrier((value, *flat))[1:]
        for name, size in zip(names, sizes):
            self.got[name], flat = list(flat[:size]), flat[size:]

    def turn(self, name, last):
        if name not in self.running:
            return last
        got = self.got[name]
        if got is not None:
            self.got[name] = list(lax.optimization_barrier((*got, *last))[: len(got)])
        try:
            sent, self.got[name] = self.running[name].send(self.got[name])
            return sent
        except StopIteration as end:
            self.done[name] = end.value
            del self.running[name]
            return last


def shaped(shape, kind):
    return jax.ShapeDtypeStruct(shape, kind)


class Staged:
    def __init__(self, buffer, copy):
        self.buffer, self.copy, self.sent = buffer, copy, False

    def wait(self):
        self.copy.wait()

    def send(self):
        if not self.sent:
            self.copy.start()
            self.sent = True

    shape = property(lambda self: self.buffer.shape)
    dtype = property(lambda self: self.buffer.dtype)

    def __getitem__(self, at):
        return self.buffer[at]

    def __setitem__(self, at, value):
        self.buffer[at] = value


def call(body, scalars, args, outs, scratch, flops, by_parts=(), limit=VMEM_LIMIT):
    args = [a if isinstance(a, tuple) else (a, None) for a in args]
    views = [jax.eval_shape(lambda v, i=i: v if i is None else v[i], a) for a, i in args]
    n_scalars, n_in, n_out = len(scalars), len(args), len(outs)

    def kernel(*refs):
        head, refs = refs[:n_scalars], refs[n_scalars:]
        sources, refs = refs[:n_in], refs[n_in:]
        targets, refs = refs[:n_out], refs[n_out:]
        taken, refs = refs[:n_in], refs[n_in:]
        made, refs = refs[: n_out - len(by_parts)], refs[n_out - len(by_parts) :]
        sems, own = refs[-1], refs[:-1]
        ins, results = [], []
        for n, (source, (_, index)) in enumerate(zip(sources, args)):
            source = source if index is None else source.at[index]
            copy = pltpu.make_async_copy(source, taken[n], sems.at[n])
            copy.start()
            ins.append(Staged(taken[n], copy))
        made = list(made)
        for n, target in enumerate(targets):
            if n in by_parts:
                results.append(target)
            else:
                buffer = made.pop(0)
                copy = pltpu.make_async_copy(buffer, target, sems.at[n_in + n])
                results.append(Staged(buffer, copy))
        body(*head, *ins, *results, *own)
        results = [r for n, r in enumerate(results) if n not in by_parts]
        for result in results:
            result.send()
        for result in results:
            result.wait()

    space = pltpu.HBM if limit == VMEM_LIMIT else pl.ANY
    smem, hbm = pl.BlockSpec(memory_space=pltpu.SMEM), pl.BlockSpec(memory_space=pltpu.HBM)
    whole = [v for n, v in enumerate(outs) if n not in by_parts]
    buffers = [pltpu.VMEM(v.shape, v.dtype) for v in (*views, *whole)]
    return pl.pallas_call(
        kernel,
        in_specs=[smem] * n_scalars + [pl.BlockSpec(memory_space=space)] * n_in,
        out_specs=[hbm] * n_out,
        out_shape=outs,
        scratch_shapes=buffers + scratch + [pltpu.SemaphoreType.DMA((n_in + n_out,))],
        compiler_params=pltpu.CompilerParams(vmem_limit_bytes=limit),
        cost_estimate=pl.CostEstimate(flops=1 << 34, bytes_accessed=1 << 24, transcendentals=0),
    )(*scalars, *[a for a, _ in args])


def on_device(
    dp_size,
    tokens,
    lengths,
    ln1_gain,
    ln1_bias,
    w_query,
    w_key,
    w_value,
    w_out,
    sort_first,
    sort_second,
    ln2_gain,
    ln2_bias,
    w_up,
    w_down,
    cotangent,
):
    rows_all, d = tokens.shape
    count = rows_all // LMAX
    ff = w_up.shape[1]
    core = side_of(1)
    ids = jnp.stack([core, side_of(2), side_of("head"), side_of(4), side_of(8)]).astype(jnp.int32)

    gain1, bias1, gain2, bias2 = (v.reshape(1, d) for v in (ln1_gain, ln1_bias, ln2_gain, ln2_bias))
    second_t = sort_second.T
    mine = call(
        slice_kernel, (ids,), (w_query, w_key, w_value, w_out), [shaped((4 * d, 2 * HD), LOW)], [],
        1 << 20,
    )[0]
    near_w = swap(mine, ["head"], dp_size)

    low_rows, wide_rows = shaped((rows_all, d), LOW), shaped((rows_all, d), F32)
    low_cols = shaped((d, rows_all), LOW)
    small_plan = shaped((count, NB, NB), F32)
    blocks = shaped((count * NB, d), F32)

    normed, normed_t, summary, pre, steps, plan, cot_t, grad_hidden = call(
        functools.partial(prepare_kernel, count), (lengths, ids),
        (tokens, gain1, bias1, sort_first, second_t, cotangent, w_down),
        [low_rows, low_cols, blocks, blocks, shaped((2 * ITERS, count, NB, NB), F32), small_plan]
        + [low_cols, shaped((rows_all, ff), LOW)],
        [], 2 * rows_all * d * ff,
    )
    near_w, normed = lax.optimization_barrier((near_w, normed))
    far_w = swap(near_w, [1], dp_size)

    (
        q, k, v, sk, sv, p, w_all, sent, kept, hidden, middle, grad_middle, grad_att, vecs2
    ) = call(
        functools.partial(forward_kernel, count), (lengths, ids),
        (w_query, w_key, w_value, w_out, near_w, far_w, normed, plan, tokens, gain2, bias2)
        + (w_up, grad_hidden, cot_t, cotangent),
        [low_rows] * 5 + [shaped((count * 2 * LMAX, LMAX), LOW), shaped((4, d, d), LOW)]
        + [shaped((4, 4, 2, PART + 32, 128), LOW)] * 2
        + [shaped((rows_all, ff), LOW), wide_rows, wide_rows, low_rows, shaped((2, d), F32)],
        [pltpu.VMEM((LMAX, d), LOW)] * 2
        + [pltpu.VMEM((d, rows_all), LOW), pltpu.VMEM((rows_all, d), LOW)]
        + [pltpu.VMEM((d, rows_all), LOW)]
        + [pltpu.VMEM((rows_all, PART), F32)] * 2 + [pltpu.VMEM((rows_all, PART), LOW)] * 4
        + [pltpu.VMEM((rows_all, d), F32)] + [pltpu.VMEM((d, d), F32)]
        + [pltpu.VMEM((2, 4, 4, 2, PART + 32, 128), LOW)]
        + [pltpu.SemaphoreType.DMA((ff // PART + 2,))],
        24 * rows_all * d * d, by_parts=(7, 8),
    )
    slots = Slots()
    slots.start("ffn", sum_chain(sent, kept, dp_size, True))
    work = [pltpu.VMEM((LMAX, d), LOW)] * 2 + [pltpu.VMEM((LMAX, d), F32)] * 4
    cuts = (0, 1, 3, count)

    def inputs_of(first, end, w, grad_att):
        rows, probs = slice(first * LMAX, end * LMAX), slice(first * 2 * LMAX, end * 2 * LMAX)
        args = ((grad_att, rows), w) + tuple((a, rows) for a in (q, k, v, sk, sv))
        return args + ((p, probs), plan)

    def after(value, last):
        return lax.optimization_barrier((value, *last))[0]

    grads = []
    for first, end in zip(cuts[:-2], cuts[1:-1]):
        out = call(
            functools.partial(backward_kernel, first, count), (lengths, ids),
            inputs_of(first, end, (w_all, slice(3, 4)), slots.before(grad_att)),
            [shaped(((end - first) * LMAX, d), LOW)] * 3 + [shaped((end - first, NB, NB), F32)],
            work, 4 << 30,
        )
        slots.after(out[-1])
        grads.append(out)
    first, late = cuts[-2], count - cuts[-2]
    late_rows = shaped((late * LMAX, d), LOW)
    sent, kept, *late_grads, gsum = call(
        functools.partial(last_kernel, cuts, count), (lengths, ids),
        inputs_of(first, count, w_all, after(grad_att, out[:1]))
        + (*(g for out in grads for g in out), normed_t, steps, pre, summary, sort_first, second_t)
        + (gain1, bias1, vecs2),
        [shaped((4, 4, 2, 136, 128), LOW)] * 2 + [late_rows] * 3 + [blocks],
        work + [pltpu.VMEM((late, NB, NB), F32), pltpu.VMEM((16, d), F32)]
        + [pltpu.VMEM((d, d), F32)] * 2,
        16 << 30,
    )
    slots.after(sent)
    grads.append(late_grads)
    seqs = [slice(s * LMAX, (s + 1) * LMAX) for s in range(count)]

    last = slots.turn("ffn", [gsum])
    slots.start("last", sum_chain(after(sent, last), kept, dp_size, LAST_HALVED))
    for name in TURNS:
        if name == "output":
            output = call(
                functools.partial(output_kernel, count), (),
                (after(w_down, last), *((hidden, r) for r in seqs), *((middle, r) for r in seqs)),
                [low_rows], [], 1 << 30,
            )[0]
            last = [output]
        elif name == "input":
            input_grad = call(
                functools.partial(input_kernel, cuts, count), (lengths, ids),
                (after(gsum, last), (w_all, slice(0, 3)), gain1)
                + tuple(g for out in grads for g in out[:3])
                + tuple((tokens, r) for r in seqs) + tuple((grad_middle, r) for r in seqs),
                [low_rows], [], 1 << 30,
            )[0]
            last = [input_grad]
        else:
            last = slots.turn(name, last)
    while "ffn" in slots.running:
        last = slots.turn("ffn", last)
    up_sum, down_sum, o_sum = call(
        place_ffn_kernel, (ids,), slots.done["ffn"],
        [shaped(s, F32) for s in ((d, ff), (ff, d), w_out.shape)],
        [pltpu.VMEM((d, d), F32)], 1 << 28, limit=20 << 20,
    )
    last = [o_sum]
    while "last" in slots.running:
        last = slots.turn("last", last)
    q_sum, k_sum, v_sum, first_sum, second_sum, *vec_sums = call(
        place_last_kernel, (ids,), slots.done["last"],
        [shaped(w_query.shape, F32)] * 3 + [shaped((d, d), F32), shaped((NB, d), F32)]
        + [shaped((1, d), F32)] * 4,
        [pltpu.VMEM((136, 128), F32), pltpu.VMEM((4, 16, d), F32)], 1 << 26, limit=8 << 20,
    )
    vec_sums = [v.reshape(d) for v in vec_sums]
    return (
        output,
        input_grad,
        vec_sums[0],
        vec_sums[1],
        q_sum,
        k_sum,
        v_sum,
        o_sum,
        first_sum,
        second_sum.T,
        vec_sums[2],
        vec_sums[3],
        up_sum,
        down_sum,
    )


def solution(mesh):
    tokens, copied, columns = P(AXES, None), P(), P(None, "head")
    return jax.shard_map(
        functools.partial(on_device, mesh.shape["dp"]),
        mesh=mesh,
        in_specs=(tokens, P("dp"), copied, copied, columns, columns, columns, P("head", None))
        + (copied,) * 6
        + (tokens,),
        out_specs=(tokens, tokens, copied, copied, columns, columns, columns, P("head", None))
        + (copied,) * 6,
        check_vma=False,
    )
```

```python
import functools

import jax
import jax.numpy as jnp
from jax import lax
from jax.experimental import pallas as pl
from jax.experimental.pallas import tpu as pltpu
from jax.sharding import PartitionSpec as P

HD = 64
BL = 32
ITERS = 8
LMAX = 256
NB = LMAX // BL
SUMMARY_SCALE = BL**-0.5
F32 = jnp.float32
LOW = jnp.bfloat16
AXES = ("dp", "head")
VMEM_LIMIT = 56 * 1024 * 1024
TURNS = ["last", "last", "ffn", "output", "last", "ffn", "input", "ffn", "ffn", "last", "last"]
LAST_HALVED = False

ERF_P = 0.3875
ERF_C = (
    0.23607149955804155,
    0.07450957017858355,
    0.6926085194492264,
    -0.6975625302575207,
    0.9269567150083973,
    -0.23258376165572045,
)


def normal_parts(v):
    size = jnp.abs(v)
    bell = jnp.exp(v * v * -0.5)
    t = 1.0 / (1.0 + size * (ERF_P * 0.5**0.5))
    poly = ERF_C[5]
    for coef in ERF_C[4::-1]:
        poly = poly * t + coef
    tail = (0.5 * t) * poly * bell
    return jnp.where(v >= 0, 1.0 - tail, tail), bell * 0.3989422804014327


def dot_nn(a, b):
    return lax.dot_general(a, b, (((1,), (0,)), ((), ())), preferred_element_type=F32)


def dot_nt(a, b):
    return lax.dot_general(a, b, (((1,), (1,)), ((), ())), preferred_element_type=F32)


def dot_tn(a, b):
    return lax.dot_general(a, b, (((0,), (0,)), ((), ())), preferred_element_type=F32)


def split3(v):
    high = v.astype(LOW)
    left = v - high.astype(F32)
    mid = left.astype(LOW)
    return high, mid, (left - mid.astype(F32)).astype(LOW)


def split2(v):
    high = v.astype(LOW)
    return high, (v - high.astype(F32)).astype(LOW)


def exact_right(dot, v, w):
    a, b, c = split3(v)
    return dot(a, w) + dot(b, w) + dot(c, w)


def exact_both(dot, v, w):
    a, b, c = split3(v)
    d, e, f = split3(w)
    return dot(a, d) + (dot(a, e) + dot(b, d)) + (dot(b, e) + dot(a, f) + dot(c, d))


def row_norm(x):
    center = x - jnp.mean(x, axis=-1, keepdims=True)
    spread = jnp.mean(center * center, axis=-1, keepdims=True)
    scale = lax.rsqrt(spread + 1e-05)
    return center * scale, scale


def norm_pull(grad, unit, scale):
    return scale * (
        grad
        - jnp.mean(grad, axis=-1, keepdims=True)
        - unit * jnp.mean(grad * unit, axis=-1, keepdims=True)
    )


def iota(shape, axis):
    return lax.broadcasted_iota(jnp.int32, shape, axis)


def plan_allowed(count, spans):
    shape = (count, NB, NB)
    seq = iota(shape, 0)
    span = jnp.zeros(shape, jnp.int32)
    for s in range(count):
        span = jnp.where(seq == s, spans[s], span)
    row, col = iota(shape, 1), iota(shape, 2)
    row_ok, col_ok = row * BL < span, col * BL < span
    return (row_ok & col_ok) | ((row == col) & ~row_ok)


def head_mask(value):
    row, lane = iota((LMAX, 8 * HD), 0), iota((LMAX, 8 * HD), 1)
    return jnp.where(row // BL == lane // HD, value, 0.0).astype(LOW)


def spread_plan(plan, flip):
    pick = jnp.where(iota((LMAX, NB), 0) // BL == iota((LMAX, NB), 1), 1.0, 0.0).astype(LOW)
    same = (iota((LMAX, LMAX), 0) % BL) == (iota((LMAX, LMAX), 1) % BL)
    parts = []
    for part in split2(plan):
        tall = (dot_nt if flip else dot_nn)(pick, part).astype(LOW)
        parts.append(jnp.where(same, dot_nt(tall, pick), 0.0).astype(LOW))
    return parts


def pair_rows(left_t, right, m, lane_low):
    both = dot_nn(left_t[2 * BL * m : 2 * BL * (m + 1), :], right[:, 2 * HD * m : 2 * HD * (m + 1)])
    return jnp.where(lane_low, both[:BL], both[BL:])


PART = 256
PIECE = 64


def prepare_kernel(
    count, lens, ids, tokens, ln_gain, ln_bias, first, second, cotangent, down,
    normed, normed_t, summary, pre, steps, plan, cot_t, grad_hidden,
):
    spans = [lens[ids[2] * count + s] for s in range(count)]
    tokens.wait()
    ln_gain.wait()
    ln_bias.wait()
    gain, bias = ln_gain[...], ln_bias[...]
    token, block = iota((NB, LMAX), 1), iota((NB, LMAX), 0)

    def norm(s, carry):
        rows = pl.ds(pl.multiple_of(s * LMAX, LMAX), LMAX)
        unit, _ = row_norm(tokens[rows, :].astype(F32))
        low = (unit * gain + bias).astype(LOW)
        normed[rows, :] = low
        normed_t[:, rows] = low.T
        member = (token // BL == block) & (token < lens[ids[2] * count + s])
        picked = jnp.where(member, 1.0, 0.0).astype(LOW)
        blocks = pl.ds(pl.multiple_of(s * NB, NB), NB)
        summary[blocks, :] = dot_nn(picked, low) * SUMMARY_SCALE
        return carry

    lax.fori_loop(0, count, norm, 0)
    for out in (normed, normed_t, summary):
        out.send()
    for value in (first, second, cotangent, down):
        value.wait()
    before = exact_right(dot_nn, summary[...], first[...])
    pre[...] = before
    gate, _ = normal_parts(before)
    logits = exact_right(dot_nt, before * gate, second[...])
    logits = logits.reshape(count, NB, NB)
    x = jnp.where(plan_allowed(count, spans), logits, -1e30)
    for k in range(2 * ITERS):
        axis = 2 - k % 2
        top = jnp.max(x, axis=axis, keepdims=True)
        x = x - (top + jnp.log(jnp.sum(jnp.exp(x - top), axis=axis, keepdims=True)))
        steps[k] = x
    plan[...] = jnp.exp(x)
    for out in (pre, steps, plan):
        out.send()
    rows = cotangent[...]
    for s in range(count):
        seq = slice(s * LMAX, (s + 1) * LMAX)
        cot_t[:, seq] = cotangent[seq, :].T
    cot_t.send()

    def expand(c, carry):
        at = pl.ds(pl.multiple_of(c * PART, PART), PART)
        grad_hidden[:, at] = dot_nt(rows, down[at, :]).astype(LOW)
        return carry

    lax.fori_loop(0, down.shape[0] // PART, expand, 0)


def forward_kernel(
    count, lens, ids, w_q, w_k, w_v, w_o, near_w, far_w, normed, plan, tokens, ln_gain, ln_bias,
    up, grad_hidden, cot_t, cotangent,
    q_out, k_out, v_out, sk_out, sv_out, p_out, w_all, sent, kept, hidden_out, middle, grad_middle,
    grad_att, grad_vecs,
    mask, mixed, mixed_t, normed2, normed2_t, up0, up1, hid0, hid1, gup0, gup1, gn_s,
    grad_s, parts, part_sems,
):
    mask[...] = head_mask(HD**-0.5)
    for value in (w_q, w_k, w_v, w_o, near_w, far_w, normed, plan):
        value.wait()
    core, head = ids[0], ids[2]
    half, quarter = 4 * HD, 2 * HD
    own = pl.ds(pl.multiple_of(head * half, half), half)
    near = pl.ds(pl.multiple_of((1 - head) * half + core * quarter, quarter), quarter)
    far = pl.ds(pl.multiple_of((1 - head) * half + (1 - core) * quarter, quarter), quarter)
    for slot, w in enumerate((w_q, w_k, w_v)):
        w_all[slot, :, own] = w[...]
        w_all[slot, :, near] = near_w[512 * slot : 512 * (slot + 1), :]
        w_all[slot, :, far] = far_w[512 * slot : 512 * (slot + 1), :]
    w_all[3, own, :] = w_o[...]
    for m in range(4):
        lanes, rows = slice(128 * m, 128 * (m + 1)), slice(1536 + 128 * m, 1664 + 128 * m)
        w_all[3, near, lanes] = near_w[rows, :]
        w_all[3, far, lanes] = far_w[rows, :]
    w_all.send()
    keep_row = iota((LMAX, 8 * HD), 0)
    key_row = iota((2 * BL, 8 * BL), 0)
    query = iota((2 * BL, 8 * BL), 1) % BL
    lane_low = iota((BL, 2 * HD), 1) < HD

    def one(s, carry):
        span = lens[ids[2] * count + s]
        seq = pl.ds(pl.multiple_of(s * LMAX, LMAX), LMAX)
        n = normed[seq, :]
        keep = keep_row < span
        q_out[seq, :] = dot_nn(n, w_all[0]).astype(LOW)
        key = jnp.where(keep, dot_nn(n, w_all[1]), 0.0).astype(LOW)
        value = jnp.where(keep, dot_nn(n, w_all[2]), 0.0).astype(LOW)
        k_out[seq, :] = key
        v_out[seq, :] = value
        high, low = spread_plan(plan[s], False)
        sk_out[seq, :] = (dot_nn(high, key) + dot_nn(low, key)).astype(LOW)
        sv_out[seq, :] = (dot_nn(high, value) + dot_nn(low, value)).astype(LOW)
        rows = [pl.ds(pl.multiple_of(s * LMAX + i * BL, BL), BL) for i in range(NB)]
        scores = []
        for r in rows:
            keys = jnp.concatenate([k_out[r, :], sk_out[r, :]], 0)
            wide = jnp.concatenate([q_out[r, :]] * 8, 0) * mask[...]
            scores.append(dot_nt(keys, wide))
        weights = []
        for i, score in enumerate(scores):
            valid = jnp.where(key_row < BL, i * BL + key_row, i * BL) < span
            score = jnp.where(valid | (i * BL + query >= span), score, -1e30)
            grown = jnp.exp(score - jnp.max(score, axis=0, keepdims=True))
            weights.append(grown * (1.0 / jnp.sum(grown, axis=0, keepdims=True)))
        for i, weight in enumerate(weights):
            at = pl.multiple_of(s * 2 * LMAX + i * 2 * BL, 2 * BL)
            p_out[pl.ds(at, 2 * BL), :] = weight.astype(LOW)
        turned = [weight.T.astype(LOW) for weight in weights]
        for i, (r, weight_t) in enumerate(zip(rows, turned)):
            values = jnp.concatenate([v_out[r, :], sv_out[r, :]], 0)
            out = jnp.concatenate([pair_rows(weight_t, values, m, lane_low) for m in range(4)], 1)
            out = jnp.where(iota((BL, 8 * HD), 0) + i * BL < span, out, 0.0)
            mixed[i * BL : (i + 1) * BL, :] = out.astype(LOW)
        blended = mixed[...]
        mixed_t[:, seq] = blended.T

        @pl.when(s == 0)
        def _():
            tokens.wait()
            ln_gain.wait()
            ln_bias.wait()

        mid = tokens[seq, :].astype(F32) + dot_nn(blended, w_all[3])
        middle[seq, :] = mid
        unit, _ = row_norm(mid)
        low2 = (unit * ln_gain[...] + ln_bias[...]).astype(LOW)
        normed2[seq, :] = low2
        normed2_t[:, seq] = low2.T
        return carry

    lax.fori_loop(0, count, one, 0)
    for out in (q_out, k_out, v_out, sk_out, sv_out, p_out, middle):
        out.send()
    for value in (up, grad_hidden, cot_t, cotangent):
        value.wait()
    units = up.shape[1] // PART // 2
    quarter = normed.shape[1] // 4
    ups, hids, gups = (up0, up1), (hid0, hid1), (gup0, gup1)

    def columns(c):
        unit = ((c // units) ^ (1 - core)) * units + c % units
        return pl.ds(pl.multiple_of(unit * PART, PART), PART)

    def expand(c, side):
        ups[side][...] = dot_nn(normed2[...], up[:, columns(c)])

    def gate_rows(c, side, rows):
        v = ups[side][rows, :]
        share, bell = normal_parts(v)
        hidden = (v * share).astype(LOW)
        hids[side][rows, :] = hidden
        hidden_out[rows, columns(c)] = hidden
        gh = grad_hidden[rows, columns(c)].astype(F32)
        gups[side][rows, :] = (gh * (share + v * bell)).astype(LOW)

    def gate(c, side):
        for r in range(up0.shape[0] // PIECE):
            gate_rows(c, side, slice(r * PIECE, (r + 1) * PIECE))

    def gate_alone(c, side):
        def piece(r, carry):
            gate_rows(c, side, pl.ds(pl.multiple_of(r * PIECE, PIECE), PIECE))
            return carry

        lax.fori_loop(0, up0.shape[0] // PIECE, piece, 0)

    def reduce(c, side):
        hidden, gup = hids[side][...], gups[side][...]
        for color, (left, right) in enumerate(((normed2_t, gup), (cot_t, hidden))):
            grad = dot_nn(left[...], right).astype(LOW)
            for j in range(PART // 128):
                for i in range(4):
                    tile = grad[quarter * i : quarter * (i + 1), 128 * j : 128 * (j + 1)]
                    at = slice(quarter * j, quarter * (j + 1))
                    parts[c // units, c % units, i, color, at, :] = tile
        gn_s[...] += dot_nt(gup, up[:, columns(c)])

    def part_copy(n, u):
        at = (u, slice(None), slice(None), slice(0, PART))
        return pltpu.make_async_copy(
            parts.at[n].at[at], (sent, kept)[n].at[at], part_sems.at[n * units + u]
        )

    gn_s[...] = jnp.zeros_like(gn_s)
    last = 2 * units - 1
    expand(0, 0)
    expand(1, 1)
    gate_alone(0, 0)

    def steps(i, carry):
        for h in range(2):
            c = 2 * i + 1 + h
            expand(c + 1, h)
            gate(c, 1 - h)
            reduce(c - 1, h)
        return carry

    lax.fori_loop(0, units - 1, steps, 0)
    for u in range(units):
        part_copy(0, u).start()
    gate(last, 1)
    hidden_out.send()
    reduce(last - 1, 0)
    reduce(last, 1)

    def pull(s, carry):
        gain, bias = carry
        seq = pl.ds(pl.multiple_of(s * LMAX, LMAX), LMAX)
        gn, mid = gn_s[seq, :], middle[seq, :]
        unit, scale = row_norm(mid)
        gmid = cotangent[seq, :].astype(F32) + norm_pull(gn * ln_gain[...], unit, scale)
        grad_middle[seq, :] = gmid
        grad_att[seq, :] = gmid.astype(LOW)
        gain = gain + jnp.sum(gn * unit, axis=0, keepdims=True)
        return gain, bias + jnp.sum(gn, axis=0, keepdims=True)

    zero = jnp.zeros((1, middle.shape[1]), F32)
    gain, bias = lax.fori_loop(0, count, pull, (zero, zero))
    for out in (grad_att, grad_middle):
        out.send()
    grad_vecs[0:1, :] = gain
    grad_vecs[1:2, :] = bias
    for u in range(units):
        part_copy(1, u).start()
    grad_s[...] = dot_nn(mixed_t[...], grad_att[...])
    tails = []
    for n, target in enumerate((sent, kept)):
        base = (core ^ (1 - n)) * units
        for j in range(units):
            for m in range(4):
                for h in range(2):
                    at = pl.multiple_of((base + j) * 64 + 32 * h, 32)
                    tile = grad_s[pl.ds(at, 32), 128 * m : 128 * (m + 1)].astype(LOW)
                    parts[n, j, 2 * (m % 2) + h, m // 2, PART : PART + 32, :] = tile
        at = (slice(None), slice(None), slice(None), slice(PART, PART + 32))
        tail = pltpu.make_async_copy(
            parts.at[n].at[at], target.at[at], part_sems.at[2 * units + n]
        )
        tail.start()
        tails.append(tail)
    for u in range(units):
        part_copy(0, u).wait()
        part_copy(1, u).wait()
    for tail in tails:
        tail.wait()


def scatter_tiles(core, sent, kept, wide, base):
    for n, target in enumerate((sent, kept)):

        def unit(k, carry, n=n, target=target):
            color, u = k // 4, k % 4
            at = (color * 8 + (core ^ (1 - n)) * 4 + u) * 32
            tile = wide[pl.ds(pl.multiple_of(at, 32), 32), :].astype(LOW)
            for p in range(4):
                for m in range(4):
                    part = tile[8 * p : 8 * (p + 1), 128 * m : 128 * (m + 1)]
                    target[u, p, color, base + 8 * m : base + 8 * (m + 1), :] = part
            return carry

        lax.fori_loop(0, 8, unit, 0)


def backward_one(
    local, plan_at, span, grad_att, w_o, q_in, k_in, v_in, sk_in, sv_in, p_in, plan,
    grad_q, grad_k, grad_v, grad_plan, mask, go_s, dks, dvs, dk_own, dv_own,
):
    base = local * LMAX
    seq = pl.ds(pl.multiple_of(base, LMAX), LMAX)
    gmixed = dot_nt(grad_att[seq, :], w_o[...]).astype(LOW)
    keep = iota((LMAX, 8 * HD), 0) < span
    go_s[...] = jnp.where(keep, gmixed, jnp.zeros_like(gmixed))
    lane_low = iota((BL, 2 * HD), 1) < HD
    rows = [pl.ds(pl.multiple_of(base + i * BL, BL), BL) for i in range(NB)]
    probs = [pl.ds(pl.multiple_of(2 * base + i * 2 * BL, 2 * BL), 2 * BL) for i in range(NB)]
    own_rows = [slice(i * BL, (i + 1) * BL) for i in range(NB)]
    grads, scores = [], []
    for r, at, mine in zip(rows, probs, own_rows):
        values = jnp.concatenate([v_in[r, :], sv_in[r, :]], 0)
        gwide = jnp.concatenate([go_s[mine, :]] * 8, 0) * mask[...]
        grads.append(dot_nt(values, gwide))
        dv = dot_nn(p_in[at, :], gwide)
        dv_own[mine, :] = dv[:BL]
        dvs[mine, :] = dv[BL:]
    for at, gweights in zip(probs, grads):
        wide = p_in[at, :].astype(F32)
        total = jnp.sum(wide * gweights, axis=0, keepdims=True)
        scores.append(wide * (gweights - total))
    turned = [gscores.T.astype(LOW) for gscores in scores]
    for r, mine, gscores in zip(rows, own_rows, scores):
        qwide = jnp.concatenate([q_in[r, :]] * 8, 0) * mask[...]
        dk = dot_nn(gscores.astype(LOW), qwide) * HD**-0.5
        dk_own[mine, :] = dk[:BL]
        dks[mine, :] = dk[BL:]
    for r, gscores_t in zip(rows, turned):
        keys = jnp.concatenate([k_in[r, :], sk_in[r, :]], 0)
        dq = jnp.concatenate([pair_rows(gscores_t, keys, m, lane_low) for m in range(4)], 1)
        grad_q[r, :] = (dq * HD**-0.5).astype(LOW)
    same = (iota((LMAX, LMAX), 0) % BL) == (iota((LMAX, LMAX), 1) % BL)
    high, low = spread_plan(plan[plan_at], True)
    cross = jnp.zeros((LMAX, LMAX), F32)
    for own, sorted_part, kept, target in (
        (dk_own, dks, k_in, grad_k),
        (dv_own, dvs, v_in, grad_v),
    ):
        g_high, g_low = split2(sorted_part[...])
        kept_rows = kept[seq, :]
        cross += dot_nt(g_high, kept_rows) + dot_nt(g_low, kept_rows)
        total = own[...] + (dot_nn(high, g_high) + (dot_nn(high, g_low) + dot_nn(low, g_high)))
        target[seq, :] = jnp.where(keep, total, 0.0).astype(LOW)
    cross = jnp.where(same, cross, 0.0)
    rows8 = jnp.sum(cross.reshape(NB, BL, LMAX), axis=1)
    pick = jnp.where(iota((LMAX, NB), 0) // BL == iota((LMAX, NB), 1), 1.0, 0.0).astype(LOW)
    grad_plan[local] = exact_right(dot_nn, rows8, pick)


def backward_kernel(
    first, count, lens, ids, grad_att, w_all, q_in, k_in, v_in, sk_in, sv_in, p_in, plan,
    grad_q, grad_k, grad_v, grad_plan, mask, *own,
):
    mask[...] = head_mask(1.0)
    ins = (grad_att, w_all, q_in, k_in, v_in, sk_in, sv_in, p_in, plan)
    for value in ins:
        value.wait()
    ins = (grad_att, w_all.buffer.at[0], *ins[2:])

    def one(n, carry):
        span = lens[ids[2] * count + first + n]
        backward_one(
            n, first + n, span, *ins, grad_q, grad_k, grad_v, grad_plan, mask, *own
        )
        return carry

    lax.fori_loop(0, grad_q.shape[0] // LMAX, one, 0)


def last_kernel(cuts, count, lens, ids, grad_att, w_all, q_in, k_in, v_in, sk_in, sv_in, p_in, plan, *refs):
    first, groups = cuts[-2], len(cuts) - 2
    early, refs = refs[: 4 * groups], refs[4 * groups :]
    normed_t, steps, pre, summary, sort_one, sort_two, ln_gain, ln_bias, vecs2 = refs[:9]
    sent, kept, grad_q, grad_k, grad_v, gsum = refs[9:15]
    mask, go_s, dks, dvs, dk_own, dv_own, grad_plan, small, grad_s, prod_s = refs[15:]
    mask[...] = head_mask(1.0)
    ins = (grad_att, w_all, q_in, k_in, v_in, sk_in, sv_in, p_in, plan)
    for value in ins:
        value.wait()
    ins = (grad_att, w_all.buffer.at[3], *ins[2:])
    own = (mask, go_s, dks, dvs, dk_own, dv_own)

    def one(n, carry):
        span = lens[ids[2] * count + first + n]
        backward_one(n, first + n, span, *ins, grad_q, grad_k, grad_v, grad_plan, *own)
        return carry

    lax.fori_loop(0, count - first, one, 0)
    for value in (*early, normed_t, steps):
        value.wait()
    kinds = [list(early[n::4]) + [late] for n, late in enumerate((grad_q, grad_k, grad_v, grad_plan))]
    spans = [lens[ids[2] * count + c] for c in range(count)]
    g = jnp.concatenate([r[...] for r in kinds[3]], 0) * plan[...]
    for k in range(2 * ITERS - 1, -1, -1):
        axis = 2 - k % 2
        g = g - jnp.exp(steps[k]) * jnp.sum(g, axis=axis, keepdims=True)
    g = jnp.where(plan_allowed(count, spans), g, 0.0).reshape(count * NB, NB)
    for out in (grad_q, grad_k, grad_v):
        out.send()
    d = normed_t.shape[0]
    bias = jnp.zeros((8, d), F32)
    for slot in range(3):
        grad = jnp.zeros((d, d), F32)
        for n, rows in enumerate(kinds[slot]):
            grad += dot_nn(normed_t[:, cuts[n] * LMAX : cuts[n + 1] * LMAX], rows[...])
        grad_s[...] = grad
        scatter_tiles(ids[0], sent, kept, grad_s, 32 * slot)
        prod = grad * w_all[slot].astype(F32)
        prod_s[...] = prod if slot == 0 else prod_s[...] + prod
        rows = [dot_nn(jnp.ones((8, part.shape[0]), LOW), part[...]) for part in kinds[slot]]
        for part in split2(sum(rows[1:], rows[0])):
            bias += dot_nt(part, w_all[slot])
    for value in (pre, summary, sort_one, sort_two, ln_gain, ln_bias, vecs2):
        value.wait()
    before = pre[...]
    share, bell = normal_parts(before)
    small[...] = jnp.zeros_like(small)
    small[0:NB, :] = exact_both(dot_tn, g, before * share)
    small[10:12, :] = vecs2[...]
    gpre = exact_right(dot_nn, g, sort_two[...]) * (share + before * bell)
    grad_s[...] = exact_both(dot_tn, summary[...], gpre)
    scatter_tiles(ids[0], sent, kept, grad_s, 96)
    spread = exact_right(dot_nt, gpre, sort_one[...]) * SUMMARY_SCALE
    gsum[...] = spread
    gsum.send()
    block = iota((count * NB, 1), 0)
    valid = jnp.zeros((count * NB, 1), jnp.int32)
    for s in range(count):
        valid = jnp.where(block // NB == s, jnp.clip(spans[s] - block % NB * BL, 0, BL), valid)
    bias = bias[0:1] + jnp.sum(spread * valid.astype(F32), axis=0, keepdims=True)
    gain = jnp.sum(spread * summary[...], axis=0, keepdims=True) * (1.0 / SUMMARY_SCALE)
    for part in split2(prod_s[...]):
        gain += dot_nt(jnp.ones((8, d), LOW), part)[0:1]
    gain = (gain - ln_bias[...] * bias) / ln_gain[...]
    small[8:9, :] = gain
    small[9:10, :] = bias
    zeros = jnp.zeros((8, 128), LOW)
    for n, target in enumerate((sent, kept)):
        at = pl.ds(pl.multiple_of((ids[0] ^ (1 - n)) * 8, 8), 8)
        for u in range(4):
            tile = small[at, 128 * u : 128 * (u + 1)].astype(LOW)
            for color in range(2):
                for i in range(4):
                    target[u, i, color, 128:136, :] = tile if color == 0 and i == 0 else zeros


def input_kernel(cuts, count, lens, ids, gsum, w_all, ln_gain, *refs):
    groups = len(cuts) - 1
    kinds = [refs[n : 3 * groups : 3] for n in range(3)]
    tokens, grad_middle = refs[3 * groups : 3 * groups + count], refs[3 * groups + count : -1]
    input_grad = refs[-1]
    for value in (gsum, w_all, ln_gain):
        value.wait()
    token, block = iota((LMAX, NB), 0), iota((LMAX, NB), 1)
    for s in range(count):
        group = max(n for n in range(groups) if cuts[n] <= s)
        if cuts[group] == s:
            for slot in range(3):
                kinds[slot][group].wait()
        tokens[s].wait()
        grad_middle[s].wait()
        unit, scale = row_norm(tokens[s][...].astype(F32))
        member = (token // BL == block) & (token < lens[ids[2] * count + s])
        picked = jnp.where(member, 1.0, 0.0).astype(LOW)
        high, mid, low = split3(gsum[s * NB : (s + 1) * NB, :])
        gn = dot_nn(picked, high) + dot_nn(picked, mid) + dot_nn(picked, low)
        at = (s - cuts[group]) * LMAX
        for slot in range(3):
            gn += dot_nt(kinds[slot][group][at : at + LMAX, :], w_all[slot])
        pulled = norm_pull(gn * ln_gain[...], unit, scale)
        input_grad[s * LMAX : (s + 1) * LMAX, :] = (grad_middle[s][...] + pulled).astype(LOW)


def output_kernel(count, down, *refs):
    hidden, middle, output = refs[:count], refs[count:-1], refs[-1]
    down.wait()
    for s in range(count):
        hidden[s].wait()
        middle[s].wait()
        total = middle[s][...] + dot_nn(hidden[s][...], down[...])
        output[s * LMAX : (s + 1) * LMAX, :] = total.astype(LOW)


def each_piece(ids, near, far, place, halved):
    core, mine = ids[0], ids[1] * 2 + ids[2]
    for n, source in enumerate((near, far)):
        for color in range(2):

            def pieces(r, carry, n=n, source=source, color=color):
                unit = (core ^ n) * 4 + (mine ^ r)
                for i in range(4):
                    part = (ids[3] ^ (i // 2)) * 2 + (ids[4] ^ (i % 2)) if halved else i
                    place(color, unit, part, source.buffer.at[r, i // 2, i % 2, color])
                return carry

            if halved:
                lax.fori_loop(0, 4, pieces, 0)
            else:
                for r in range(4):
                    pieces(r, 0)


def place_ffn_kernel(ids, near, far, grad_up, grad_down, grad_o, o_s):
    near.wait()
    far.wait()

    def place(color, unit, part, source):
        quarter = pl.ds(pl.multiple_of(part * 128, 128), 128)
        for j in range(2):
            at = pl.ds(pl.multiple_of(unit * PART + 128 * j, 128), 128)
            block = source[128 * j : 128 * (j + 1), :].astype(F32)
            if color == 0:
                grad_up[quarter, at] = block
            else:
                grad_down[at, quarter] = block.T
        rows = pl.ds(pl.multiple_of(unit * 64 + (part % 2) * 32, 32), 32)
        lanes = pl.ds(pl.multiple_of(256 * color + (part // 2) * 128, 128), 128)
        o_s[rows, lanes] = source[PART : PART + 32, :].astype(F32)

    each_piece(ids, near, far, place, True)
    grad_o[...] = o_s[pl.ds(pl.multiple_of(ids[2] * 256, 256), 256), :]


def place_last_kernel(
    ids, near, far, grad_q, grad_k, grad_v, grad_first, second, gain1, bias1, gain2, bias2, wide, small
):
    near.wait()
    far.wait()
    head = ids[2]

    def place(color, unit, part, source):
        rows = pl.ds(pl.multiple_of(color * 256 + unit * 32 + part * 8, 8), 8)
        wide[...] = source[...].astype(F32)
        for slot, out in enumerate((grad_q, grad_k, grad_v)):
            for t in range(2):
                at = pl.ds(pl.multiple_of((4 * slot + 2 * head + t) * 8, 8), 8)
                out[rows, 128 * t : 128 * (t + 1)] = wide[at, :]
        for m in range(4):
            grad_first[rows, 128 * m : 128 * (m + 1)] = wide[96 + 8 * m : 104 + 8 * m, :]
        if color == 0:
            high = pl.ds(pl.multiple_of((unit // 4) * 8, 8), 8)
            lanes = pl.ds(pl.multiple_of((unit % 4) * 128, 128), 128)
            small[part, high, lanes] = wide[128:136, :]

    each_piece(ids, near, far, place, LAST_HALVED)
    second[...] = small[0, 0:NB, :]
    for n, out in enumerate((gain1, bias1, gain2, bias2)):
        out[...] = small[0, 8 + n : 9 + n, :]


def slice_kernel(ids, w_q, w_k, w_v, w_o, mine):
    core = ids[0]
    lanes = pl.ds(pl.multiple_of(core * 2 * HD, 2 * HD), 2 * HD)
    for slot, w in enumerate((w_q, w_k, w_v)):
        w.wait()
        mine[512 * slot : 512 * (slot + 1), :] = w[:, lanes]
    w_o.wait()
    for m in range(4):
        mine[1536 + 128 * m : 1664 + 128 * m, :] = w_o[lanes, 128 * m : 128 * (m + 1)]


def swap(values, bits, dp_size):
    dp_bits = sum(bit for bit in bits if bit != "head")
    flip = int("head" in bits)
    pairs = [(d * 2 + h, (d ^ dp_bits) * 2 + (h ^ flip)) for d in range(dp_size) for h in range(2)]
    return lax.ppermute(values, AXES, pairs)


def side_of(bit):
    if bit == "head":
        return lax.axis_index("head")
    return (lax.axis_index("dp") // bit) % 2


def pick(values, index, axis=0):
    return lax.dynamic_index_in_dim(values, index, axis, keepdims=False)


def pick_all(arrays, index):
    return [pick(a, index) for a in arrays]


def low_sum(arrays):
    total = arrays[0].astype(F32)
    for a in arrays[1:]:
        total = total + a.astype(F32)
    return total.astype(LOW)


def line_bits(dp_size):
    bits, bit = [], 4
    while bit < dp_size:
        bits.append(bit)
        bit *= 2
    return bits


PLANE = (["head"], [2], [2, "head"])


def sum_chain(sent, kept, dp_size, halve):
    line = line_bits(dp_size)
    got = swap(sent, [1], dp_size)
    got, = yield [sent], [got]
    shape = (4, 2, 2) + kept.shape[2:]
    sums = [kept.reshape(shape), got.reshape(shape)]
    mine = side_of(2) * 2 + side_of("head")
    sents = [low_sum(pick_all(sums, mine ^ (n + 1))) for n in range(3)]
    gots = [swap(v, bits, dp_size) for v, bits in zip(sents, PLANE)]
    gots = yield sents, gots
    sums = pick_all(sums, mine) + list(gots)
    if halve:
        for bit in line[:2]:
            side = side_of(bit)
            sent = low_sum(pick_all(sums, 1 - side))
            got = swap(sent, [bit], dp_size)
            got, = yield [sent], [got]
            sums = pick_all(sums, side) + [got]
    near = low_sum(sums)
    for bit in line[2:] if halve else line:
        got = swap(near, [bit], dp_size)
        got, = yield [near], [got]
        near = low_sum([near, got])
    if halve:
        for bit in (line[1], line[0]):
            got = swap(near, [bit], dp_size)
            got, = yield [near], [got]
            near = jnp.stack([near, got])
    gots = [swap(near, bits, dp_size) for bits in PLANE]
    gots = yield [near], gots
    near = jnp.stack([near, *gots])
    far = swap(near, [1], dp_size)
    far, = yield [near], [far]
    return near, far


class Slots:
    def __init__(self):
        self.running, self.done, self.got = {}, {}, {}

    def start(self, name, chain):
        self.running[name], self.got[name] = chain, None

    def step(self):
        sent = []
        for name, chain in list(self.running.items()):
            try:
                new, self.got[name] = chain.send(self.got[name])
                sent += new
            except StopIteration as end:
                self.done[name] = end.value
                del self.running[name], self.got[name]
        return sent

    def before(self, value):
        return lax.optimization_barrier((value, *self.step()))[0]

    def after(self, value):
        names = list(self.running)
        sizes = [len(self.got[n]) for n in names]
        flat = [g for n in names for g in self.got[n]]
        flat = lax.optimization_barrier((value, *flat))[1:]
        for name, size in zip(names, sizes):
            self.got[name], flat = list(flat[:size]), flat[size:]

    def turn(self, name, last):
        if name not in self.running:
            return last
        got = self.got[name]
        if got is not None:
            self.got[name] = list(lax.optimization_barrier((*got, *last))[: len(got)])
        try:
            sent, self.got[name] = self.running[name].send(self.got[name])
            return sent
        except StopIteration as end:
            self.done[name] = end.value
            del self.running[name]
            return last


def shaped(shape, kind):
    return jax.ShapeDtypeStruct(shape, kind)


class Staged:
    def __init__(self, buffer, copy):
        self.buffer, self.copy, self.sent = buffer, copy, False

    def wait(self):
        self.copy.wait()

    def send(self):
        if not self.sent:
            self.copy.start()
            self.sent = True

    shape = property(lambda self: self.buffer.shape)
    dtype = property(lambda self: self.buffer.dtype)

    def __getitem__(self, at):
        return self.buffer[at]

    def __setitem__(self, at, value):
        self.buffer[at] = value


def call(body, scalars, args, outs, scratch, flops, by_parts=(), limit=VMEM_LIMIT):
    args = [a if isinstance(a, tuple) else (a, None) for a in args]
    views = [jax.eval_shape(lambda v, i=i: v if i is None else v[i], a) for a, i in args]
    n_scalars, n_in, n_out = len(scalars), len(args), len(outs)

    def kernel(*refs):
        head, refs = refs[:n_scalars], refs[n_scalars:]
        sources, refs = refs[:n_in], refs[n_in:]
        targets, refs = refs[:n_out], refs[n_out:]
        taken, refs = refs[:n_in], refs[n_in:]
        made, refs = refs[: n_out - len(by_parts)], refs[n_out - len(by_parts) :]
        sems, own = refs[-1], refs[:-1]
        ins, results = [], []
        for n, (source, (_, index)) in enumerate(zip(sources, args)):
            source = source if index is None else source.at[index]
            copy = pltpu.make_async_copy(source, taken[n], sems.at[n])
            copy.start()
            ins.append(Staged(taken[n], copy))
        made = list(made)
        for n, target in enumerate(targets):
            if n in by_parts:
                results.append(target)
            else:
                buffer = made.pop(0)
                copy = pltpu.make_async_copy(buffer, target, sems.at[n_in + n])
                results.append(Staged(buffer, copy))
        body(*head, *ins, *results, *own)
        results = [r for n, r in enumerate(results) if n not in by_parts]
        for result in results:
            result.send()
        for result in results:
            result.wait()

    space = pltpu.HBM if limit == VMEM_LIMIT else pl.ANY
    smem, hbm = pl.BlockSpec(memory_space=pltpu.SMEM), pl.BlockSpec(memory_space=pltpu.HBM)
    whole = [v for n, v in enumerate(outs) if n not in by_parts]
    buffers = [pltpu.VMEM(v.shape, v.dtype) for v in (*views, *whole)]
    return pl.pallas_call(
        kernel,
        in_specs=[smem] * n_scalars + [pl.BlockSpec(memory_space=space)] * n_in,
        out_specs=[hbm] * n_out,
        out_shape=outs,
        scratch_shapes=buffers + scratch + [pltpu.SemaphoreType.DMA((n_in + n_out,))],
        compiler_params=pltpu.CompilerParams(vmem_limit_bytes=limit),
        cost_estimate=pl.CostEstimate(flops=1 << 34, bytes_accessed=1 << 24, transcendentals=0),
    )(*scalars, *[a for a, _ in args])


def on_device(
    dp_size,
    tokens,
    lengths,
    ln1_gain,
    ln1_bias,
    w_query,
    w_key,
    w_value,
    w_out,
    sort_first,
    sort_second,
    ln2_gain,
    ln2_bias,
    w_up,
    w_down,
    cotangent,
):
    rows_all, d = tokens.shape
    count = rows_all // LMAX
    ff = w_up.shape[1]
    core = side_of(1)
    ids = jnp.stack([core, side_of(2), side_of("head"), side_of(4), side_of(8)]).astype(jnp.int32)

    gain1, bias1, gain2, bias2 = (v.reshape(1, d) for v in (ln1_gain, ln1_bias, ln2_gain, ln2_bias))
    second_t = sort_second.T
    mine = call(
        slice_kernel, (ids,), (w_query, w_key, w_value, w_out), [shaped((4 * d, 2 * HD), LOW)], [],
        1 << 20,
    )[0]
    near_w = swap(mine, ["head"], dp_size)

    low_rows, wide_rows = shaped((rows_all, d), LOW), shaped((rows_all, d), F32)
    low_cols = shaped((d, rows_all), LOW)
    small_plan = shaped((count, NB, NB), F32)
    blocks = shaped((count * NB, d), F32)

    normed, normed_t, summary, pre, steps, plan, cot_t, grad_hidden = call(
        functools.partial(prepare_kernel, count), (lengths, ids),
        (tokens, gain1, bias1, sort_first, second_t, cotangent, w_down),
        [low_rows, low_cols, blocks, blocks, shaped((2 * ITERS, count, NB, NB), F32), small_plan]
        + [low_cols, shaped((rows_all, ff), LOW)],
        [], 2 * rows_all * d * ff,
    )
    near_w, normed = lax.optimization_barrier((near_w, normed))
    far_w = swap(near_w, [1], dp_size)

    (
        q, k, v, sk, sv, p, w_all, sent, kept, hidden, middle, grad_middle, grad_att, vecs2
    ) = call(
        functools.partial(forward_kernel, count), (lengths, ids),
        (w_query, w_key, w_value, w_out, near_w, far_w, normed, plan, tokens, gain2, bias2)
        + (w_up, grad_hidden, cot_t, cotangent),
        [low_rows] * 5 + [shaped((count * 2 * LMAX, LMAX), LOW), shaped((4, d, d), LOW)]
        + [shaped((4, 4, 2, PART + 32, 128), LOW)] * 2
        + [shaped((rows_all, ff), LOW), wide_rows, wide_rows, low_rows, shaped((2, d), F32)],
        [pltpu.VMEM((LMAX, d), LOW)] * 2
        + [pltpu.VMEM((d, rows_all), LOW), pltpu.VMEM((rows_all, d), LOW)]
        + [pltpu.VMEM((d, rows_all), LOW)]
        + [pltpu.VMEM((rows_all, PART), F32)] * 2 + [pltpu.VMEM((rows_all, PART), LOW)] * 4
        + [pltpu.VMEM((rows_all, d), F32)] + [pltpu.VMEM((d, d), F32)]
        + [pltpu.VMEM((2, 4, 4, 2, PART + 32, 128), LOW)]
        + [pltpu.SemaphoreType.DMA((ff // PART + 2,))],
        24 * rows_all * d * d, by_parts=(7, 8),
    )
    slots = Slots()
    slots.start("ffn", sum_chain(sent, kept, dp_size, True))
    work = [pltpu.VMEM((LMAX, d), LOW)] * 2 + [pltpu.VMEM((LMAX, d), F32)] * 4
    cuts = (0, 1, count)

    def inputs_of(first, end, w, grad_att):
        rows, probs = slice(first * LMAX, end * LMAX), slice(first * 2 * LMAX, end * 2 * LMAX)
        args = ((grad_att, rows), w) + tuple((a, rows) for a in (q, k, v, sk, sv))
        return args + ((p, probs), plan)

    def after(value, last):
        return lax.optimization_barrier((value, *last))[0]

    grads = []
    for first, end in zip(cuts[:-2], cuts[1:-1]):
        out = call(
            functools.partial(backward_kernel, first, count), (lengths, ids),
            inputs_of(first, end, (w_all, slice(3, 4)), slots.before(grad_att)),
            [shaped(((end - first) * LMAX, d), LOW)] * 3 + [shaped((end - first, NB, NB), F32)],
            work, 4 << 30,
        )
        slots.after(out[-1])
        grads.append(out)
    first, late = cuts[-2], count - cuts[-2]
    late_rows = shaped((late * LMAX, d), LOW)
    sent, kept, *late_grads, gsum = call(
        functools.partial(last_kernel, cuts, count), (lengths, ids),
        inputs_of(first, count, w_all, slots.before(grad_att))
        + (*(g for out in grads for g in out), normed_t, steps, pre, summary, sort_first, second_t)
        + (gain1, bias1, vecs2),
        [shaped((4, 4, 2, 136, 128), LOW)] * 2 + [late_rows] * 3 + [blocks],
        work + [pltpu.VMEM((late, NB, NB), F32), pltpu.VMEM((16, d), F32)]
        + [pltpu.VMEM((d, d), F32)] * 2,
        16 << 30,
    )
    slots.after(sent)
    grads.append(late_grads)
    seqs = [slice(s * LMAX, (s + 1) * LMAX) for s in range(count)]

    last = slots.turn("ffn", [gsum])
    slots.start("last", sum_chain(after(sent, last), kept, dp_size, LAST_HALVED))
    for name in TURNS:
        if name == "output":
            output = call(
                functools.partial(output_kernel, count), (),
                (after(w_down, last), *((hidden, r) for r in seqs), *((middle, r) for r in seqs)),
                [low_rows], [], 1 << 30,
            )[0]
            last = [output]
        elif name == "input":
            input_grad = call(
                functools.partial(input_kernel, cuts, count), (lengths, ids),
                (after(gsum, last), (w_all, slice(0, 3)), gain1)
                + tuple(g for out in grads for g in out[:3])
                + tuple((tokens, r) for r in seqs) + tuple((grad_middle, r) for r in seqs),
                [low_rows], [], 1 << 30,
            )[0]
            last = [input_grad]
        else:
            last = slots.turn(name, last)
    while "ffn" in slots.running:
        last = slots.turn("ffn", last)
    up_sum, down_sum, o_sum = call(
        place_ffn_kernel, (ids,), slots.done["ffn"],
        [shaped(s, F32) for s in ((d, ff), (ff, d), w_out.shape)],
        [pltpu.VMEM((d, d), F32)], 1 << 28, limit=20 << 20,
    )
    last = [o_sum]
    while "last" in slots.running:
        last = slots.turn("last", last)
    q_sum, k_sum, v_sum, first_sum, second_sum, *vec_sums = call(
        place_last_kernel, (ids,), slots.done["last"],
        [shaped(w_query.shape, F32)] * 3 + [shaped((d, d), F32), shaped((NB, d), F32)]
        + [shaped((1, d), F32)] * 4,
        [pltpu.VMEM((136, 128), F32), pltpu.VMEM((4, 16, d), F32)], 1 << 26, limit=8 << 20,
    )
    vec_sums = [v.reshape(d) for v in vec_sums]
    return (
        output,
        input_grad,
        vec_sums[0],
        vec_sums[1],
        q_sum,
        k_sum,
        v_sum,
        o_sum,
        first_sum,
        second_sum.T,
        vec_sums[2],
        vec_sums[3],
        up_sum,
        down_sum,
    )


def solution(mesh):
    tokens, copied, columns = P(AXES, None), P(), P(None, "head")
    return jax.shard_map(
        functools.partial(on_device, mesh.shape["dp"]),
        mesh=mesh,
        in_specs=(tokens, P("dp"), copied, copied, columns, columns, columns, P("head", None))
        + (copied,) * 6
        + (tokens,),
        out_specs=(tokens, tokens, copied, copied, columns, columns, columns, P("head", None))
        + (copied,) * 6,
        check_vma=False,
    )
```

```python
import functools

import jax
import jax.numpy as jnp
from jax import lax
from jax.experimental import pallas as pl
from jax.experimental.pallas import tpu as pltpu
from jax.sharding import PartitionSpec as P

HD = 64
BL = 32
ITERS = 8
LMAX = 256
NB = LMAX // BL
SUMMARY_SCALE = BL**-0.5
F32 = jnp.float32
LOW = jnp.bfloat16
AXES = ("dp", "head")
VMEM_LIMIT = 56 * 1024 * 1024
TURNS = ["last", "last", "ffn", "output", "last", "ffn", "input", "ffn", "ffn", "last", "last"]
LAST_HALVED = False

ERF_P = 0.3875
ERF_C = (
    0.23607149955804155,
    0.07450957017858355,
    0.6926085194492264,
    -0.6975625302575207,
    0.9269567150083973,
    -0.23258376165572045,
)


def normal_parts(v):
    size = jnp.abs(v)
    bell = jnp.exp(v * v * -0.5)
    t = 1.0 / (1.0 + size * (ERF_P * 0.5**0.5))
    poly = ERF_C[5]
    for coef in ERF_C[4::-1]:
        poly = poly * t + coef
    tail = (0.5 * t) * poly * bell
    return jnp.where(v >= 0, 1.0 - tail, tail), bell * 0.3989422804014327


def dot_nn(a, b):
    return lax.dot_general(a, b, (((1,), (0,)), ((), ())), preferred_element_type=F32)


def dot_nt(a, b):
    return lax.dot_general(a, b, (((1,), (1,)), ((), ())), preferred_element_type=F32)


def dot_tn(a, b):
    return lax.dot_general(a, b, (((0,), (0,)), ((), ())), preferred_element_type=F32)


def split3(v):
    high = v.astype(LOW)
    left = v - high.astype(F32)
    mid = left.astype(LOW)
    return high, mid, (left - mid.astype(F32)).astype(LOW)


def split2(v):
    high = v.astype(LOW)
    return high, (v - high.astype(F32)).astype(LOW)


def exact_right(dot, v, w):
    a, b, c = split3(v)
    return dot(a, w) + dot(b, w) + dot(c, w)


def exact_both(dot, v, w):
    a, b, c = split3(v)
    d, e, f = split3(w)
    return dot(a, d) + (dot(a, e) + dot(b, d)) + (dot(b, e) + dot(a, f) + dot(c, d))


def row_norm(x):
    center = x - jnp.mean(x, axis=-1, keepdims=True)
    spread = jnp.mean(center * center, axis=-1, keepdims=True)
    scale = lax.rsqrt(spread + 1e-05)
    return center * scale, scale


def norm_pull(grad, unit, scale):
    return scale * (
        grad
        - jnp.mean(grad, axis=-1, keepdims=True)
        - unit * jnp.mean(grad * unit, axis=-1, keepdims=True)
    )


def iota(shape, axis):
    return lax.broadcasted_iota(jnp.int32, shape, axis)


def plan_allowed(count, spans):
    shape = (count, NB, NB)
    seq = iota(shape, 0)
    span = jnp.zeros(shape, jnp.int32)
    for s in range(count):
        span = jnp.where(seq == s, spans[s], span)
    row, col = iota(shape, 1), iota(shape, 2)
    row_ok, col_ok = row * BL < span, col * BL < span
    return (row_ok & col_ok) | ((row == col) & ~row_ok)


def head_mask(value):
    row, lane = iota((LMAX, 8 * HD), 0), iota((LMAX, 8 * HD), 1)
    return jnp.where(row // BL == lane // HD, value, 0.0).astype(LOW)


def spread_plan(plan, flip):
    pick = jnp.where(iota((LMAX, NB), 0) // BL == iota((LMAX, NB), 1), 1.0, 0.0).astype(LOW)
    same = (iota((LMAX, LMAX), 0) % BL) == (iota((LMAX, LMAX), 1) % BL)
    parts = []
    for part in split2(plan):
        tall = (dot_nt if flip else dot_nn)(pick, part).astype(LOW)
        parts.append(jnp.where(same, dot_nt(tall, pick), 0.0).astype(LOW))
    return parts


def pair_rows(left_t, right, m, lane_low):
    both = dot_nn(left_t[2 * BL * m : 2 * BL * (m + 1), :], right[:, 2 * HD * m : 2 * HD * (m + 1)])
    return jnp.where(lane_low, both[:BL], both[BL:])


PART = 256
PIECE = 64


def prepare_kernel(
    count, lens, ids, tokens, ln_gain, ln_bias, first, second, cotangent, down,
    normed, normed_t, summary, pre, steps, plan, cot_t, grad_hidden,
):
    spans = [lens[ids[2] * count + s] for s in range(count)]
    tokens.wait()
    ln_gain.wait()
    ln_bias.wait()
    gain, bias = ln_gain[...], ln_bias[...]
    token, block = iota((NB, LMAX), 1), iota((NB, LMAX), 0)

    def norm(s, carry):
        rows = pl.ds(pl.multiple_of(s * LMAX, LMAX), LMAX)
        unit, _ = row_norm(tokens[rows, :].astype(F32))
        low = (unit * gain + bias).astype(LOW)
        normed[rows, :] = low
        normed_t[:, rows] = low.T
        member = (token // BL == block) & (token < lens[ids[2] * count + s])
        picked = jnp.where(member, 1.0, 0.0).astype(LOW)
        blocks = pl.ds(pl.multiple_of(s * NB, NB), NB)
        summary[blocks, :] = dot_nn(picked, low) * SUMMARY_SCALE
        return carry

    lax.fori_loop(0, count, norm, 0)
    for out in (normed, normed_t, summary):
        out.send()
    for value in (first, second, cotangent, down):
        value.wait()
    before = exact_right(dot_nn, summary[...], first[...])
    pre[...] = before
    gate, _ = normal_parts(before)
    logits = exact_right(dot_nt, before * gate, second[...])
    logits = logits.reshape(count, NB, NB)
    x = jnp.where(plan_allowed(count, spans), logits, -1e30)
    for k in range(2 * ITERS):
        axis = 2 - k % 2
        top = jnp.max(x, axis=axis, keepdims=True)
        x = x - (top + jnp.log(jnp.sum(jnp.exp(x - top), axis=axis, keepdims=True)))
        steps[k] = x
    plan[...] = jnp.exp(x)
    for out in (pre, steps, plan):
        out.send()
    rows = cotangent[...]
    for s in range(count):
        seq = slice(s * LMAX, (s + 1) * LMAX)
        cot_t[:, seq] = cotangent[seq, :].T
    cot_t.send()

    def expand(c, carry):
        at = pl.ds(pl.multiple_of(c * PART, PART), PART)
        grad_hidden[:, at] = dot_nt(rows, down[at, :]).astype(LOW)
        return carry

    lax.fori_loop(0, down.shape[0] // PART, expand, 0)


def forward_kernel(
    count, lens, ids, w_q, w_k, w_v, w_o, near_w, far_w, normed, plan, tokens, ln_gain, ln_bias,
    up, grad_hidden, cot_t, cotangent,
    q_out, k_out, v_out, sk_out, sv_out, p_out, w_all, sent, kept, hidden_out, middle, grad_middle,
    grad_att, grad_vecs,
    mask, mixed, mixed_t, normed2, normed2_t, up0, up1, hid0, hid1, gup0, gup1, gn_s,
    grad_s, parts, part_sems,
):
    mask[...] = head_mask(HD**-0.5)
    for value in (w_q, w_k, w_v, w_o, near_w, far_w, normed, plan):
        value.wait()
    core, head = ids[0], ids[2]
    half, quarter = 4 * HD, 2 * HD
    own = pl.ds(pl.multiple_of(head * half, half), half)
    near = pl.ds(pl.multiple_of((1 - head) * half + core * quarter, quarter), quarter)
    far = pl.ds(pl.multiple_of((1 - head) * half + (1 - core) * quarter, quarter), quarter)
    for slot, w in enumerate((w_q, w_k, w_v)):
        w_all[slot, :, own] = w[...]
        w_all[slot, :, near] = near_w[512 * slot : 512 * (slot + 1), :]
        w_all[slot, :, far] = far_w[512 * slot : 512 * (slot + 1), :]
    w_all[3, own, :] = w_o[...]
    for m in range(4):
        lanes, rows = slice(128 * m, 128 * (m + 1)), slice(1536 + 128 * m, 1664 + 128 * m)
        w_all[3, near, lanes] = near_w[rows, :]
        w_all[3, far, lanes] = far_w[rows, :]
    w_all.send()
    keep_row = iota((LMAX, 8 * HD), 0)
    key_row = iota((2 * BL, 8 * BL), 0)
    query = iota((2 * BL, 8 * BL), 1) % BL
    lane_low = iota((BL, 2 * HD), 1) < HD

    def one(s, carry):
        span = lens[ids[2] * count + s]
        seq = pl.ds(pl.multiple_of(s * LMAX, LMAX), LMAX)
        n = normed[seq, :]
        keep = keep_row < span
        q_out[seq, :] = dot_nn(n, w_all[0]).astype(LOW)
        key = jnp.where(keep, dot_nn(n, w_all[1]), 0.0).astype(LOW)
        value = jnp.where(keep, dot_nn(n, w_all[2]), 0.0).astype(LOW)
        k_out[seq, :] = key
        v_out[seq, :] = value
        high, low = spread_plan(plan[s], False)
        sk_out[seq, :] = (dot_nn(high, key) + dot_nn(low, key)).astype(LOW)
        sv_out[seq, :] = (dot_nn(high, value) + dot_nn(low, value)).astype(LOW)
        rows = [pl.ds(pl.multiple_of(s * LMAX + i * BL, BL), BL) for i in range(NB)]
        scores = []
        for r in rows:
            keys = jnp.concatenate([k_out[r, :], sk_out[r, :]], 0)
            wide = jnp.concatenate([q_out[r, :]] * 8, 0) * mask[...]
            scores.append(dot_nt(keys, wide))
        weights = []
        for i, score in enumerate(scores):
            valid = jnp.where(key_row < BL, i * BL + key_row, i * BL) < span
            score = jnp.where(valid | (i * BL + query >= span), score, -1e30)
            grown = jnp.exp(score - jnp.max(score, axis=0, keepdims=True))
            weights.append(grown * (1.0 / jnp.sum(grown, axis=0, keepdims=True)))
        for i, weight in enumerate(weights):
            at = pl.multiple_of(s * 2 * LMAX + i * 2 * BL, 2 * BL)
            p_out[pl.ds(at, 2 * BL), :] = weight.astype(LOW)
        turned = [weight.T.astype(LOW) for weight in weights]
        for i, (r, weight_t) in enumerate(zip(rows, turned)):
            values = jnp.concatenate([v_out[r, :], sv_out[r, :]], 0)
            out = jnp.concatenate([pair_rows(weight_t, values, m, lane_low) for m in range(4)], 1)
            out = jnp.where(iota((BL, 8 * HD), 0) + i * BL < span, out, 0.0)
            mixed[i * BL : (i + 1) * BL, :] = out.astype(LOW)
        blended = mixed[...]
        mixed_t[:, seq] = blended.T

        @pl.when(s == 0)
        def _():
            tokens.wait()
            ln_gain.wait()
            ln_bias.wait()

        mid = tokens[seq, :].astype(F32) + dot_nn(blended, w_all[3])
        middle[seq, :] = mid
        unit, _ = row_norm(mid)
        low2 = (unit * ln_gain[...] + ln_bias[...]).astype(LOW)
        normed2[seq, :] = low2
        normed2_t[:, seq] = low2.T
        return carry

    lax.fori_loop(0, count, one, 0)
    for out in (q_out, k_out, v_out, sk_out, sv_out, p_out, middle):
        out.send()
    for value in (up, grad_hidden, cot_t, cotangent):
        value.wait()
    units = up.shape[1] // PART // 2
    quarter = normed.shape[1] // 4
    ups, hids, gups = (up0, up1), (hid0, hid1), (gup0, gup1)

    def columns(c):
        unit = ((c // units) ^ (1 - core)) * units + c % units
        return pl.ds(pl.multiple_of(unit * PART, PART), PART)

    def expand(c, side):
        ups[side][...] = dot_nn(normed2[...], up[:, columns(c)])

    def gate_rows(c, side, rows):
        v = ups[side][rows, :]
        share, bell = normal_parts(v)
        hidden = (v * share).astype(LOW)
        hids[side][rows, :] = hidden
        hidden_out[rows, columns(c)] = hidden
        gh = grad_hidden[rows, columns(c)].astype(F32)
        gups[side][rows, :] = (gh * (share + v * bell)).astype(LOW)

    def gate(c, side):
        for r in range(up0.shape[0] // PIECE):
            gate_rows(c, side, slice(r * PIECE, (r + 1) * PIECE))

    def gate_alone(c, side):
        def piece(r, carry):
            gate_rows(c, side, pl.ds(pl.multiple_of(r * PIECE, PIECE), PIECE))
            return carry

        lax.fori_loop(0, up0.shape[0] // PIECE, piece, 0)

    def reduce(c, side):
        hidden, gup = hids[side][...], gups[side][...]
        for color, (left, right) in enumerate(((normed2_t, gup), (cot_t, hidden))):
            grad = dot_nn(left[...], right).astype(LOW)
            for j in range(PART // 128):
                for i in range(4):
                    tile = grad[quarter * i : quarter * (i + 1), 128 * j : 128 * (j + 1)]
                    at = slice(quarter * j, quarter * (j + 1))
                    parts[c // units, c % units, i, color, at, :] = tile
        gn_s[...] += dot_nt(gup, up[:, columns(c)])

    def part_copy(n, u):
        at = (u, slice(None), slice(None), slice(0, PART))
        return pltpu.make_async_copy(
            parts.at[n].at[at], (sent, kept)[n].at[at], part_sems.at[n * units + u]
        )

    gn_s[...] = jnp.zeros_like(gn_s)
    last = 2 * units - 1
    expand(0, 0)
    expand(1, 1)
    gate_alone(0, 0)

    def steps(i, carry):
        for h in range(2):
            c = 2 * i + 1 + h
            expand(c + 1, h)
            gate(c, 1 - h)
            reduce(c - 1, h)
        return carry

    lax.fori_loop(0, units - 1, steps, 0)
    for u in range(units):
        part_copy(0, u).start()
    gate(last, 1)
    hidden_out.send()
    reduce(last - 1, 0)
    reduce(last, 1)

    def pull(s, carry):
        gain, bias = carry
        seq = pl.ds(pl.multiple_of(s * LMAX, LMAX), LMAX)
        gn, mid = gn_s[seq, :], middle[seq, :]
        unit, scale = row_norm(mid)
        gmid = cotangent[seq, :].astype(F32) + norm_pull(gn * ln_gain[...], unit, scale)
        grad_middle[seq, :] = gmid
        grad_att[seq, :] = gmid.astype(LOW)
        gain = gain + jnp.sum(gn * unit, axis=0, keepdims=True)
        return gain, bias + jnp.sum(gn, axis=0, keepdims=True)

    zero = jnp.zeros((1, middle.shape[1]), F32)
    gain, bias = lax.fori_loop(0, count, pull, (zero, zero))
    for out in (grad_att, grad_middle):
        out.send()
    grad_vecs[0:1, :] = gain
    grad_vecs[1:2, :] = bias
    for u in range(units):
        part_copy(1, u).start()
    grad_s[...] = dot_nn(mixed_t[...], grad_att[...])
    tails = []
    for n, target in enumerate((sent, kept)):
        base = (core ^ (1 - n)) * units
        for j in range(units):
            for m in range(4):
                for h in range(2):
                    at = pl.multiple_of((base + j) * 64 + 32 * h, 32)
                    tile = grad_s[pl.ds(at, 32), 128 * m : 128 * (m + 1)].astype(LOW)
                    parts[n, j, 2 * (m % 2) + h, m // 2, PART : PART + 32, :] = tile
        at = (slice(None), slice(None), slice(None), slice(PART, PART + 32))
        tail = pltpu.make_async_copy(
            parts.at[n].at[at], target.at[at], part_sems.at[2 * units + n]
        )
        tail.start()
        tails.append(tail)
    for u in range(units):
        part_copy(0, u).wait()
        part_copy(1, u).wait()
    for tail in tails:
        tail.wait()


def scatter_tiles(core, sent, kept, wide, base):
    for n, target in enumerate((sent, kept)):

        def unit(k, carry, n=n, target=target):
            color, u = k // 4, k % 4
            at = (color * 8 + (core ^ (1 - n)) * 4 + u) * 32
            tile = wide[pl.ds(pl.multiple_of(at, 32), 32), :].astype(LOW)
            for p in range(4):
                for m in range(4):
                    part = tile[8 * p : 8 * (p + 1), 128 * m : 128 * (m + 1)]
                    target[u, p, color, base + 8 * m : base + 8 * (m + 1), :] = part
            return carry

        lax.fori_loop(0, 8, unit, 0)


def backward_one(
    local, plan_at, span, grad_att, w_o, q_in, k_in, v_in, sk_in, sv_in, p_in, plan,
    grad_q, grad_k, grad_v, grad_plan, mask, go_s, dks, dvs, dk_own, dv_own,
):
    base = local * LMAX
    seq = pl.ds(pl.multiple_of(base, LMAX), LMAX)
    gmixed = dot_nt(grad_att[seq, :], w_o[...]).astype(LOW)
    keep = iota((LMAX, 8 * HD), 0) < span
    go_s[...] = jnp.where(keep, gmixed, jnp.zeros_like(gmixed))
    lane_low = iota((BL, 2 * HD), 1) < HD
    rows = [pl.ds(pl.multiple_of(base + i * BL, BL), BL) for i in range(NB)]
    probs = [pl.ds(pl.multiple_of(2 * base + i * 2 * BL, 2 * BL), 2 * BL) for i in range(NB)]
    own_rows = [slice(i * BL, (i + 1) * BL) for i in range(NB)]
    grads, scores = [], []
    for r, at, mine in zip(rows, probs, own_rows):
        values = jnp.concatenate([v_in[r, :], sv_in[r, :]], 0)
        gwide = jnp.concatenate([go_s[mine, :]] * 8, 0) * mask[...]
        grads.append(dot_nt(values, gwide))
        dv = dot_nn(p_in[at, :], gwide)
        dv_own[mine, :] = dv[:BL]
        dvs[mine, :] = dv[BL:]
    for at, gweights in zip(probs, grads):
        wide = p_in[at, :].astype(F32)
        total = jnp.sum(wide * gweights, axis=0, keepdims=True)
        scores.append(wide * (gweights - total))
    turned = [gscores.T.astype(LOW) for gscores in scores]
    for r, mine, gscores in zip(rows, own_rows, scores):
        qwide = jnp.concatenate([q_in[r, :]] * 8, 0) * mask[...]
        dk = dot_nn(gscores.astype(LOW), qwide) * HD**-0.5
        dk_own[mine, :] = dk[:BL]
        dks[mine, :] = dk[BL:]
    for r, gscores_t in zip(rows, turned):
        keys = jnp.concatenate([k_in[r, :], sk_in[r, :]], 0)
        dq = jnp.concatenate([pair_rows(gscores_t, keys, m, lane_low) for m in range(4)], 1)
        grad_q[r, :] = (dq * HD**-0.5).astype(LOW)
    same = (iota((LMAX, LMAX), 0) % BL) == (iota((LMAX, LMAX), 1) % BL)
    high, low = spread_plan(plan[plan_at], True)
    cross = jnp.zeros((LMAX, LMAX), F32)
    for own, sorted_part, kept, target in (
        (dk_own, dks, k_in, grad_k),
        (dv_own, dvs, v_in, grad_v),
    ):
        g_high, g_low = split2(sorted_part[...])
        kept_rows = kept[seq, :]
        cross += dot_nt(g_high, kept_rows) + dot_nt(g_low, kept_rows)
        total = own[...] + (dot_nn(high, g_high) + (dot_nn(high, g_low) + dot_nn(low, g_high)))
        target[seq, :] = jnp.where(keep, total, 0.0).astype(LOW)
    cross = jnp.where(same, cross, 0.0)
    rows8 = jnp.sum(cross.reshape(NB, BL, LMAX), axis=1)
    pick = jnp.where(iota((LMAX, NB), 0) // BL == iota((LMAX, NB), 1), 1.0, 0.0).astype(LOW)
    grad_plan[local] = exact_right(dot_nn, rows8, pick)


def backward_kernel(
    first, count, lens, ids, grad_att, w_all, q_in, k_in, v_in, sk_in, sv_in, p_in, plan,
    grad_q, grad_k, grad_v, grad_plan, mask, *own,
):
    mask[...] = head_mask(1.0)
    ins = (grad_att, w_all, q_in, k_in, v_in, sk_in, sv_in, p_in, plan)
    for value in ins:
        value.wait()
    ins = (grad_att, w_all.buffer.at[0], *ins[2:])

    def one(n, carry):
        span = lens[ids[2] * count + first + n]
        backward_one(
            n, first + n, span, *ins, grad_q, grad_k, grad_v, grad_plan, mask, *own
        )
        return carry

    lax.fori_loop(0, grad_q.shape[0] // LMAX, one, 0)


def last_kernel(cuts, count, lens, ids, grad_att, w_all, q_in, k_in, v_in, sk_in, sv_in, p_in, plan, *refs):
    first, groups = cuts[-2], len(cuts) - 2
    early, refs = refs[: 4 * groups], refs[4 * groups :]
    normed_t, steps, pre, summary, sort_one, sort_two, ln_gain, ln_bias, vecs2 = refs[:9]
    sent, kept, grad_q, grad_k, grad_v, gsum = refs[9:15]
    mask, go_s, dks, dvs, dk_own, dv_own, grad_plan, small, grad_s, prod_s = refs[15:]
    mask[...] = head_mask(1.0)
    ins = (grad_att, w_all, q_in, k_in, v_in, sk_in, sv_in, p_in, plan)
    for value in ins:
        value.wait()
    ins = (grad_att, w_all.buffer.at[3], *ins[2:])
    own = (mask, go_s, dks, dvs, dk_own, dv_own)

    def one(n, carry):
        span = lens[ids[2] * count + first + n]
        backward_one(n, first + n, span, *ins, grad_q, grad_k, grad_v, grad_plan, *own)
        return carry

    lax.fori_loop(0, count - first, one, 0)
    for value in (*early, normed_t, steps):
        value.wait()
    kinds = [list(early[n::4]) + [late] for n, late in enumerate((grad_q, grad_k, grad_v, grad_plan))]
    spans = [lens[ids[2] * count + c] for c in range(count)]
    g = jnp.concatenate([r[...] for r in kinds[3]], 0) * plan[...]
    for k in range(2 * ITERS - 1, -1, -1):
        axis = 2 - k % 2
        g = g - jnp.exp(steps[k]) * jnp.sum(g, axis=axis, keepdims=True)
    g = jnp.where(plan_allowed(count, spans), g, 0.0).reshape(count * NB, NB)
    for out in (grad_q, grad_k, grad_v):
        out.send()
    d = normed_t.shape[0]
    bias = jnp.zeros((8, d), F32)
    for slot in range(3):
        grad = jnp.zeros((d, d), F32)
        for n, rows in enumerate(kinds[slot]):
            grad += dot_nn(normed_t[:, cuts[n] * LMAX : cuts[n + 1] * LMAX], rows[...])
        grad_s[...] = grad
        scatter_tiles(ids[0], sent, kept, grad_s, 32 * slot)
        prod = grad * w_all[slot].astype(F32)
        prod_s[...] = prod if slot == 0 else prod_s[...] + prod
        rows = [dot_nn(jnp.ones((8, part.shape[0]), LOW), part[...]) for part in kinds[slot]]
        for part in split2(sum(rows[1:], rows[0])):
            bias += dot_nt(part, w_all[slot])
    for value in (pre, summary, sort_one, sort_two, ln_gain, ln_bias, vecs2):
        value.wait()
    before = pre[...]
    share, bell = normal_parts(before)
    small[...] = jnp.zeros_like(small)
    small[0:NB, :] = exact_both(dot_tn, g, before * share)
    small[10:12, :] = vecs2[...]
    gpre = exact_right(dot_nn, g, sort_two[...]) * (share + before * bell)
    grad_s[...] = exact_both(dot_tn, summary[...], gpre)
    scatter_tiles(ids[0], sent, kept, grad_s, 96)
    spread = exact_right(dot_nt, gpre, sort_one[...]) * SUMMARY_SCALE
    gsum[...] = spread
    gsum.send()
    block = iota((count * NB, 1), 0)
    valid = jnp.zeros((count * NB, 1), jnp.int32)
    for s in range(count):
        valid = jnp.where(block // NB == s, jnp.clip(spans[s] - block % NB * BL, 0, BL), valid)
    bias = bias[0:1] + jnp.sum(spread * valid.astype(F32), axis=0, keepdims=True)
    gain = jnp.sum(spread * summary[...], axis=0, keepdims=True) * (1.0 / SUMMARY_SCALE)
    for part in split2(prod_s[...]):
        gain += dot_nt(jnp.ones((8, d), LOW), part)[0:1]
    gain = (gain - ln_bias[...] * bias) / ln_gain[...]
    small[8:9, :] = gain
    small[9:10, :] = bias
    zeros = jnp.zeros((8, 128), LOW)
    for n, target in enumerate((sent, kept)):
        at = pl.ds(pl.multiple_of((ids[0] ^ (1 - n)) * 8, 8), 8)
        for u in range(4):
            tile = small[at, 128 * u : 128 * (u + 1)].astype(LOW)
            for color in range(2):
                for i in range(4):
                    target[u, i, color, 128:136, :] = tile if color == 0 and i == 0 else zeros


def input_kernel(cuts, count, lens, ids, gsum, w_all, ln_gain, *refs):
    groups = len(cuts) - 1
    kinds = [refs[n : 3 * groups : 3] for n in range(3)]
    tokens, grad_middle = refs[3 * groups : 3 * groups + count], refs[3 * groups + count : -1]
    input_grad = refs[-1]
    for value in (gsum, w_all, ln_gain):
        value.wait()
    token, block = iota((LMAX, NB), 0), iota((LMAX, NB), 1)
    for s in range(count):
        group = max(n for n in range(groups) if cuts[n] <= s)
        if cuts[group] == s:
            for slot in range(3):
                kinds[slot][group].wait()
        tokens[s].wait()
        grad_middle[s].wait()
        unit, scale = row_norm(tokens[s][...].astype(F32))
        member = (token // BL == block) & (token < lens[ids[2] * count + s])
        picked = jnp.where(member, 1.0, 0.0).astype(LOW)
        high, mid, low = split3(gsum[s * NB : (s + 1) * NB, :])
        gn = dot_nn(picked, high) + dot_nn(picked, mid) + dot_nn(picked, low)
        at = (s - cuts[group]) * LMAX
        for slot in range(3):
            gn += dot_nt(kinds[slot][group][at : at + LMAX, :], w_all[slot])
        pulled = norm_pull(gn * ln_gain[...], unit, scale)
        input_grad[s * LMAX : (s + 1) * LMAX, :] = (grad_middle[s][...] + pulled).astype(LOW)


def output_kernel(count, down, *refs):
    hidden, middle, output = refs[:count], refs[count:-1], refs[-1]
    down.wait()
    for s in range(count):
        hidden[s].wait()
        middle[s].wait()
        total = middle[s][...] + dot_nn(hidden[s][...], down[...])
        output[s * LMAX : (s + 1) * LMAX, :] = total.astype(LOW)


def each_piece(ids, near, far, place, halved):
    core, mine = ids[0], ids[1] * 2 + ids[2]
    for n, source in enumerate((near, far)):
        for color in range(2):

            def pieces(r, carry, n=n, source=source, color=color):
                unit = (core ^ n) * 4 + (mine ^ r)
                for i in range(4):
                    part = (ids[3] ^ (i // 2)) * 2 + (ids[4] ^ (i % 2)) if halved else i
                    place(color, unit, part, source.buffer.at[r, i // 2, i % 2, color])
                return carry

            if halved:
                lax.fori_loop(0, 4, pieces, 0)
            else:
                for r in range(4):
                    pieces(r, 0)


def place_ffn_kernel(ids, near, far, grad_up, grad_down, grad_o, o_s):
    near.wait()
    far.wait()

    def place(color, unit, part, source):
        quarter = pl.ds(pl.multiple_of(part * 128, 128), 128)
        for j in range(2):
            at = pl.ds(pl.multiple_of(unit * PART + 128 * j, 128), 128)
            block = source[128 * j : 128 * (j + 1), :].astype(F32)
            if color == 0:
                grad_up[quarter, at] = block
            else:
                grad_down[at, quarter] = block.T
        rows = pl.ds(pl.multiple_of(unit * 64 + (part % 2) * 32, 32), 32)
        lanes = pl.ds(pl.multiple_of(256 * color + (part // 2) * 128, 128), 128)
        o_s[rows, lanes] = source[PART : PART + 32, :].astype(F32)

    each_piece(ids, near, far, place, True)
    grad_o[...] = o_s[pl.ds(pl.multiple_of(ids[2] * 256, 256), 256), :]


def place_last_kernel(
    ids, near, far, grad_q, grad_k, grad_v, grad_first, second, gain1, bias1, gain2, bias2, wide, small
):
    near.wait()
    far.wait()
    head = ids[2]

    def place(color, unit, part, source):
        rows = pl.ds(pl.multiple_of(color * 256 + unit * 32 + part * 8, 8), 8)
        wide[...] = source[...].astype(F32)
        for slot, out in enumerate((grad_q, grad_k, grad_v)):
            for t in range(2):
                at = pl.ds(pl.multiple_of((4 * slot + 2 * head + t) * 8, 8), 8)
                out[rows, 128 * t : 128 * (t + 1)] = wide[at, :]
        for m in range(4):
            grad_first[rows, 128 * m : 128 * (m + 1)] = wide[96 + 8 * m : 104 + 8 * m, :]
        if color == 0:
            high = pl.ds(pl.multiple_of((unit // 4) * 8, 8), 8)
            lanes = pl.ds(pl.multiple_of((unit % 4) * 128, 128), 128)
            small[part, high, lanes] = wide[128:136, :]

    each_piece(ids, near, far, place, LAST_HALVED)
    second[...] = small[0, 0:NB, :]
    for n, out in enumerate((gain1, bias1, gain2, bias2)):
        out[...] = small[0, 8 + n : 9 + n, :]


def slice_kernel(ids, w_q, w_k, w_v, w_o, mine, taken, sems):
    part = pl.ds(pl.multiple_of(ids[0] * 2 * HD, 2 * HD), 2 * HD)
    sources = [w.at[:, part] for w in (w_q, w_k, w_v)]
    sources += [w_o.at[part, 128 * m : 128 * (m + 1)] for m in range(4)]
    copies, at = [], 0
    for n, source in enumerate(sources):
        target = taken.at[at : at + source.shape[0], :]
        copies.append(pltpu.make_async_copy(source, target, sems.at[n]))
        at += source.shape[0]
    for copy in copies:
        copy.start()
    for copy in copies:
        copy.wait()
    out = pltpu.make_async_copy(taken, mine, sems.at[len(copies)])
    out.start()
    out.wait()


def swap(values, bits, dp_size):
    dp_bits = sum(bit for bit in bits if bit != "head")
    flip = int("head" in bits)
    pairs = [(d * 2 + h, (d ^ dp_bits) * 2 + (h ^ flip)) for d in range(dp_size) for h in range(2)]
    return lax.ppermute(values, AXES, pairs)


def side_of(bit):
    if bit == "head":
        return lax.axis_index("head")
    return (lax.axis_index("dp") // bit) % 2


def pick(values, index, axis=0):
    return lax.dynamic_index_in_dim(values, index, axis, keepdims=False)


def pick_all(arrays, index):
    return [pick(a, index) for a in arrays]


def low_sum(arrays):
    total = arrays[0].astype(F32)
    for a in arrays[1:]:
        total = total + a.astype(F32)
    return total.astype(LOW)


def line_bits(dp_size):
    bits, bit = [], 4
    while bit < dp_size:
        bits.append(bit)
        bit *= 2
    return bits


PLANE = (["head"], [2], [2, "head"])


def sum_chain(sent, kept, dp_size, halve):
    line = line_bits(dp_size)
    got = swap(sent, [1], dp_size)
    got, = yield [sent], [got]
    shape = (4, 2, 2) + kept.shape[2:]
    sums = [kept.reshape(shape), got.reshape(shape)]
    mine = side_of(2) * 2 + side_of("head")
    sents = [low_sum(pick_all(sums, mine ^ (n + 1))) for n in range(3)]
    gots = [swap(v, bits, dp_size) for v, bits in zip(sents, PLANE)]
    gots = yield sents, gots
    sums = pick_all(sums, mine) + list(gots)
    if halve:
        for bit in line[:2]:
            side = side_of(bit)
            sent = low_sum(pick_all(sums, 1 - side))
            got = swap(sent, [bit], dp_size)
            got, = yield [sent], [got]
            sums = pick_all(sums, side) + [got]
    near = low_sum(sums)
    for bit in line[2:] if halve else line:
        got = swap(near, [bit], dp_size)
        got, = yield [near], [got]
        near = low_sum([near, got])
    if halve:
        for bit in (line[1], line[0]):
            got = swap(near, [bit], dp_size)
            got, = yield [near], [got]
            near = jnp.stack([near, got])
    gots = [swap(near, bits, dp_size) for bits in PLANE]
    gots = yield [near], gots
    near = jnp.stack([near, *gots])
    far = swap(near, [1], dp_size)
    far, = yield [near], [far]
    return near, far


class Slots:
    def __init__(self):
        self.running, self.done, self.got = {}, {}, {}

    def start(self, name, chain):
        self.running[name], self.got[name] = chain, None

    def step(self):
        sent = []
        for name, chain in list(self.running.items()):
            try:
                new, self.got[name] = chain.send(self.got[name])
                sent += new
            except StopIteration as end:
                self.done[name] = end.value
                del self.running[name], self.got[name]
        return sent

    def before(self, value):
        return lax.optimization_barrier((value, *self.step()))[0]

    def after(self, value):
        names = list(self.running)
        sizes = [len(self.got[n]) for n in names]
        flat = [g for n in names for g in self.got[n]]
        flat = lax.optimization_barrier((value, *flat))[1:]
        for name, size in zip(names, sizes):
            self.got[name], flat = list(flat[:size]), flat[size:]

    def turn(self, name, last):
        if name not in self.running:
            return last
        got = self.got[name]
        if got is not None:
            self.got[name] = list(lax.optimization_barrier((*got, *last))[: len(got)])
        try:
            sent, self.got[name] = self.running[name].send(self.got[name])
            return sent
        except StopIteration as end:
            self.done[name] = end.value
            del self.running[name]
            return last


def shaped(shape, kind):
    return jax.ShapeDtypeStruct(shape, kind)


class Staged:
    def __init__(self, buffer, copy):
        self.buffer, self.copy, self.sent = buffer, copy, False

    def wait(self):
        self.copy.wait()

    def send(self):
        if not self.sent:
            self.copy.start()
            self.sent = True

    shape = property(lambda self: self.buffer.shape)
    dtype = property(lambda self: self.buffer.dtype)

    def __getitem__(self, at):
        return self.buffer[at]

    def __setitem__(self, at, value):
        self.buffer[at] = value


def call(body, scalars, args, outs, scratch, flops, by_parts=(), limit=VMEM_LIMIT):
    args = [a if isinstance(a, tuple) else (a, None) for a in args]
    views = [jax.eval_shape(lambda v, i=i: v if i is None else v[i], a) for a, i in args]
    n_scalars, n_in, n_out = len(scalars), len(args), len(outs)

    def kernel(*refs):
        head, refs = refs[:n_scalars], refs[n_scalars:]
        sources, refs = refs[:n_in], refs[n_in:]
        targets, refs = refs[:n_out], refs[n_out:]
        taken, refs = refs[:n_in], refs[n_in:]
        made, refs = refs[: n_out - len(by_parts)], refs[n_out - len(by_parts) :]
        sems, own = refs[-1], refs[:-1]
        ins, results = [], []
        for n, (source, (_, index)) in enumerate(zip(sources, args)):
            source = source if index is None else source.at[index]
            copy = pltpu.make_async_copy(source, taken[n], sems.at[n])
            copy.start()
            ins.append(Staged(taken[n], copy))
        made = list(made)
        for n, target in enumerate(targets):
            if n in by_parts:
                results.append(target)
            else:
                buffer = made.pop(0)
                copy = pltpu.make_async_copy(buffer, target, sems.at[n_in + n])
                results.append(Staged(buffer, copy))
        body(*head, *ins, *results, *own)
        results = [r for n, r in enumerate(results) if n not in by_parts]
        for result in results:
            result.send()
        for result in results:
            result.wait()

    space = pltpu.HBM if limit == VMEM_LIMIT else pl.ANY
    smem, hbm = pl.BlockSpec(memory_space=pltpu.SMEM), pl.BlockSpec(memory_space=pltpu.HBM)
    whole = [v for n, v in enumerate(outs) if n not in by_parts]
    buffers = [pltpu.VMEM(v.shape, v.dtype) for v in (*views, *whole)]
    return pl.pallas_call(
        kernel,
        in_specs=[smem] * n_scalars + [pl.BlockSpec(memory_space=space)] * n_in,
        out_specs=[hbm] * n_out,
        out_shape=outs,
        scratch_shapes=buffers + scratch + [pltpu.SemaphoreType.DMA((n_in + n_out,))],
        compiler_params=pltpu.CompilerParams(vmem_limit_bytes=limit),
        cost_estimate=pl.CostEstimate(flops=1 << 34, bytes_accessed=1 << 24, transcendentals=0),
    )(*scalars, *[a for a, _ in args])


def on_device(
    dp_size,
    tokens,
    lengths,
    ln1_gain,
    ln1_bias,
    w_query,
    w_key,
    w_value,
    w_out,
    sort_first,
    sort_second,
    ln2_gain,
    ln2_bias,
    w_up,
    w_down,
    cotangent,
):
    rows_all, d = tokens.shape
    count = rows_all // LMAX
    ff = w_up.shape[1]
    core = side_of(1)
    ids = jnp.stack([core, side_of(2), side_of("head"), side_of(4), side_of(8)]).astype(jnp.int32)

    gain1, bias1, gain2, bias2 = (v.reshape(1, d) for v in (ln1_gain, ln1_bias, ln2_gain, ln2_bias))
    second_t = sort_second.T
    hbm = pl.BlockSpec(memory_space=pltpu.HBM)
    mine = pl.pallas_call(
        slice_kernel,
        in_specs=[pl.BlockSpec(memory_space=pltpu.SMEM)] + [hbm] * 4,
        out_specs=hbm,
        out_shape=shaped((4 * d, 2 * HD), LOW),
        scratch_shapes=[pltpu.VMEM((4 * d, 2 * HD), LOW), pltpu.SemaphoreType.DMA((8,))],
    )(ids, w_query, w_key, w_value, w_out)
    near_w = swap(mine, ["head"], dp_size)

    low_rows, wide_rows = shaped((rows_all, d), LOW), shaped((rows_all, d), F32)
    low_cols = shaped((d, rows_all), LOW)
    small_plan = shaped((count, NB, NB), F32)
    blocks = shaped((count * NB, d), F32)

    normed, normed_t, summary, pre, steps, plan, cot_t, grad_hidden = call(
        functools.partial(prepare_kernel, count), (lengths, ids),
        (tokens, gain1, bias1, sort_first, second_t, cotangent, w_down),
        [low_rows, low_cols, blocks, blocks, shaped((2 * ITERS, count, NB, NB), F32), small_plan]
        + [low_cols, shaped((rows_all, ff), LOW)],
        [], 2 * rows_all * d * ff,
    )
    near_w, normed = lax.optimization_barrier((near_w, normed))
    far_w = swap(near_w, [1], dp_size)

    (
        q, k, v, sk, sv, p, w_all, sent, kept, hidden, middle, grad_middle, grad_att, vecs2
    ) = call(
        functools.partial(forward_kernel, count), (lengths, ids),
        (w_query, w_key, w_value, w_out, near_w, far_w, normed, plan, tokens, gain2, bias2)
        + (w_up, grad_hidden, cot_t, cotangent),
        [low_rows] * 5 + [shaped((count * 2 * LMAX, LMAX), LOW), shaped((4, d, d), LOW)]
        + [shaped((4, 4, 2, PART + 32, 128), LOW)] * 2
        + [shaped((rows_all, ff), LOW), wide_rows, wide_rows, low_rows, shaped((2, d), F32)],
        [pltpu.VMEM((LMAX, d), LOW)] * 2
        + [pltpu.VMEM((d, rows_all), LOW), pltpu.VMEM((rows_all, d), LOW)]
        + [pltpu.VMEM((d, rows_all), LOW)]
        + [pltpu.VMEM((rows_all, PART), F32)] * 2 + [pltpu.VMEM((rows_all, PART), LOW)] * 4
        + [pltpu.VMEM((rows_all, d), F32)] + [pltpu.VMEM((d, d), F32)]
        + [pltpu.VMEM((2, 4, 4, 2, PART + 32, 128), LOW)]
        + [pltpu.SemaphoreType.DMA((ff // PART + 2,))],
        24 * rows_all * d * d, by_parts=(7, 8),
    )
    slots = Slots()
    slots.start("ffn", sum_chain(sent, kept, dp_size, True))
    work = [pltpu.VMEM((LMAX, d), LOW)] * 2 + [pltpu.VMEM((LMAX, d), F32)] * 4
    cuts = (0, 1, count)

    def inputs_of(first, end, w, grad_att):
        rows, probs = slice(first * LMAX, end * LMAX), slice(first * 2 * LMAX, end * 2 * LMAX)
        args = ((grad_att, rows), w) + tuple((a, rows) for a in (q, k, v, sk, sv))
        return args + ((p, probs), plan)

    def after(value, last):
        return lax.optimization_barrier((value, *last))[0]

    grads = []
    for first, end in zip(cuts[:-2], cuts[1:-1]):
        out = call(
            functools.partial(backward_kernel, first, count), (lengths, ids),
            inputs_of(first, end, (w_all, slice(3, 4)), slots.before(grad_att)),
            [shaped(((end - first) * LMAX, d), LOW)] * 3 + [shaped((end - first, NB, NB), F32)],
            work, 4 << 30,
        )
        slots.after(out[-1])
        grads.append(out)
    first, late = cuts[-2], count - cuts[-2]
    late_rows = shaped((late * LMAX, d), LOW)
    sent, kept, *late_grads, gsum = call(
        functools.partial(last_kernel, cuts, count), (lengths, ids),
        inputs_of(first, count, w_all, slots.before(grad_att))
        + (*(g for out in grads for g in out), normed_t, steps, pre, summary, sort_first, second_t)
        + (gain1, bias1, vecs2),
        [shaped((4, 4, 2, 136, 128), LOW)] * 2 + [late_rows] * 3 + [blocks],
        work + [pltpu.VMEM((late, NB, NB), F32), pltpu.VMEM((16, d), F32)]
        + [pltpu.VMEM((d, d), F32)] * 2,
        16 << 30,
    )
    slots.after(sent)
    grads.append(late_grads)
    seqs = [slice(s * LMAX, (s + 1) * LMAX) for s in range(count)]

    last = slots.turn("ffn", [gsum])
    slots.start("last", sum_chain(after(sent, last), kept, dp_size, LAST_HALVED))
    for name in TURNS:
        if name == "output":
            output = call(
                functools.partial(output_kernel, count), (),
                (after(w_down, last), *((hidden, r) for r in seqs), *((middle, r) for r in seqs)),
                [low_rows], [], 1 << 30,
            )[0]
            last = [output]
        elif name == "input":
            input_grad = call(
                functools.partial(input_kernel, cuts, count), (lengths, ids),
                (after(gsum, last), (w_all, slice(0, 3)), gain1)
                + tuple(g for out in grads for g in out[:3])
                + tuple((tokens, r) for r in seqs) + tuple((grad_middle, r) for r in seqs),
                [low_rows], [], 1 << 30,
            )[0]
            last = [input_grad]
        else:
            last = slots.turn(name, last)
    while "ffn" in slots.running:
        last = slots.turn("ffn", last)
    up_sum, down_sum, o_sum = call(
        place_ffn_kernel, (ids,), slots.done["ffn"],
        [shaped(s, F32) for s in ((d, ff), (ff, d), w_out.shape)],
        [pltpu.VMEM((d, d), F32)], 1 << 28, limit=20 << 20,
    )
    last = [o_sum]
    while "last" in slots.running:
        last = slots.turn("last", last)
    q_sum, k_sum, v_sum, first_sum, second_sum, *vec_sums = call(
        place_last_kernel, (ids,), slots.done["last"],
        [shaped(w_query.shape, F32)] * 3 + [shaped((d, d), F32), shaped((NB, d), F32)]
        + [shaped((1, d), F32)] * 4,
        [pltpu.VMEM((136, 128), F32), pltpu.VMEM((4, 16, d), F32)], 1 << 26, limit=8 << 20,
    )
    vec_sums = [v.reshape(d) for v in vec_sums]
    return (
        output,
        input_grad,
        vec_sums[0],
        vec_sums[1],
        q_sum,
        k_sum,
        v_sum,
        o_sum,
        first_sum,
        second_sum.T,
        vec_sums[2],
        vec_sums[3],
        up_sum,
        down_sum,
    )


def solution(mesh):
    tokens, copied, columns = P(AXES, None), P(), P(None, "head")
    return jax.shard_map(
        functools.partial(on_device, mesh.shape["dp"]),
        mesh=mesh,
        in_specs=(tokens, P("dp"), copied, copied, columns, columns, columns, P("head", None))
        + (copied,) * 6
        + (tokens,),
        out_specs=(tokens, tokens, copied, copied, columns, columns, columns, P("head", None))
        + (copied,) * 6,
        check_vma=False,
    )
```
